32 devices in a mesh: rep: 2 (over core), shard: 16 (over z, y, x).
Axes of the slice: x: 2, y: 2, z: 4, core: 2. Of those that a mesh axis runs over, the one named last changes fastest.
Arguments:
- tokens: bfloat16 [12288, 1536], P(('rep', 'shard')), may hold values from -6 to 6
- prompt_ids: int32 [32, 4], P(('rep', 'shard')), may hold values from 0 to 1
- seq_offsets: int32 [32, 4], P(('rep', 'shard')), may hold values from 32 to 64, as said below
- attn_gain: bfloat16 [1536], P('shard'), may hold values from 0.5 to 1.5
- w_query: bfloat16 [1536, 1536], P('shard'), may hold values from -0.15625 to 0.15625
- w_key: bfloat16 [1536, 1536], P('shard'), may hold values from -0.15625 to 0.15625
- w_value: bfloat16 [1536, 1536], P('shard'), may hold values from -0.15625 to 0.15625
- w_outgate: bfloat16 [1536, 1536], P('shard'), may hold values from -0.15625 to 0.15625
- w_forget: bfloat16 [1536, 24], P('shard'), may hold values from -0.15625 to 0.15625
- forget_bias: bfloat16 [24], replicated, may hold values from 1 to 8
- w_output: bfloat16 [1536, 1536], P('shard'), may hold values from -0.625 to 0.625
- ffn_gain: bfloat16 [1536], P('shard'), may hold values from 0.5 to 1.5
- w_gate: bfloat16 [1536, 4096], P('shard'), may hold values from -0.15625 to 0.15625
- w_up: bfloat16 [1536, 4096], P('shard'), may hold values from -0.15625 to 0.15625
- w_down: bfloat16 [4096, 1536], P('shard'), may hold values from -0.09375 to 0.09375
- cotangent: bfloat16 [12288, 1536], P(('rep', 'shard')), may hold values from -6 to 6
Outputs:
- layer_out: bfloat16 [12288, 1536], P(('rep', 'shard'))
- tokens_grad: float32 [12288, 1536], P(('rep', 'shard'))
- attn_gain_grad: float32 [1536], P('shard')
- query_grad: float32 [1536, 1536], P('shard')
- key_grad: float32 [1536, 1536], P('shard')
- value_grad: float32 [1536, 1536], P('shard')
- outgate_grad: float32 [1536, 1536], P('shard')
- forget_grad: float32 [1536, 24], P('shard')
- forget_bias_grad: float32 [24], replicated
- output_grad: float32 [1536, 1536], P('shard')
- ffn_gain_grad: float32 [1536], P('shard')
- gate_grad: float32 [1536, 4096], P('shard')
- up_grad: float32 [1536, 4096], P('shard')
- down_grad: float32 [4096, 1536], P('shard')
The draws below stay inside these ranges and needn't reach their ends.
Inputs may be any that keep to these rules, and one draw needn't show every extreme that they name: `prompt_ids`: each continuation follows one of the 2 prompts of its own block. `seq_offsets`: in every block at least one continuation follows its whole prompt.
All inputs are finite; a program needn't handle non-finite values.
Results may differ from the reference program's by a relative error of at most 0.023.
Values may be sent and summed in bfloat16 or wider, within the bound.
No kernel may reach another device: no remote copies, remote signals or barrier semaphores. Data moves between devices by JAX's collectives and lax.ppermute only.
A program may use at most 320 MiB of HBM per device.

```python
import jax
import jax.numpy as jnp
from jax import lax

D = 1536
HEADS = 24
FF = 4096
PLEN = 64
CLEN = 64
NP = 2
NC = 4
ROWS = 384
BLOCKS = 32
TOKENS = 12288


def draw_seq_offsets(key, part):
    key_values, key_choice = jax.random.split(jax.random.fold_in(key, 17))
    values = jax.random.randint(key_values, (BLOCKS, NC), PLEN // 2, PLEN + 1)
    chosen = jax.random.randint(key_choice, (BLOCKS, 1), 0, NC)
    slot_index = jnp.arange(NC, dtype=jnp.int32)[None, :]
    return jnp.where(slot_index == chosen, PLEN, values).astype(jnp.int32)


def touch_ends(values, own_key, least, largest):
    extent = values.shape
    index_at = [jax.random.randint(jax.random.fold_in(own_key, axis), (), 0, extent[axis]) for axis in range(len(extent))]
    values = values.at[tuple(index_at)].set(least)
    longest = extent.index(max(extent))
    index_at[longest] = (index_at[longest] + 1) % extent[longest]
    return values.at[tuple(index_at)].set(largest)


def levels(key, dims, cuts, smallest, largest):
    factor_of = 1.0
    for axis_at, parts in cuts:
        draws = jax.random.uniform(jax.random.fold_in(jax.random.fold_in(key, 6), axis_at), (parts,), jnp.float32, smallest / len(cuts), largest / len(cuts))
        factor_of = factor_of * jnp.repeat(jnp.exp(draws), dims[axis_at] // parts).reshape((-1,) + (1,) * (len(dims) - 1 - axis_at))
    return factor_of


def scatter_about(stream_key, dims, width, reach, pieces=(), held_as=jnp.bfloat16):
    values = jax.random.normal(stream_key, dims, jnp.float32) * width
    if len(pieces) > 0:
        values = levels(stream_key, dims, pieces, -0.22, 0.18) * values
    return jnp.clip(values, min=-reach, max=reach).astype(held_as)


def setup_inputs(seed: int = 0) -> dict:
    splits = jax.random.split(jax.random.key(seed), 17)
    return {
        "tokens": scatter_about(splits[0], (TOKENS, D), 1.0, 6.0, ((0, 32),)),
        "prompt_ids": touch_ends(jax.random.randint(splits[1], (BLOCKS, NC), 0, NP), jax.random.fold_in(splits[1], 1), 0, NP - 1).astype(jnp.int32),
        "seq_offsets": draw_seq_offsets(jax.random.fold_in(splits[16], 71), 0),
        "attn_gain": jnp.clip(1.0 + 0.1 * jax.random.normal(splits[3], (D,), jnp.float32), 0.5, 1.5).astype(jnp.bfloat16),
        "w_query": scatter_about(splits[4], (D, D), D ** -0.5, 0.15625, ((0, 16),)),
        "w_key": scatter_about(splits[5], (D, D), D ** -0.5, 0.15625, ((0, 16),)),
        "w_value": scatter_about(splits[6], (D, D), D ** -0.5, 0.15625, ((0, 16),)),
        "w_outgate": scatter_about(splits[7], (D, D), D ** -0.5, 0.15625, ((0, 16),)),
        "w_forget": scatter_about(splits[8], (D, HEADS), D ** -0.5, 0.15625, ((0, 16),)),
        "forget_bias": jnp.clip(jax.random.uniform(splits[9], (HEADS,), jnp.float32, 1.0, 8.0), 1.0, 8.0).astype(jnp.bfloat16),
        "w_output": scatter_about(splits[10], (D, D), (D // 16) ** -0.5, 0.625, ((0, 16),)),
        "ffn_gain": jnp.clip(1.0 + 0.1 * jax.random.normal(splits[11], (D,), jnp.float32), 0.5, 1.5).astype(jnp.bfloat16),
        "w_gate": scatter_about(splits[12], (D, FF), D ** -0.5, 0.15625, ((0, 16),)),
        "w_up": scatter_about(splits[13], (D, FF), D ** -0.5, 0.15625, ((0, 16),)),
        "w_down": scatter_about(splits[14], (FF, D), FF ** -0.5, 0.09375, ((0, 16),)),
        "cotangent": scatter_about(splits[15], (TOKENS, D), 1.0, 6.0, ((0, 32),)),
    }


EPS = 1e-06
NEGATIVE = -1e+30
HIGHEST = lax.Precision.HIGHEST

@jax.custom_vjp
def low(v):
    return lax.optimization_barrier(v.astype(jnp.bfloat16)).astype(jnp.float32)

@jax.custom_vjp
def low_back(v):
    return v

def low_keep(v):
    return (low(v), None)

def low_pass(kept, grad):
    return (grad,)

def back_keep(v):
    return (v, None)

def back_low(kept, grad):
    return (low(grad),)
low.defvjp(low_keep, low_pass)
low_back.defvjp(back_keep, back_low)

def chain_mask(prompt_ids, offsets):
    positions = jnp.arange(NP * PLEN + NC * CLEN, dtype=jnp.int32)
    in_prompt = positions < NP * PLEN
    after_prompts = positions - NP * PLEN
    sequence = jnp.where(in_prompt, positions // PLEN, NP + after_prompts // CLEN)
    within = jnp.where(in_prompt, positions % PLEN, after_prompts % CLEN)
    cont_index = sequence - NP
    selector = (cont_index[:, None] == jnp.arange(NC, dtype=jnp.int32)[None, :]).astype(jnp.int32)
    owner_id = jnp.where(in_prompt, -1, lax.optimization_barrier(jnp.sum(selector * prompt_ids[None, :], axis=1)))
    reach_end = lax.optimization_barrier(jnp.sum(selector * offsets[None, :], axis=1))
    same_seq = (sequence[:, None] == sequence[None, :]) & (within[None, :] <= within[:, None])
    from_prompt = (owner_id[:, None] == sequence[None, :]) & (within[None, :] < reach_end[:, None])
    return same_seq | from_prompt

def matmul(left_side, right_side):
    return jnp.dot(left_side, right_side, precision=HIGHEST)

def normalize(values):
    return values * lax.rsqrt(lax.optimization_barrier(jnp.mean(values * values, axis=1, keepdims=True)) + EPS)

def block_forward(block_x, block_ids, block_offsets, params):
    gain_one, query_w, key_w, value_w, outgate_w, forget_w, bias_w, output_w, gain_two, gate_w, up_w, down_w = params
    chain_ok = chain_mask(block_ids, block_offsets)
    row_count = block_x.shape[0]
    head_count = forget_w.shape[1]
    head_dim = block_x.shape[1] // head_count
    normed1 = low(normalize(block_x) * gain_one)
    query_low = low(low_back(matmul(normed1, query_w))).reshape(row_count, head_count, head_dim)
    key_low = low(low_back(matmul(normed1, key_w))).reshape(row_count, head_count, head_dim)
    value_low = low(low_back(matmul(normed1, value_w))).reshape(row_count, head_count, head_dim)
    outgate_pre = low_back(matmul(normed1, outgate_w))
    forget_in = low_back(matmul(normed1, forget_w)) + bias_w
    decay_sum = matmul(chain_ok.astype(jnp.float32), jax.nn.log_sigmoid(forget_in))
    product = low_back(jnp.einsum('qhd,khd->hqk', query_low, key_low, precision=HIGHEST))
    decay_t = decay_sum.T
    logits = product * head_dim ** (-0.5) + decay_t[:, :, None] - decay_t[:, None, :]
    logits = jnp.where(chain_ok[None, :, :], logits, NEGATIVE)
    shifted = jnp.exp(logits - lax.optimization_barrier(jnp.max(logits, axis=2, keepdims=True)))
    prob_low = low(shifted / lax.optimization_barrier(jnp.sum(shifted, axis=2, keepdims=True)))
    attended = low_back(jnp.einsum('hqk,khd->qhd', prob_low, value_low, precision=HIGHEST)).reshape(row_count, -1)
    gated = low(attended * jax.nn.sigmoid(outgate_pre))
    residual = block_x + low_back(matmul(gated, output_w))
    normed2 = low(normalize(residual) * gain_two)
    gate_pre = low_back(matmul(normed2, gate_w))
    up_pre = low_back(matmul(normed2, up_w))
    act_low = low(jax.nn.silu(gate_pre) * up_pre)
    return residual + low_back(matmul(act_low, down_w))

def reference(tokens, prompt_ids, seq_offsets, attn_gain, w_query, w_key, w_value, w_outgate, w_forget, forget_bias, w_output, ffn_gain, w_gate, w_up, w_down, cotangent):
    params = (attn_gain.astype(jnp.float32), w_query.astype(jnp.float32), w_key.astype(jnp.float32), w_value.astype(jnp.float32), w_outgate.astype(jnp.float32), w_forget.astype(jnp.float32), forget_bias.astype(jnp.float32), w_output.astype(jnp.float32), ffn_gain.astype(jnp.float32), w_gate.astype(jnp.float32), w_up.astype(jnp.float32), w_down.astype(jnp.float32))
    inputs = tokens.astype(jnp.float32)
    block_fn = jax.checkpoint(block_forward)

    def forward(layer_in, weights):
        blocks = layer_in.reshape(BLOCKS, ROWS, D)

        def scan_step(scan_state, scan_item):
            return (scan_state, block_fn(scan_item[0], scan_item[1], scan_item[2], weights))
        unused, results = lax.scan(scan_step, jnp.zeros((), jnp.float32), (blocks, prompt_ids, seq_offsets))
        return results.reshape(TOKENS, D)
    outputs, pullback = jax.vjp(forward, inputs, params)
    grad_inputs, grad_params = pullback(cotangent.astype(jnp.float32))
    return (outputs.astype(jnp.bfloat16), grad_inputs, grad_params[0], grad_params[1], grad_params[2], grad_params[3], grad_params[4], grad_params[5], grad_params[6], grad_params[7], grad_params[8], grad_params[9], grad_params[10], grad_params[11])
```

```python
import jax
import jax.numpy as jnp
from jax import lax
from jax.sharding import PartitionSpec as P

PLEN = 64
CLEN = 64
NP = 2
NC = 4


EPS = 1e-06
NEGATIVE = -1e30


def chain_mask(prompt_ids, offsets):
    positions = jnp.arange(NP * PLEN + NC * CLEN, dtype=jnp.int32)
    in_prompt = positions < NP * PLEN
    after_prompts = positions - NP * PLEN
    sequence = jnp.where(in_prompt, positions // PLEN, NP + after_prompts // CLEN)
    within = jnp.where(in_prompt, positions % PLEN, after_prompts % CLEN)
    cont_index = sequence - NP
    selector = (cont_index[:, None] == jnp.arange(NC, dtype=jnp.int32)[None, :]).astype(jnp.int32)
    owner_id = jnp.where(in_prompt, -1, jnp.sum(selector * prompt_ids[None, :], axis=1))
    reach_end = jnp.sum(selector * offsets[None, :], axis=1)
    same_seq = (sequence[:, None] == sequence[None, :]) & (within[None, :] <= within[:, None])
    from_prompt = (owner_id[:, None] == sequence[None, :]) & (within[None, :] < reach_end[:, None])
    return same_seq | from_prompt


def normalize(values):
    inverse = lax.rsqrt(jnp.mean(values * values, axis=1, keepdims=True) + EPS)
    return (values * inverse, inverse)


def norm_back(grad_scaled, scaled, inverse):
    return inverse * (grad_scaled - scaled * jnp.mean(grad_scaled * scaled, axis=1, keepdims=True))


def matmul(left_side, right_side):
    return jnp.dot(left_side, right_side, preferred_element_type=jnp.float32)


def matmul_tn(left_side, right_side):
    return lax.dot_general(
        left_side, right_side, (((0,), (0,)), ((), ())), preferred_element_type=jnp.float32
    )


def matmul_nt(left_side, right_side):
    return lax.dot_general(
        left_side, right_side, (((1,), (1,)), ((), ())), preferred_element_type=jnp.float32
    )


def grid_of(count):
    grid = ((4, count // 4), (2, count // 8))
    return grid if count == 16 else grid + ((2, count // 16),)


def coord_of(index, dim):
    return (index // dim[1]) % dim[0]


def moves(count, dim, steps):
    pairs = []
    for source in range(count):
        at = coord_of(source, dim)
        if at in steps:
            pairs.append((source, source + (steps[at] - at) * dim[1]))
    return pairs


SWAP2 = {0: 1, 1: 0}
PAIRS = {0: 1, 1: 0, 2: 3, 3: 2}
MIDDLE = {1: 2, 2: 1}
OUTWARD = {1: 0, 2: 3}
INWARD = {0: 1, 3: 2}
FARTHER = {0: 2, 2: 0, 1: 3, 3: 1}


def both(low_first, mine, other):
    return jnp.stack([jnp.where(low_first, mine, other), jnp.where(low_first, other, mine)])


def gather_dim(held, count, index, dim):
    at = coord_of(index, dim)
    if dim[0] == 2:
        other = lax.ppermute(held, "shard", moves(count, dim, SWAP2))
        return both(at == 0, held, other)
    other = lax.ppermute(held, "shard", moves(count, dim, PAIRS))
    half = both(at % 2 == 0, held, other)
    middle = lax.ppermute(half, "shard", moves(count, dim, MIDDLE))
    outer = lax.ppermute(middle, "shard", moves(count, dim, OUTWARD))
    far = jnp.where((at == 1) | (at == 2), middle, outer)
    return both(at < 2, half, far).reshape((4,) + held.shape)


def gather_rows(block, count, index):
    grid = grid_of(count)
    held = block
    for dim in grid:
        held = gather_dim(held, count, index, dim)
    turn = tuple(range(len(grid) - 1, -1, -1))
    held = jnp.transpose(held, turn + (len(grid), len(grid) + 1))
    return held.reshape(-1, block.shape[-1])


def add_low(left_side, right_side):
    return (left_side.astype(jnp.float32) + right_side.astype(jnp.float32)).astype(jnp.bfloat16)


def pick(values, at, axis):
    return lax.dynamic_index_in_dim(values, at, axis, keepdims=False)


def scatter_dim(values, axis, count, index, dim):
    at = coord_of(index, dim)
    if dim[0] == 2:
        other = lax.ppermute(pick(values, 1 - at, axis), "shard", moves(count, dim, SWAP2))
        return add_low(pick(values, at, axis), other)
    shape = values.shape
    halves = values.reshape(shape[:axis] + (2, 2) + shape[axis + 1 :])
    far = pick(halves, 1 - at // 2, axis)
    near = pick(halves, at // 2, axis)
    arrived = lax.ppermute(far, "shard", moves(count, dim, INWARD))
    arrived = lax.ppermute(add_low(far, arrived), "shard", moves(count, dim, MIDDLE))
    near = add_low(near, arrived)
    other = lax.ppermute(pick(near, 1 - at % 2, axis), "shard", moves(count, dim, PAIRS))
    return add_low(pick(near, at % 2, axis), other)


def scatter_rows(values, count, index):
    grid = grid_of(count)
    rows = values.shape[0] // (count // 2)
    held = values.reshape(tuple(dim[0] for dim in grid) + (rows, values.shape[1]))
    for axis in range(len(grid) - 1, -1, -1):
        held = scatter_dim(held, axis, count, index, grid[axis])
    return held


def sum_all(values, count, reps):
    total = values
    for dim in grid_of(count) + ((2, 1),):
        if dim[0] == 2:
            total = total + lax.ppermute(total, "shard", moves(count, dim, SWAP2))
        else:
            total = total + lax.ppermute(total, "shard", moves(count, dim, PAIRS))
            total = total + lax.ppermute(total, "shard", moves(count, dim, FARTHER))
    step = 1
    while step < reps:
        total = total + lax.ppermute(total, "rep", [(r, r ^ step) for r in range(reps)])
        step *= 2
    return total


def local(
    tokens,
    prompt_ids,
    seq_offsets,
    attn_gain,
    w_query,
    w_key,
    w_value,
    w_outgate,
    w_forget,
    forget_bias,
    w_output,
    ffn_gain,
    w_gate,
    w_up,
    w_down,
    cotangent,
    *,
    reps,
    count,
):
    own_rows = tokens.shape[0]
    model_width = tokens.shape[1]
    head_count = w_forget.shape[1]
    head_dim = model_width // head_count
    score_scale = head_dim ** (-0.5)
    team = 4
    core = lax.axis_index("rep") % 2
    index = lax.axis_index("shard")
    side = index % 2
    rank = 2 * side + core
    quarter = model_width // team
    heads = head_count // team
    shard_rows = w_query.shape[0]
    shard_ff = w_down.shape[0]
    unit = shard_ff // 2
    quarter_ff = w_gate.shape[1] // team
    core_pairs = [(r, r ^ 1) for r in range(reps)]
    side_pairs = [(s, s ^ 1) for s in range(count)]

    def swap_core(values):
        return lax.ppermute(values, "rep", core_pairs)

    def swap_side(values):
        return lax.ppermute(values, "shard", side_pairs)

    def team_rows(values):
        pair = jnp.concatenate([values, swap_side(values)], axis=0)
        return jnp.concatenate([pair, swap_core(pair)], axis=0)

    def team_sum(partial):
        half = 2 * own_rows
        pair = partial[:half] + swap_core(partial[half:].astype(jnp.bfloat16)).astype(jnp.float32)
        return pair[:own_rows] + swap_side(pair[own_rows:].astype(jnp.bfloat16)).astype(jnp.float32)

    def gather(block):
        return gather_rows(block, count, index)

    def scatter(values):
        return scatter_rows(values, count, index)

    def cols_of(values, who):
        return lax.dynamic_slice_in_dim(values, who * quarter, quarter, axis=1)

    def units_of(values, which_side):
        cut = values.reshape(values.shape[0], count // 2, 2, 2, unit)
        return pick(pick(cut, core, 3), which_side, 2).reshape(values.shape[0], quarter_ff)

    def pair_rows(mine, sent):
        return both(side == 0, mine, swap_side(sent)).reshape(-1, mine.shape[1])

    small = jnp.concatenate(
        [
            w_forget,
            attn_gain[:, None],
            ffn_gain[:, None],
            jnp.zeros((shard_rows, 128 - head_count - 2), jnp.bfloat16),
        ],
        axis=1,
    )
    far_rank = rank ^ 2

    def columns(who, *weights):
        return [cols_of(w, who) for w in weights]

    first = gather(
        pair_rows(
            jnp.concatenate(columns(rank, w_query, w_key, w_value) + [small], axis=1),
            jnp.concatenate(columns(far_rank, w_query, w_key, w_value) + [small], axis=1),
        )
    )
    second = gather(
        pair_rows(
            jnp.concatenate(columns(rank, w_outgate, w_output), axis=1),
            jnp.concatenate(columns(far_rank, w_outgate, w_output), axis=1),
        )
    )
    gate_w = gather(pair_rows(units_of(w_gate, side), units_of(w_gate, 1 - side)))
    up_w = gather(pair_rows(units_of(w_up, side), units_of(w_up, 1 - side)))
    down_w = gather(lax.dynamic_slice_in_dim(w_down, core * unit, unit, axis=0))

    query_w = first[:, :quarter]
    key_w = first[:, quarter : 2 * quarter]
    value_w = first[:, 2 * quarter : 3 * quarter]
    forget_w = lax.dynamic_slice_in_dim(
        first[:, 3 * quarter : 3 * quarter + head_count], rank * heads, heads, axis=1
    )
    gain_one = first[:, 3 * quarter + head_count].astype(jnp.float32)
    gain_two = first[:, 3 * quarter + head_count + 1].astype(jnp.float32)
    outgate_w = second[:, :quarter]
    output_cols = second[:, quarter:]

    def turn_rows(values):
        cut = values.reshape(2, 2, quarter, quarter)
        mine = pick(cut, side, 0)
        pair = both(side == 0, mine, swap_side(pick(cut, 1 - side, 0)))
        kept = pick(pair, core, 1)
        quad = both(core == 0, kept, swap_core(pick(pair, 1 - core, 1)))
        return jnp.transpose(quad, (2, 1, 0, 3)).reshape(quarter, model_width)

    def turn_cols(values):
        cut = values.reshape(quarter, 2, 2, quarter)
        mine = pick(cut, core, 2)
        pair = both(core == 0, mine, swap_core(pick(cut, 1 - core, 2)))
        kept = pick(pair, side, 2)
        quad = both(side == 0, kept, swap_side(pick(pair, 1 - side, 2)))
        return quad.reshape(model_width, quarter)

    output_w = turn_rows(output_cols)

    tokens_all = team_rows(tokens)
    cotangent_all = team_rows(cotangent)
    facts_all = team_rows(jnp.concatenate([prompt_ids[0], seq_offsets[0]])[None, :])
    chain_ok = jnp.stack([chain_mask(facts_all[b, :NC], facts_all[b, NC:]) for b in range(team)])
    chain_float = chain_ok.astype(jnp.float32)

    inputs_all = tokens_all.astype(jnp.float32)
    scaled_all, inverse_all = normalize(inputs_all)
    scaled1 = scaled_all[:own_rows]
    inverse1 = inverse_all[:own_rows]
    inputs = inputs_all[:own_rows]
    normed1 = (scaled_all * gain_one).astype(jnp.bfloat16)
    row_count = normed1.shape[0]

    def split_heads(values):
        return values.reshape(team, own_rows, heads, head_dim)

    query_low = split_heads(matmul(normed1, query_w).astype(jnp.bfloat16))
    key_low = split_heads(matmul(normed1, key_w).astype(jnp.bfloat16))
    value_low = split_heads(matmul(normed1, value_w).astype(jnp.bfloat16))
    outgate_pre = matmul(normed1, outgate_w)
    bias_mine = lax.dynamic_slice_in_dim(
        forget_bias.astype(jnp.float32), rank * heads, heads, axis=0
    )
    forget_in = matmul(normed1, forget_w) + bias_mine[None, :]
    log_forget = jax.nn.log_sigmoid(forget_in).reshape(team, own_rows, heads)
    decay_sum = jnp.einsum(
        "bij,bjh->bhi", chain_float, log_forget, precision=lax.Precision.HIGHEST
    )

    def decayed_scores():
        logits = jnp.einsum(
            "bqhd,bkhd->bhqk", query_low, key_low, preferred_element_type=jnp.float32
        )
        logits = logits * score_scale + decay_sum[:, :, :, None] - decay_sum[:, :, None, :]
        return jnp.where(chain_ok[:, None, :, :], logits, NEGATIVE)

    logits = decayed_scores()
    top_score = jnp.max(logits, axis=3, keepdims=True)
    exp_scores = jnp.exp(logits - top_score)
    denominator = jnp.sum(exp_scores, axis=3, keepdims=True)
    log_total = top_score + jnp.log(denominator)
    probs_low = (exp_scores / denominator).astype(jnp.bfloat16)
    attended = jnp.einsum(
        "bhqk,bkhd->bqhd", probs_low, value_low, preferred_element_type=jnp.float32
    ).reshape(row_count, quarter)
    gate_open = jax.nn.sigmoid(outgate_pre)
    gated_low = (attended * gate_open).astype(jnp.bfloat16)

    residual = inputs + team_sum(matmul(gated_low, output_w))
    scaled2, inverse2 = normalize(residual)
    normed2 = team_rows((scaled2 * gain_two).astype(jnp.bfloat16))
    gate_pre = matmul(normed2, gate_w)
    up_pre = matmul(normed2, up_w)
    sig_gate = jax.nn.sigmoid(gate_pre)
    silu_gate = gate_pre * sig_gate
    act_low = (silu_gate * up_pre).astype(jnp.bfloat16)
    layer_out = (residual + team_sum(matmul(act_low, down_w))).astype(jnp.bfloat16)

    grad_act = matmul_nt(cotangent_all, down_w)
    grad_gate = (grad_act * up_pre * sig_gate * (1.0 + gate_pre * (1.0 - sig_gate))).astype(
        jnp.bfloat16
    )
    grad_up = (grad_act * silu_gate).astype(jnp.bfloat16)
    grad_down = scatter(matmul_tn(act_low, cotangent_all).astype(jnp.bfloat16))
    grad_gate_w = scatter(matmul_tn(normed2, grad_gate).astype(jnp.bfloat16))
    grad_up_w = scatter(matmul_tn(normed2, grad_up).astype(jnp.bfloat16))
    grad_normed2 = team_sum(matmul_nt(grad_gate, gate_w) + matmul_nt(grad_up, up_w))
    grad_gain2 = jnp.sum(grad_normed2 * scaled2, axis=0)
    grad_resid = cotangent.astype(jnp.float32) + norm_back(
        grad_normed2 * gain_two, scaled2, inverse2
    )
    grad_attn = team_rows(grad_resid.astype(jnp.bfloat16))
    grad_gated = matmul_nt(grad_attn, output_w)
    grad_output_cols = turn_cols(matmul_tn(gated_low, grad_attn).astype(jnp.bfloat16))
    grad_attended = split_heads((grad_gated * gate_open).astype(jnp.bfloat16))
    grad_outgate = (grad_gated * attended * gate_open * (1.0 - gate_open)).astype(jnp.bfloat16)
    grad_outgate_w = matmul_tn(normed1, grad_outgate).astype(jnp.bfloat16)
    sum_second = scatter(jnp.concatenate([grad_outgate_w, grad_output_cols], axis=1))
    logits = decayed_scores()
    prob_full = jnp.exp(logits - log_total)
    prob_again = prob_full.astype(jnp.bfloat16)
    grad_probs = jnp.einsum(
        "bqhd,bkhd->bhqk", grad_attended, value_low, preferred_element_type=jnp.float32
    )
    grad_value = jnp.einsum(
        "bhqk,bqhd->bkhd", prob_again, grad_attended, preferred_element_type=jnp.float32
    )
    grad_logits = prob_full * (grad_probs - jnp.sum(prob_full * grad_probs, axis=3, keepdims=True))
    grad_qk = (grad_logits * score_scale).astype(jnp.bfloat16)
    grad_query = jnp.einsum("bhqk,bkhd->bqhd", grad_qk, key_low, preferred_element_type=jnp.float32)
    grad_key = jnp.einsum("bhqk,bqhd->bkhd", grad_qk, query_low, preferred_element_type=jnp.float32)
    grad_decay = jnp.sum(grad_logits, axis=3) - jnp.sum(grad_logits, axis=2)
    grad_log_forget = jnp.einsum(
        "bij,bhi->bjh", chain_float, grad_decay, precision=lax.Precision.HIGHEST
    ).reshape(row_count, heads)
    grad_forget_in = grad_log_forget * jax.nn.sigmoid(-forget_in)
    bias_sum = lax.dynamic_update_slice_in_dim(
        jnp.zeros((head_count,), jnp.float32),
        jnp.sum(grad_forget_in, axis=0),
        rank * heads,
        axis=0,
    )
    grad_bias = sum_all(bias_sum[None, :], count, reps)[0]
    grad_query_low = grad_query.reshape(row_count, quarter).astype(jnp.bfloat16)
    grad_key_low = grad_key.reshape(row_count, quarter).astype(jnp.bfloat16)
    grad_value_low = grad_value.reshape(row_count, quarter).astype(jnp.bfloat16)
    grad_forget_low = grad_forget_in.astype(jnp.bfloat16)

    grad_normed1 = team_sum(
        matmul_nt(grad_query_low, query_w)
        + matmul_nt(grad_key_low, key_w)
        + matmul_nt(grad_value_low, value_w)
        + matmul_nt(grad_outgate, outgate_w)
        + matmul_nt(grad_forget_low, forget_w)
    )
    grad_query_w = matmul_tn(normed1, grad_query_low).astype(jnp.bfloat16)
    grad_key_w = matmul_tn(normed1, grad_key_low).astype(jnp.bfloat16)
    grad_value_w = matmul_tn(normed1, grad_value_low).astype(jnp.bfloat16)
    grad_forget_w = lax.dynamic_update_slice_in_dim(
        jnp.zeros((model_width, head_count), jnp.float32),
        matmul_tn(normed1, grad_forget_low),
        rank * heads,
        axis=1,
    )
    grad_gain1 = jnp.sum(grad_normed1 * scaled1, axis=0)
    tokens_grad = grad_resid + norm_back(grad_normed1 * gain_one, scaled1, inverse1)
    grad_small = jnp.concatenate(
        [
            grad_forget_w,
            grad_gain1[:, None],
            grad_gain2[:, None],
            jnp.zeros((model_width, 128 - head_count - 2), jnp.float32),
        ],
        axis=1,
    ).astype(jnp.bfloat16)
    sum_first = scatter(jnp.concatenate([grad_query_w, grad_key_w, grad_value_w], axis=1))
    sum_small = scatter(grad_small)

    def replicas(values):
        total = values
        step = 2
        while step < reps:
            other = lax.ppermute(total, "rep", [(r, r ^ step) for r in range(reps)])
            total = add_low(total, other)
            step *= 2
        return total

    def own_of(values):
        pair = replicas(values).reshape(2, shard_rows, values.shape[1])
        sides = both(side == 0, pick(pair, side, 0), swap_side(pick(pair, 1 - side, 0)))
        cores = both(core == 0, sides, swap_core(sides))
        return jnp.transpose(cores.astype(jnp.float32), (1, 0, 2, 3))

    def whole_cols(values):
        parts = values.shape[1] // quarter
        quad = own_of(values).reshape(2, 2, shard_rows, parts, quarter)
        quad = jnp.transpose(quad, (3, 2, 0, 1, 4)).reshape(parts, shard_rows, model_width)
        return [quad[p] for p in range(parts)]

    def whole_units(values):
        quad = own_of(values).reshape(2, 2, shard_rows, count // 2, unit)
        return jnp.transpose(quad, (2, 3, 0, 1, 4)).reshape(shard_rows, team * quarter_ff)

    small_pair = replicas(sum_small).reshape(2, shard_rows, sum_small.shape[1])
    small_own = add_low(pick(small_pair, side, 0), swap_side(pick(small_pair, 1 - side, 0)))
    small_own = small_own.astype(jnp.float32) + swap_core(small_own).astype(jnp.float32)
    down_mine = replicas(grad_down)
    down_own = both(core == 0, down_mine, swap_core(down_mine)).astype(jnp.float32)
    query_g, key_g, value_g = whole_cols(sum_first)
    outgate_g, output_g = whole_cols(sum_second)
    return (
        layer_out,
        tokens_grad,
        small_own[:, head_count],
        query_g,
        key_g,
        value_g,
        outgate_g,
        small_own[:, :head_count],
        grad_bias,
        output_g,
        small_own[:, head_count + 1],
        whole_units(grad_gate_w),
        whole_units(grad_up_w),
        down_own.reshape(shard_ff, model_width),
    )


def solution(mesh):
    in_specs = (
        P(("rep", "shard"), None),
        P(("rep", "shard"), None),
        P(("rep", "shard"), None),
        P("shard"),
        P("shard", None),
        P("shard", None),
        P("shard", None),
        P("shard", None),
        P("shard", None),
        P(),
        P("shard", None),
        P("shard"),
        P("shard", None),
        P("shard", None),
        P("shard", None),
        P(("rep", "shard"), None),
    )
    out_specs = (
        P(("rep", "shard"), None),
        P(("rep", "shard"), None),
        P("shard"),
        P("shard", None),
        P("shard", None),
        P("shard", None),
        P("shard", None),
        P("shard", None),
        P(),
        P("shard", None),
        P("shard"),
        P("shard", None),
        P("shard", None),
        P("shard", None),
    )

    def program(*arrays):
        return local(*arrays, reps=mesh.shape["rep"], count=mesh.shape["shard"])

    return jax.shard_map(program, mesh=mesh, in_specs=in_specs, out_specs=out_specs, check_vma=False)
```

```python
import jax
import jax.numpy as jnp
from jax import lax
from jax.experimental import pallas as pl
from jax.experimental.pallas import tpu as pltpu
from jax.sharding import PartitionSpec as P

PLEN = 64
CLEN = 64
NP = 2
NC = 4


EPS = 1e-06
NEGATIVE = -1e30


def chain_mask(prompt_ids, offsets):
    positions = jnp.arange(NP * PLEN + NC * CLEN, dtype=jnp.int32)
    in_prompt = positions < NP * PLEN
    after_prompts = positions - NP * PLEN
    sequence = jnp.where(in_prompt, positions // PLEN, NP + after_prompts // CLEN)
    within = jnp.where(in_prompt, positions % PLEN, after_prompts % CLEN)
    cont_index = sequence - NP
    selector = (cont_index[:, None] == jnp.arange(NC, dtype=jnp.int32)[None, :]).astype(jnp.int32)
    owner_id = jnp.where(in_prompt, -1, jnp.sum(selector * prompt_ids[None, :], axis=1))
    reach_end = jnp.sum(selector * offsets[None, :], axis=1)
    same_seq = (sequence[:, None] == sequence[None, :]) & (within[None, :] <= within[:, None])
    from_prompt = (owner_id[:, None] == sequence[None, :]) & (within[None, :] < reach_end[:, None])
    return same_seq | from_prompt


def normalize(values):
    inverse = lax.rsqrt(jnp.mean(values * values, axis=1, keepdims=True) + EPS)
    return (values * inverse, inverse)


def norm_back(grad_scaled, scaled, inverse):
    return inverse * (grad_scaled - scaled * jnp.mean(grad_scaled * scaled, axis=1, keepdims=True))


PROMPTS = NP * PLEN


def dot_nn(left_side, right_side):
    return jnp.dot(left_side, right_side, preferred_element_type=jnp.float32)


def dot_nt(left_side, right_side):
    return lax.dot_general(
        left_side, right_side, (((1,), (1,)), ((), ())), preferred_element_type=jnp.float32
    )


def dot_tn(left_side, right_side):
    return lax.dot_general(
        left_side, right_side, (((0,), (0,)), ((), ())), preferred_element_type=jnp.float32
    )


def key_mask(facts, block, rows):
    row = lax.broadcasted_iota(jnp.int32, (PROMPTS, PROMPTS), 0)
    col = lax.broadcasted_iota(jnp.int32, (PROMPTS, PROMPTS), 1)
    parts = [(row // PLEN == col // PLEN) & (col <= row)]
    within = lax.broadcasted_iota(jnp.int32, (CLEN, PLEN + CLEN), 0)
    key = lax.broadcasted_iota(jnp.int32, (CLEN, PLEN + CLEN), 1)
    for c in range(NC):
        reach = facts[block, NC + c]
        parts.append(((key < PLEN) & (key < reach)) | ((key >= PLEN) & (key - PLEN <= within)))
    return parts


def probs_of(query, keys, decay_col, decay_row, facts, block, masks, scale):
    logits = []
    for part, mask in enumerate(masks):
        if part == 0:
            rows = slice(0, PROMPTS)
            row_decay = decay_row[:, :PROMPTS]
        else:
            start = PROMPTS + (part - 1) * CLEN
            rows = slice(start, start + CLEN)
            first = facts[block, part - 1] == 0
            prompt_decay = jnp.where(first, decay_row[:, :PLEN], decay_row[:, PLEN:PROMPTS])
            row_decay = jnp.concatenate([prompt_decay, decay_row[:, start : start + CLEN]], axis=1)
        product = dot_nt(query[rows], keys[part]) * scale
        logits.append(jnp.where(mask, product + decay_col[rows] - row_decay, NEGATIVE))
    logits = jnp.concatenate(logits, axis=0)
    shifted = jnp.exp(logits - jnp.max(logits, axis=1, keepdims=True))
    return shifted / jnp.sum(shifted, axis=1, keepdims=True)


def part_rows(part):
    if part == 0:
        return slice(0, PROMPTS)
    start = PROMPTS + (part - 1) * CLEN
    return slice(start, start + CLEN)


def part_keys(ref, lanes, facts, block):
    parts = [ref[:PROMPTS, lanes]]
    for c in range(NC):
        start = pl.multiple_of(facts[block, c] * PLEN, PLEN)
        own = part_rows(c + 1)
        parts.append(jnp.concatenate([ref[pl.ds(start, PLEN), lanes], ref[own, lanes]], axis=0))
    return parts


def attend(qkv, decay_cols, decay_rows, facts, heads, head_dim, team, rows):
    width = heads * head_dim
    scale = head_dim ** (-0.5)

    def body(facts_ref, qkv_ref, col_ref, row_ref, out_ref):
        block = pl.program_id(0)
        masks = key_mask(facts_ref, block, rows)
        for h in range(heads):
            lanes = slice(h * head_dim, (h + 1) * head_dim)
            key_lanes = slice(width + h * head_dim, width + (h + 1) * head_dim)
            value_lanes = slice(2 * width + h * head_dim, 2 * width + (h + 1) * head_dim)
            keys = part_keys(qkv_ref, key_lanes, facts_ref, block)
            values = part_keys(qkv_ref, value_lanes, facts_ref, block)
            probs = probs_of(
                qkv_ref[:, lanes], keys, col_ref[0, :, h : h + 1], row_ref[0, h : h + 1, :],
                facts_ref, block, masks, scale,
            ).astype(jnp.bfloat16)
            for part in range(NC + 1):
                at = part_rows(part)
                out_ref[at, lanes] = dot_nn(probs[at], values[part])

    return pl.pallas_call(
        body,
        grid_spec=pltpu.PrefetchScalarGridSpec(
            num_scalar_prefetch=1,
            grid=(team,),
            in_specs=[
                pl.BlockSpec((rows, qkv.shape[1]), lambda b, f: (b, 0)),
                pl.BlockSpec((1, rows, heads), lambda b, f: (b, 0, 0)),
                pl.BlockSpec((1, heads, rows), lambda b, f: (b, 0, 0)),
            ],
            out_specs=pl.BlockSpec((rows, width), lambda b, f: (b, 0)),
        ),
        out_shape=jax.ShapeDtypeStruct((team * rows, width), jnp.float32),
        cost_estimate=pl.CostEstimate(
            flops=4 * team * rows * PROMPTS * width,
            bytes_accessed=8 * team * rows * width * 2,
            transcendentals=team * rows * PROMPTS * heads,
        ),
        name="attend",
    )(facts, qkv, decay_cols, decay_rows)


def attend_back(qkv, grad_attended, decay_cols, decay_rows, facts, heads, head_dim, team, rows):
    width = heads * head_dim
    scale = head_dim ** (-0.5)

    def body(facts_ref, qkv_ref, grad_ref, col_ref, row_ref, out_ref, sum_ref, low_ref, key_acc, value_acc):
        block = pl.program_id(0)
        masks = key_mask(facts_ref, block, rows)
        for h in range(heads):
            lanes = slice(h * head_dim, (h + 1) * head_dim)
            key_lanes = slice(width + h * head_dim, width + (h + 1) * head_dim)
            value_lanes = slice(2 * width + h * head_dim, 2 * width + (h + 1) * head_dim)
            keys = part_keys(qkv_ref, key_lanes, facts_ref, block)
            values = part_keys(qkv_ref, value_lanes, facts_ref, block)
            query = qkv_ref[:, lanes]
            grad = grad_ref[:, lanes]
            probs = probs_of(
                query, keys, col_ref[0, :, h : h + 1], row_ref[0, h : h + 1, :],
                facts_ref, block, masks, scale,
            )
            grad_probs = jnp.concatenate(
                [dot_nt(grad[part_rows(p)], values[p]) for p in range(NC + 1)], axis=0
            )
            mean = jnp.sum(probs * grad_probs, axis=1, keepdims=True)
            grad_logits = probs * (grad_probs - mean)
            sum_ref[0, :, h : h + 1] = jnp.sum(grad_logits, axis=1, keepdims=True)
            probs_low = probs.astype(jnp.bfloat16)
            grad_qk = (grad_logits * scale).astype(jnp.bfloat16)
            prompt_sum = jnp.sum(grad_logits[:PROMPTS], axis=0, keepdims=True)
            for part in range(NC + 1):
                at = part_rows(part)
                out_ref[at, lanes] = dot_nn(grad_qk[at], keys[part]).astype(jnp.bfloat16)
                grad_keys = dot_tn(grad_qk[at], query[at])
                grad_values = dot_tn(probs_low[at], grad[at])
                if part == 0:
                    key_acc[...] = grad_keys
                    value_acc[...] = grad_values
                    continue
                start = pl.multiple_of(facts_ref[block, part - 1] * PLEN, PLEN)
                key_acc[pl.ds(start, PLEN), :] += grad_keys[:PLEN]
                value_acc[pl.ds(start, PLEN), :] += grad_values[:PLEN]
                out_ref[at, key_lanes] = grad_keys[PLEN:].astype(jnp.bfloat16)
                out_ref[at, value_lanes] = grad_values[PLEN:].astype(jnp.bfloat16)
                column = jnp.sum(grad_logits[at], axis=0, keepdims=True)
                first = facts_ref[block, part - 1] == 0
                nothing = jnp.zeros((1, PLEN), jnp.float32)
                prompt_sum += jnp.concatenate(
                    [
                        jnp.where(first, column[:, :PLEN], nothing),
                        jnp.where(first, nothing, column[:, :PLEN]),
                    ],
                    axis=1,
                )
                low_ref[0, h : h + 1, at] = column[:, PLEN:]
            low_ref[0, h : h + 1, :PROMPTS] = prompt_sum
            out_ref[:PROMPTS, key_lanes] = key_acc[...].astype(jnp.bfloat16)
            out_ref[:PROMPTS, value_lanes] = value_acc[...].astype(jnp.bfloat16)

    return pl.pallas_call(
        body,
        grid_spec=pltpu.PrefetchScalarGridSpec(
            num_scalar_prefetch=1,
            grid=(team,),
            in_specs=[
                pl.BlockSpec((rows, qkv.shape[1]), lambda b, f: (b, 0)),
                pl.BlockSpec((rows, width), lambda b, f: (b, 0)),
                pl.BlockSpec((1, rows, heads), lambda b, f: (b, 0, 0)),
                pl.BlockSpec((1, heads, rows), lambda b, f: (b, 0, 0)),
            ],
            out_specs=[
                pl.BlockSpec((rows, 3 * width), lambda b, f: (b, 0)),
                pl.BlockSpec((1, rows, heads), lambda b, f: (b, 0, 0)),
                pl.BlockSpec((1, heads, rows), lambda b, f: (b, 0, 0)),
            ],
            scratch_shapes=[
                pltpu.VMEM((PROMPTS, head_dim), jnp.float32),
                pltpu.VMEM((PROMPTS, head_dim), jnp.float32),
            ],
        ),
        out_shape=[
            jax.ShapeDtypeStruct((team * rows, 3 * width), jnp.bfloat16),
            jax.ShapeDtypeStruct((team, rows, heads), jnp.float32),
            jax.ShapeDtypeStruct((team, heads, rows), jnp.float32),
        ],
        cost_estimate=pl.CostEstimate(
            flops=10 * team * rows * PROMPTS * width,
            bytes_accessed=7 * team * rows * width * 2,
            transcendentals=team * rows * PROMPTS * heads,
        ),
        name="attend_back",
    )(facts, qkv, grad_attended, decay_cols, decay_rows)


def matmul(left_side, right_side):
    return jnp.dot(left_side, right_side, preferred_element_type=jnp.float32)


def matmul_tn(left_side, right_side):
    return lax.dot_general(
        left_side, right_side, (((0,), (0,)), ((), ())), preferred_element_type=jnp.float32
    )


def matmul_nt(left_side, right_side):
    return lax.dot_general(
        left_side, right_side, (((1,), (1,)), ((), ())), preferred_element_type=jnp.float32
    )


def line_groups(count):
    step = count // 4
    return [[first + step * k for k in range(4)] for first in range(step)]


def middle_strides(count):
    strides = []
    step = count // 8
    while step > 1:
        strides.append(step)
        step //= 2
    return strides


def swap_pairs(count, step):
    return [(s, s ^ step) for s in range(count)]


def both(low_first, mine, other, axis=0):
    return jnp.stack(
        [jnp.where(low_first, mine, other), jnp.where(low_first, other, mine)], axis=axis
    )


def pick(values, at, axis):
    return lax.dynamic_index_in_dim(values, at, axis, keepdims=False)


def add_low(left_side, right_side):
    return (left_side.astype(jnp.float32) + right_side.astype(jnp.float32)).astype(jnp.bfloat16)


def after(values, *others):
    return lax.optimization_barrier((values,) + others)[0]


def gather_line(block, count):
    return lax.all_gather(block, "shard", axis=0, tiled=True, axis_index_groups=line_groups(count))


def gather_rest(line, count, index):
    width = line.shape[1]
    held = line.reshape(4, -1, width)
    for step in reversed(middle_strides(count)):
        other = lax.ppermute(held, "shard", swap_pairs(count, step))
        held = both((index // step) % 2 == 0, held, other, axis=1).reshape(4, -1, width)
    return held.reshape(-1, width), other


def scatter_rest(values, count, index):
    width = values.shape[1]
    held = values.reshape(4, -1, width)
    strides = middle_strides(count)
    parts = []
    for step in strides:
        if parts:
            held = add_low(*parts)
        at = (index // step) % 2
        halves = held.reshape(4, 2, -1, width)
        other = lax.ppermute(pick(halves, 1 - at, 1), "shard", swap_pairs(count, step))
        parts = [pick(halves, at, 1), other]

    def finish(*others):
        return add_low(parts[0], after(parts[1], *others)).reshape(-1, width)

    return finish


def scatter_line(values, count):
    return lax.psum_scatter(
        values, "shard", scatter_dimension=0, tiled=True, axis_index_groups=line_groups(count)
    )


def sum_all(values, count, reps):
    total = values
    step = 1
    while step < count:
        total = total + lax.ppermute(total, "shard", swap_pairs(count, step))
        step *= 2
    step = 1
    while step < reps:
        total = total + lax.ppermute(total, "rep", [(r, r ^ step) for r in range(reps)])
        step *= 2
    return total


def local(
    tokens,
    prompt_ids,
    seq_offsets,
    attn_gain,
    w_query,
    w_key,
    w_value,
    w_outgate,
    w_forget,
    forget_bias,
    w_output,
    ffn_gain,
    w_gate,
    w_up,
    w_down,
    cotangent,
    *,
    reps,
    count,
):
    own_rows = tokens.shape[0]
    model_width = tokens.shape[1]
    head_count = w_forget.shape[1]
    head_dim = model_width // head_count
    score_scale = head_dim ** (-0.5)
    team = 4
    core = lax.axis_index("rep") % 2
    index = lax.axis_index("shard")
    side = index % 2
    rank = 2 * side + core
    quarter = model_width // team
    heads = head_count // team
    shard_rows = w_query.shape[0]
    shard_ff = w_down.shape[0]
    unit = shard_ff // 2
    quarter_ff = w_gate.shape[1] // team
    core_pairs = [(r, r ^ 1) for r in range(reps)]
    side_pairs = [(s, s ^ 1) for s in range(count)]

    def swap_core(values):
        return lax.ppermute(values, "rep", core_pairs)

    def swap_side(values):
        return lax.ppermute(values, "shard", side_pairs)

    def team_rows(values):
        pair = jnp.concatenate([values, swap_side(values)], axis=0)
        return jnp.concatenate([pair, swap_core(pair)], axis=0)

    def core_sum(partial):
        half = 2 * own_rows
        return partial[:half] + swap_core(partial[half:].astype(jnp.bfloat16)).astype(jnp.float32)

    def side_sum(pair):
        return pair[:own_rows] + swap_side(pair[own_rows:].astype(jnp.bfloat16)).astype(jnp.float32)

    def team_sum(partial):
        return side_sum(core_sum(partial))

    def cols_of(values, who):
        return lax.dynamic_slice_in_dim(values, who * quarter, quarter, axis=1)

    def units_of(values, which_side):
        cut = values.reshape(values.shape[0], count // 2, 2, 2, unit)
        return pick(pick(cut, core, 3), which_side, 2).reshape(values.shape[0], quarter_ff)

    def pair_rows(mine, sent):
        return both(side == 0, mine, swap_side(sent)).reshape(-1, mine.shape[1])

    small = jnp.concatenate(
        [
            w_forget,
            attn_gain[:, None],
            ffn_gain[:, None],
            jnp.zeros((shard_rows, 128 - head_count - 2), jnp.bfloat16),
        ],
        axis=1,
    )
    far_rank = rank ^ 2

    def columns(who, *weights):
        return [cols_of(w, who) for w in weights]

    first_block = pair_rows(
        jnp.concatenate(columns(rank, w_query, w_key, w_value) + [small], axis=1),
        jnp.concatenate(columns(far_rank, w_query, w_key, w_value) + [small], axis=1),
    )
    rest_block = pair_rows(
        jnp.concatenate(
            columns(rank, w_outgate, w_output) + [units_of(w_gate, side), units_of(w_up, side)],
            axis=1,
        ),
        after(
            jnp.concatenate(
                columns(far_rank, w_outgate, w_output)
                + [units_of(w_gate, 1 - side), units_of(w_up, 1 - side)],
                axis=1,
            ),
            first_block,
        ),
    )
    first_line = gather_line(first_block, count)
    second_line = gather_line(after(rest_block[:, : 2 * quarter], first_line), count)
    gate_line = gather_line(
        after(rest_block[:, 2 * quarter : 2 * quarter + quarter_ff], second_line), count
    )
    up_line = gather_line(after(rest_block[:, 2 * quarter + quarter_ff :], gate_line), count)
    down_line = gather_line(
        after(lax.dynamic_slice_in_dim(w_down, core * unit, unit, axis=0), up_line), count
    )
    first, first_last = gather_rest(first_line, count, index)
    second, second_last = gather_rest(second_line, count, index)
    gate_w, gate_last = gather_rest(gate_line, count, index)
    up_w, up_last = gather_rest(up_line, count, index)
    down_w, down_last = gather_rest(down_line, count, index)

    forget_w = lax.dynamic_slice_in_dim(
        first[:, 3 * quarter : 3 * quarter + head_count], rank * heads, heads, axis=1
    )
    gain_one = first[:, 3 * quarter + head_count].astype(jnp.float32)
    gain_two = first[:, 3 * quarter + head_count + 1].astype(jnp.float32)
    outgate_w = second[:, :quarter]
    output_cols = second[:, quarter:]

    def turn_rows(values):
        cut = values.reshape(2, 2, quarter, quarter)
        mine = pick(cut, side, 0)
        pair = both(side == 0, mine, swap_side(pick(cut, 1 - side, 0)))
        kept = pick(pair, core, 1)
        quad = both(core == 0, kept, swap_core(pick(pair, 1 - core, 1)))
        return jnp.transpose(quad, (2, 1, 0, 3)).reshape(quarter, model_width)

    def turn_cols(values):
        cut = values.reshape(quarter, 2, 2, quarter)
        mine = pick(cut, core, 2)
        pair = both(core == 0, mine, swap_core(pick(cut, 1 - core, 2)))
        kept = pick(pair, side, 2)
        quad = both(side == 0, kept, swap_side(pick(pair, 1 - side, 2)))
        return quad.reshape(model_width, quarter)

    output_w = turn_rows(output_cols)

    tokens_all = team_rows(after(tokens, rest_block))
    cotangent_all = team_rows(after(cotangent, tokens_all))
    facts_all = team_rows(jnp.concatenate([prompt_ids[0], seq_offsets[0]])[None, :])
    chain_ok = jnp.stack([chain_mask(facts_all[b, :NC], facts_all[b, NC:]) for b in range(team)])
    chain_float = chain_ok.astype(jnp.float32)

    inputs_all = tokens_all.astype(jnp.float32)
    scaled_all, inverse_all = normalize(inputs_all)
    scaled1 = scaled_all[:own_rows]
    inverse1 = inverse_all[:own_rows]
    inputs = inputs_all[:own_rows]
    normed1 = after(
        (scaled_all * gain_one).astype(jnp.bfloat16), gate_line, cotangent_all
    )
    row_count = normed1.shape[0]

    qkv_low = matmul(normed1, first[:, : 3 * quarter]).astype(jnp.bfloat16)
    outgate_pre = matmul(normed1, outgate_w)
    bias_mine = lax.dynamic_slice_in_dim(
        forget_bias.astype(jnp.float32), rank * heads, heads, axis=0
    )
    forget_in = matmul(normed1, forget_w) + bias_mine[None, :]
    log_forget = jax.nn.log_sigmoid(forget_in).reshape(team, own_rows, heads)
    decay_sum = jnp.einsum(
        "bij,bjh->bhi", chain_float, log_forget, precision=lax.Precision.HIGHEST
    )

    decay_cols = jnp.transpose(decay_sum, (0, 2, 1))
    attended = attend(
        after(qkv_low, gate_last),
        decay_cols,
        decay_sum,
        facts_all,
        heads,
        head_dim,
        team,
        own_rows,
    )
    gate_open = jax.nn.sigmoid(outgate_pre)
    gated_low = after((attended * gate_open).astype(jnp.bfloat16), up_line)

    residual = inputs + after(team_sum(matmul(gated_low, output_w)), up_last)
    scaled2, inverse2 = normalize(residual)
    normed2 = after(team_rows((scaled2 * gain_two).astype(jnp.bfloat16)), down_line)
    gate_pre = matmul(normed2, gate_w)
    up_pre = matmul(normed2, up_w)
    sig_gate = jax.nn.sigmoid(gate_pre)
    silu_gate = gate_pre * sig_gate
    act_low = (silu_gate * up_pre).astype(jnp.bfloat16)
    grad_act = matmul_nt(cotangent_all, down_w)
    grad_gate = (grad_act * up_pre * sig_gate * (1.0 + gate_pre * (1.0 - sig_gate))).astype(
        jnp.bfloat16
    )
    grad_up = (grad_act * silu_gate).astype(jnp.bfloat16)
    down_sum = scatter_rest(matmul_tn(act_low, cotangent_all).astype(jnp.bfloat16), count, index)
    pair_normed2 = core_sum(matmul_nt(grad_gate, gate_w) + matmul_nt(grad_up, up_w))
    normed2_gate = after(normed2, pair_normed2)
    part_gate_w = matmul_tn(normed2_gate, grad_gate).astype(jnp.bfloat16)
    gate_sum = scatter_rest(part_gate_w, count, index)
    down_held = down_sum(pair_normed2)
    grad_down = scatter_line(down_held, count)
    normed2_up = after(normed2_gate, down_held)
    part_up_w = matmul_tn(normed2_up, grad_up).astype(jnp.bfloat16)
    up_sum = scatter_rest(part_up_w, count, index)
    grad_normed2 = after(side_sum(pair_normed2), down_held, part_gate_w, part_up_w)
    grad_gain2 = jnp.sum(grad_normed2 * scaled2, axis=0)
    grad_resid = cotangent.astype(jnp.float32) + norm_back(
        grad_normed2 * gain_two, scaled2, inverse2
    )
    grad_attn_own = grad_resid.astype(jnp.bfloat16)
    pair_out = core_sum(matmul(after(act_low, grad_attn_own), down_w))
    gate_held = gate_sum(pair_out)
    grad_gate_w = scatter_line(gate_held, count)
    grad_attn = after(team_rows(grad_attn_own), gate_held)
    layer_out = (residual + side_sum(after(pair_out, grad_attn))).astype(jnp.bfloat16)
    grad_gated = matmul_nt(grad_attn, output_w)
    grad_output_cols = turn_cols(matmul_tn(gated_low, grad_attn).astype(jnp.bfloat16))
    grad_attended = (grad_gated * gate_open).astype(jnp.bfloat16)
    grad_outgate = (grad_gated * attended * gate_open * (1.0 - gate_open)).astype(jnp.bfloat16)
    grad_outgate_w = matmul_tn(normed1, grad_outgate).astype(jnp.bfloat16)
    second_sum = scatter_rest(
        jnp.concatenate([grad_outgate_w, grad_output_cols], axis=1), count, index
    )
    grad_qkv, grad_logit_rows, grad_logit_cols = attend_back(
        qkv_low, grad_attended, decay_cols, decay_sum, facts_all, heads, head_dim, team, own_rows
    )
    up_held = up_sum(grad_qkv)
    grad_up_w = scatter_line(up_held, count)
    grad_decay = jnp.transpose(grad_logit_rows, (0, 2, 1)) - grad_logit_cols
    grad_log_forget = jnp.einsum(
        "bij,bhi->bjh", chain_float, grad_decay, precision=lax.Precision.HIGHEST
    ).reshape(row_count, heads)
    grad_forget_in = grad_log_forget * jax.nn.sigmoid(-forget_in)
    bias_sum = lax.dynamic_update_slice_in_dim(
        jnp.zeros((head_count,), jnp.float32),
        jnp.sum(grad_forget_in, axis=0),
        rank * heads,
        axis=0,
    )
    grad_bias = sum_all(bias_sum[None, :], count, reps)[0]
    grad_forget_low = lax.dynamic_update_slice_in_dim(
        jnp.zeros((row_count, small.shape[1]), jnp.bfloat16),
        grad_forget_in.astype(jnp.bfloat16),
        rank * heads,
        axis=1,
    )
    grad_first = jnp.concatenate([grad_qkv, grad_forget_low], axis=1)
    part_normed1 = matmul_nt(grad_first, first) + matmul_nt(grad_outgate, outgate_w)
    grad_gain1 = jnp.sum(part_normed1 * scaled_all, axis=0)
    grad_normed1 = team_sum(part_normed1)
    tokens_grad = grad_resid + norm_back(grad_normed1 * gain_one, scaled1, inverse1)
    column = jnp.arange(first.shape[1], dtype=jnp.int32)[None, :] - 3 * quarter - head_count
    grad_first_w = (
        matmul_tn(normed1, grad_first)
        + jnp.where(column == 0, grad_gain1[:, None], 0.0)
        + jnp.where(column == 1, grad_gain2[:, None], 0.0)
    )
    first_sum = scatter_rest(after(grad_first_w.astype(jnp.bfloat16), up_held), count, index)
    second_held = second_sum(grad_first_w)
    sum_second = scatter_line(second_held, count)
    first_held = first_sum(second_held)
    sum_first = scatter_line(first_held, count)
    grad_down = after(grad_down, grad_first_w)
    grad_gate_w = after(grad_gate_w, grad_first_w)
    grad_up_w = after(grad_up_w, second_held)
    sum_second = after(sum_second, first_held)
    sum_small = sum_first[:, 3 * quarter :]
    sum_first = sum_first[:, : 3 * quarter]

    def replicas(values):
        total = values
        step = 2
        while step < reps:
            other = lax.ppermute(total, "rep", [(r, r ^ step) for r in range(reps)])
            total = add_low(total, other)
            step *= 2
        return total

    def own_of(values):
        pair = replicas(values).reshape(2, shard_rows, values.shape[1])
        sides = both(side == 0, pick(pair, side, 0), swap_side(pick(pair, 1 - side, 0)))
        cores = both(core == 0, sides, swap_core(sides))
        return jnp.transpose(cores.astype(jnp.float32), (1, 0, 2, 3))

    def whole_cols(values):
        parts = values.shape[1] // quarter
        quad = own_of(values).reshape(2, 2, shard_rows, parts, quarter)
        quad = jnp.transpose(quad, (3, 2, 0, 1, 4)).reshape(parts, shard_rows, model_width)
        return [quad[p] for p in range(parts)]

    def whole_units(values):
        quad = own_of(values).reshape(2, 2, shard_rows, count // 2, unit)
        return jnp.transpose(quad, (2, 3, 0, 1, 4)).reshape(shard_rows, team * quarter_ff)

    small_pair = replicas(sum_small).reshape(2, shard_rows, sum_small.shape[1])
    small_own = add_low(pick(small_pair, side, 0), swap_side(pick(small_pair, 1 - side, 0)))
    small_own = small_own.astype(jnp.float32) + swap_core(small_own).astype(jnp.float32)
    down_mine = replicas(grad_down)
    down_own = both(core == 0, down_mine, swap_core(down_mine)).astype(jnp.float32)
    query_g, key_g, value_g = whole_cols(sum_first)
    outgate_g, output_g = whole_cols(sum_second)
    return (
        layer_out,
        tokens_grad,
        small_own[:, head_count],
        query_g,
        key_g,
        value_g,
        outgate_g,
        small_own[:, :head_count],
        grad_bias,
        output_g,
        small_own[:, head_count + 1],
        whole_units(grad_gate_w),
        whole_units(grad_up_w),
        down_own.reshape(shard_ff, model_width),
    )


def solution(mesh):
    in_specs = (
        P(("rep", "shard"), None),
        P(("rep", "shard"), None),
        P(("rep", "shard"), None),
        P("shard"),
        P("shard", None),
        P("shard", None),
        P("shard", None),
        P("shard", None),
        P("shard", None),
        P(),
        P("shard", None),
        P("shard"),
        P("shard", None),
        P("shard", None),
        P("shard", None),
        P(("rep", "shard"), None),
    )
    out_specs = (
        P(("rep", "shard"), None),
        P(("rep", "shard"), None),
        P("shard"),
        P("shard", None),
        P("shard", None),
        P("shard", None),
        P("shard", None),
        P("shard", None),
        P(),
        P("shard", None),
        P("shard"),
        P("shard", None),
        P("shard", None),
        P("shard", None),
    )

    def program(*arrays):
        return local(*arrays, reps=mesh.shape["rep"], count=mesh.shape["shard"])

    return jax.shard_map(program, mesh=mesh, in_specs=in_specs, out_specs=out_specs, check_vma=False)
```

```python
import jax
import jax.numpy as jnp
from jax import lax
from jax.experimental import pallas as pl
from jax.experimental.pallas import tpu as pltpu
from jax.sharding import PartitionSpec as P

PLEN = 64
CLEN = 64
NP = 2
NC = 4


EPS = 1e-06
NEGATIVE = -1e30


def chain_mask(prompt_ids, offsets):
    positions = jnp.arange(NP * PLEN + NC * CLEN, dtype=jnp.int32)
    in_prompt = positions < NP * PLEN
    after_prompts = positions - NP * PLEN
    sequence = jnp.where(in_prompt, positions // PLEN, NP + after_prompts // CLEN)
    within = jnp.where(in_prompt, positions % PLEN, after_prompts % CLEN)
    cont_index = sequence - NP
    selector = (cont_index[:, None] == jnp.arange(NC, dtype=jnp.int32)[None, :]).astype(jnp.int32)
    owner_id = jnp.where(in_prompt, -1, jnp.sum(selector * prompt_ids[None, :], axis=1))
    reach_end = jnp.sum(selector * offsets[None, :], axis=1)
    same_seq = (sequence[:, None] == sequence[None, :]) & (within[None, :] <= within[:, None])
    from_prompt = (owner_id[:, None] == sequence[None, :]) & (within[None, :] < reach_end[:, None])
    return same_seq | from_prompt


def normalize(values):
    inverse = lax.rsqrt(jnp.mean(values * values, axis=1, keepdims=True) + EPS)
    return (values * inverse, inverse)


def norm_back(grad_scaled, scaled, inverse):
    return inverse * (grad_scaled - scaled * jnp.mean(grad_scaled * scaled, axis=1, keepdims=True))


PROMPTS = NP * PLEN


def dot_nn(left_side, right_side):
    return jnp.dot(left_side, right_side, preferred_element_type=jnp.float32)


def dot_nt(left_side, right_side):
    return lax.dot_general(
        left_side, right_side, (((1,), (1,)), ((), ())), preferred_element_type=jnp.float32
    )


def dot_tn(left_side, right_side):
    return lax.dot_general(
        left_side, right_side, (((0,), (0,)), ((), ())), preferred_element_type=jnp.float32
    )


def key_mask(facts, block, rows):
    row = lax.broadcasted_iota(jnp.int32, (PROMPTS, PROMPTS), 0)
    col = lax.broadcasted_iota(jnp.int32, (PROMPTS, PROMPTS), 1)
    parts = [(row // PLEN == col // PLEN) & (col <= row)]
    within = lax.broadcasted_iota(jnp.int32, (CLEN, PLEN + CLEN), 0)
    key = lax.broadcasted_iota(jnp.int32, (CLEN, PLEN + CLEN), 1)
    for c in range(NC):
        reach = facts[block, NC + c]
        parts.append(((key < PLEN) & (key < reach)) | ((key >= PLEN) & (key - PLEN <= within)))
    return parts


def probs_of(query, keys, decay_col, decay_row, facts, block, masks, scale):
    logits = []
    for part, mask in enumerate(masks):
        if part == 0:
            rows = slice(0, PROMPTS)
            row_decay = decay_row[:, :PROMPTS]
        else:
            start = PROMPTS + (part - 1) * CLEN
            rows = slice(start, start + CLEN)
            first = facts[block, part - 1] == 0
            prompt_decay = jnp.where(first, decay_row[:, :PLEN], decay_row[:, PLEN:PROMPTS])
            row_decay = jnp.concatenate([prompt_decay, decay_row[:, start : start + CLEN]], axis=1)
        product = dot_nt(query[rows], keys[part]) * scale
        logits.append(jnp.where(mask, product + decay_col[rows] - row_decay, NEGATIVE))
    logits = jnp.concatenate(logits, axis=0)
    shifted = jnp.exp(logits - jnp.max(logits, axis=1, keepdims=True))
    return shifted / jnp.sum(shifted, axis=1, keepdims=True)


def part_rows(part):
    if part == 0:
        return slice(0, PROMPTS)
    start = PROMPTS + (part - 1) * CLEN
    return slice(start, start + CLEN)


def part_keys(ref, lanes, facts, block):
    parts = [ref[:PROMPTS, lanes]]
    for c in range(NC):
        start = pl.multiple_of(facts[block, c] * PLEN, PLEN)
        own = part_rows(c + 1)
        parts.append(jnp.concatenate([ref[pl.ds(start, PLEN), lanes], ref[own, lanes]], axis=0))
    return parts


def attend(qkv, decay_cols, decay_rows, facts, heads, head_dim, team, rows):
    width = heads * head_dim
    scale = head_dim ** (-0.5)

    def body(facts_ref, qkv_ref, col_ref, row_ref, out_ref):
        block = pl.program_id(0)
        masks = key_mask(facts_ref, block, rows)
        for h in range(heads):
            lanes = slice(h * head_dim, (h + 1) * head_dim)
            key_lanes = slice(width + h * head_dim, width + (h + 1) * head_dim)
            value_lanes = slice(2 * width + h * head_dim, 2 * width + (h + 1) * head_dim)
            keys = part_keys(qkv_ref, key_lanes, facts_ref, block)
            values = part_keys(qkv_ref, value_lanes, facts_ref, block)
            probs = probs_of(
                qkv_ref[:, lanes], keys, col_ref[0, :, h : h + 1], row_ref[0, h : h + 1, :],
                facts_ref, block, masks, scale,
            ).astype(jnp.bfloat16)
            for part in range(NC + 1):
                at = part_rows(part)
                out_ref[at, lanes] = dot_nn(probs[at], values[part])

    return pl.pallas_call(
        body,
        grid_spec=pltpu.PrefetchScalarGridSpec(
            num_scalar_prefetch=1,
            grid=(team,),
            in_specs=[
                pl.BlockSpec((rows, qkv.shape[1]), lambda b, f: (b, 0)),
                pl.BlockSpec((1, rows, heads), lambda b, f: (b, 0, 0)),
                pl.BlockSpec((1, heads, rows), lambda b, f: (b, 0, 0)),
            ],
            out_specs=pl.BlockSpec((rows, width), lambda b, f: (b, 0)),
        ),
        out_shape=jax.ShapeDtypeStruct((team * rows, width), jnp.float32),
        cost_estimate=pl.CostEstimate(
            flops=64 * team * rows * rows * width,
            bytes_accessed=8 * team * rows * width * 2,
            transcendentals=team * rows * PROMPTS * heads,
        ),
        name="attend",
    )(facts, qkv, decay_cols, decay_rows)


def attend_back(qkv, grad_attended, decay_cols, decay_rows, facts, heads, head_dim, team, rows):
    width = heads * head_dim
    scale = head_dim ** (-0.5)

    def body(facts_ref, qkv_ref, grad_ref, col_ref, row_ref, out_ref, sum_ref, low_ref, key_acc, value_acc):
        block = pl.program_id(0)
        masks = key_mask(facts_ref, block, rows)
        for h in range(heads):
            lanes = slice(h * head_dim, (h + 1) * head_dim)
            key_lanes = slice(width + h * head_dim, width + (h + 1) * head_dim)
            value_lanes = slice(2 * width + h * head_dim, 2 * width + (h + 1) * head_dim)
            keys = part_keys(qkv_ref, key_lanes, facts_ref, block)
            values = part_keys(qkv_ref, value_lanes, facts_ref, block)
            query = qkv_ref[:, lanes]
            grad = grad_ref[:, lanes]
            probs = probs_of(
                query, keys, col_ref[0, :, h : h + 1], row_ref[0, h : h + 1, :],
                facts_ref, block, masks, scale,
            )
            grad_probs = jnp.concatenate(
                [dot_nt(grad[part_rows(p)], values[p]) for p in range(NC + 1)], axis=0
            )
            mean = jnp.sum(probs * grad_probs, axis=1, keepdims=True)
            grad_logits = probs * (grad_probs - mean)
            sum_ref[0, :, h : h + 1] = jnp.sum(grad_logits, axis=1, keepdims=True)
            probs_low = probs.astype(jnp.bfloat16)
            grad_qk = (grad_logits * scale).astype(jnp.bfloat16)
            prompt_sum = jnp.sum(grad_logits[:PROMPTS], axis=0, keepdims=True)
            for part in range(NC + 1):
                at = part_rows(part)
                out_ref[at, lanes] = dot_nn(grad_qk[at], keys[part]).astype(jnp.bfloat16)
                grad_keys = dot_tn(grad_qk[at], query[at])
                grad_values = dot_tn(probs_low[at], grad[at])
                if part == 0:
                    key_acc[...] = grad_keys
                    value_acc[...] = grad_values
                    continue
                start = pl.multiple_of(facts_ref[block, part - 1] * PLEN, PLEN)
                key_acc[pl.ds(start, PLEN), :] += grad_keys[:PLEN]
                value_acc[pl.ds(start, PLEN), :] += grad_values[:PLEN]
                out_ref[at, key_lanes] = grad_keys[PLEN:].astype(jnp.bfloat16)
                out_ref[at, value_lanes] = grad_values[PLEN:].astype(jnp.bfloat16)
                column = jnp.sum(grad_logits[at], axis=0, keepdims=True)
                first = facts_ref[block, part - 1] == 0
                nothing = jnp.zeros((1, PLEN), jnp.float32)
                prompt_sum += jnp.concatenate(
                    [
                        jnp.where(first, column[:, :PLEN], nothing),
                        jnp.where(first, nothing, column[:, :PLEN]),
                    ],
                    axis=1,
                )
                low_ref[0, h : h + 1, at] = column[:, PLEN:]
            low_ref[0, h : h + 1, :PROMPTS] = prompt_sum
            out_ref[:PROMPTS, key_lanes] = key_acc[...].astype(jnp.bfloat16)
            out_ref[:PROMPTS, value_lanes] = value_acc[...].astype(jnp.bfloat16)

    return pl.pallas_call(
        body,
        grid_spec=pltpu.PrefetchScalarGridSpec(
            num_scalar_prefetch=1,
            grid=(team,),
            in_specs=[
                pl.BlockSpec((rows, qkv.shape[1]), lambda b, f: (b, 0)),
                pl.BlockSpec((rows, width), lambda b, f: (b, 0)),
                pl.BlockSpec((1, rows, heads), lambda b, f: (b, 0, 0)),
                pl.BlockSpec((1, heads, rows), lambda b, f: (b, 0, 0)),
            ],
            out_specs=[
                pl.BlockSpec((rows, 3 * width), lambda b, f: (b, 0)),
                pl.BlockSpec((1, rows, heads), lambda b, f: (b, 0, 0)),
                pl.BlockSpec((1, heads, rows), lambda b, f: (b, 0, 0)),
            ],
            scratch_shapes=[
                pltpu.VMEM((PROMPTS, head_dim), jnp.float32),
                pltpu.VMEM((PROMPTS, head_dim), jnp.float32),
            ],
        ),
        out_shape=[
            jax.ShapeDtypeStruct((team * rows, 3 * width), jnp.bfloat16),
            jax.ShapeDtypeStruct((team, rows, heads), jnp.float32),
            jax.ShapeDtypeStruct((team, heads, rows), jnp.float32),
        ],
        cost_estimate=pl.CostEstimate(
            flops=80 * team * rows * rows * width,
            bytes_accessed=7 * team * rows * width * 2,
            transcendentals=team * rows * PROMPTS * heads,
        ),
        name="attend_back",
    )(facts, qkv, grad_attended, decay_cols, decay_rows)


def matmul(left_side, right_side):
    return jnp.dot(left_side, right_side, preferred_element_type=jnp.float32)


def matmul_tn(left_side, right_side):
    return lax.dot_general(
        left_side, right_side, (((0,), (0,)), ((), ())), preferred_element_type=jnp.float32
    )


def matmul_nt(left_side, right_side):
    return lax.dot_general(
        left_side, right_side, (((1,), (1,)), ((), ())), preferred_element_type=jnp.float32
    )


def line_groups(count):
    step = count // 4
    return [[first + step * k for k in range(4)] for first in range(step)]


def middle_strides(count):
    strides = []
    step = count // 8
    while step > 1:
        strides.append(step)
        step //= 2
    return strides


def swap_pairs(count, step):
    return [(s, s ^ step) for s in range(count)]


def both(low_first, mine, other, axis=0):
    return jnp.stack(
        [jnp.where(low_first, mine, other), jnp.where(low_first, other, mine)], axis=axis
    )


def pick(values, at, axis):
    return lax.dynamic_index_in_dim(values, at, axis, keepdims=False)


def add_low(left_side, right_side):
    return (left_side.astype(jnp.float32) + right_side.astype(jnp.float32)).astype(jnp.bfloat16)


def after(values, *others):
    return lax.optimization_barrier((values,) + others)[0]


def gather_line(block, count):
    return lax.all_gather(block, "shard", axis=0, tiled=True, axis_index_groups=line_groups(count))


def gather_rest(line, count, index):
    width = line.shape[1]
    held = line.reshape(4, -1, width)
    for step in reversed(middle_strides(count)):
        other = lax.ppermute(held, "shard", swap_pairs(count, step))
        held = both((index // step) % 2 == 0, held, other, axis=1).reshape(4, -1, width)
    return held.reshape(-1, width), other


def scatter_rest(values, count, index):
    width = values.shape[1]
    held = values.reshape(4, -1, width)
    strides = middle_strides(count)
    parts = []
    for step in strides:
        if parts:
            held = add_low(*parts)
        at = (index // step) % 2
        halves = held.reshape(4, 2, -1, width)
        other = lax.ppermute(pick(halves, 1 - at, 1), "shard", swap_pairs(count, step))
        parts = [pick(halves, at, 1), other]

    def finish(*others):
        return add_low(parts[0], after(parts[1], *others)).reshape(-1, width)

    return finish


def scatter_line(values, count):
    return lax.psum_scatter(
        values, "shard", scatter_dimension=0, tiled=True, axis_index_groups=line_groups(count)
    )


def sum_all(values, count, reps):
    total = values
    for step in middle_strides(count):
        total = total + lax.ppermute(total, "shard", swap_pairs(count, step))
    near = total
    for step in (count // 2, count // 4, 1):
        total = total + lax.ppermute(total, "shard", swap_pairs(count, step))
    step = 1
    while step < reps:
        total = total + lax.ppermute(total, "rep", [(r, r ^ step) for r in range(reps)])
        step *= 2
    return near, total[0]


def local(
    tokens,
    prompt_ids,
    seq_offsets,
    attn_gain,
    w_query,
    w_key,
    w_value,
    w_outgate,
    w_forget,
    forget_bias,
    w_output,
    ffn_gain,
    w_gate,
    w_up,
    w_down,
    cotangent,
    *,
    reps,
    count,
):
    own_rows = tokens.shape[0]
    model_width = tokens.shape[1]
    head_count = w_forget.shape[1]
    head_dim = model_width // head_count
    score_scale = head_dim ** (-0.5)
    team = 4
    core = lax.axis_index("rep") % 2
    index = lax.axis_index("shard")
    side = index % 2
    rank = 2 * side + core
    quarter = model_width // team
    heads = head_count // team
    shard_rows = w_query.shape[0]
    shard_ff = w_down.shape[0]
    unit = shard_ff // 2
    quarter_ff = w_gate.shape[1] // team
    core_pairs = [(r, r ^ 1) for r in range(reps)]
    side_pairs = [(s, s ^ 1) for s in range(count)]

    def swap_core(values):
        return lax.ppermute(values, "rep", core_pairs)

    def swap_side(values):
        return lax.ppermute(values, "shard", side_pairs)

    def team_rows(values):
        pair = jnp.concatenate([values, swap_side(values)], axis=0)
        return jnp.concatenate([pair, swap_core(pair)], axis=0)

    def core_sum(partial):
        half = 2 * own_rows
        return partial[:half] + swap_core(partial[half:].astype(jnp.bfloat16)).astype(jnp.float32)

    def side_sum(pair):
        return pair[:own_rows] + swap_side(pair[own_rows:].astype(jnp.bfloat16)).astype(jnp.float32)

    def team_sum(partial):
        return side_sum(core_sum(partial))

    def cols_of(values, who):
        return lax.dynamic_slice_in_dim(values, who * quarter, quarter, axis=1)

    def units_of(values, which_side):
        cut = values.reshape(values.shape[0], count // 2, 2, 2, unit)
        return pick(pick(cut, core, 3), which_side, 2).reshape(values.shape[0], quarter_ff)

    def pair_rows(mine, sent):
        return both(side == 0, mine, swap_side(sent)).reshape(-1, mine.shape[1])

    small = jnp.concatenate(
        [
            w_forget,
            attn_gain[:, None],
            ffn_gain[:, None],
            jnp.zeros((shard_rows, 128 - head_count - 2), jnp.bfloat16),
        ],
        axis=1,
    )
    far_rank = rank ^ 2

    def columns(who, *weights):
        return [cols_of(w, who) for w in weights]

    first_block = pair_rows(
        jnp.concatenate(columns(rank, w_query, w_key, w_value) + [small], axis=1),
        jnp.concatenate(columns(far_rank, w_query, w_key, w_value) + [small], axis=1),
    )
    rest_block = pair_rows(
        jnp.concatenate(
            columns(rank, w_outgate, w_output) + [units_of(w_gate, side), units_of(w_up, side)],
            axis=1,
        ),
        after(
            jnp.concatenate(
                columns(far_rank, w_outgate, w_output)
                + [units_of(w_gate, 1 - side), units_of(w_up, 1 - side)],
                axis=1,
            ),
            first_block,
        ),
    )
    first_line = gather_line(first_block, count)
    second_line = gather_line(after(rest_block[:, : 2 * quarter], first_line), count)
    gate_line = gather_line(
        after(rest_block[:, 2 * quarter : 2 * quarter + quarter_ff], second_line), count
    )
    up_line = gather_line(after(rest_block[:, 2 * quarter + quarter_ff :], gate_line), count)
    down_line = gather_line(
        after(lax.dynamic_slice_in_dim(w_down, core * unit, unit, axis=0), up_line), count
    )
    first, first_last = gather_rest(first_line, count, index)
    second, second_last = gather_rest(second_line, count, index)
    gate_w, gate_last = gather_rest(gate_line, count, index)
    up_w, up_last = gather_rest(up_line, count, index)
    down_w, down_last = gather_rest(down_line, count, index)

    forget_w = lax.dynamic_slice_in_dim(
        first[:, 3 * quarter : 3 * quarter + head_count], rank * heads, heads, axis=1
    )
    gain_one = first[:, 3 * quarter + head_count].astype(jnp.float32)
    gain_two = first[:, 3 * quarter + head_count + 1].astype(jnp.float32)
    outgate_w = second[:, :quarter]
    output_cols = second[:, quarter:]

    def turn_rows(values):
        cut = values.reshape(2, 2, quarter, quarter)
        mine = pick(cut, side, 0)
        pair = both(side == 0, mine, swap_side(pick(cut, 1 - side, 0)))
        kept = pick(pair, core, 1)
        quad = both(core == 0, kept, swap_core(pick(pair, 1 - core, 1)))
        return jnp.transpose(quad, (2, 1, 0, 3)).reshape(quarter, model_width)

    def turn_cols(values):
        cut = values.reshape(quarter, 2, 2, quarter)
        mine = pick(cut, core, 2)
        pair = both(core == 0, mine, swap_core(pick(cut, 1 - core, 2)))
        kept = pick(pair, side, 2)
        quad = both(side == 0, kept, swap_side(pick(pair, 1 - side, 2)))
        return quad.reshape(model_width, quarter)

    tokens_all = team_rows(after(tokens, rest_block))
    cotangent_all = team_rows(after(cotangent, tokens_all))
    facts_all = team_rows(jnp.concatenate([prompt_ids[0], seq_offsets[0]])[None, :])
    chain_ok = jnp.stack([chain_mask(facts_all[b, :NC], facts_all[b, NC:]) for b in range(team)])
    chain_float = chain_ok.astype(jnp.float32)

    inputs_all = tokens_all.astype(jnp.float32)
    scaled_all, inverse_all = normalize(inputs_all)
    scaled1 = scaled_all[:own_rows]
    inverse1 = inverse_all[:own_rows]
    inputs = inputs_all[:own_rows]
    normed1 = after(
        (scaled_all * gain_one).astype(jnp.bfloat16), second_line, cotangent_all
    )
    row_count = normed1.shape[0]

    qkv_low = matmul(normed1, first[:, : 3 * quarter]).astype(jnp.bfloat16)
    output_w = turn_rows(after(output_cols, qkv_low))
    outgate_pre = matmul(normed1, outgate_w)
    bias_mine = lax.dynamic_slice_in_dim(
        forget_bias.astype(jnp.float32), rank * heads, heads, axis=0
    )
    forget_in = matmul(normed1, forget_w) + bias_mine[None, :]
    log_forget = jax.nn.log_sigmoid(forget_in).reshape(team, own_rows, heads)
    decay_sum = jnp.einsum(
        "bij,bjh->bhi", chain_float, log_forget, precision=lax.Precision.HIGHEST
    )

    decay_cols = jnp.transpose(decay_sum, (0, 2, 1))
    attended = attend(
        after(qkv_low, gate_line),
        decay_cols,
        decay_sum,
        facts_all,
        heads,
        head_dim,
        team,
        own_rows,
    )
    gate_open = jax.nn.sigmoid(outgate_pre)
    gated_low = (after(attended, up_line, gate_last) * gate_open).astype(jnp.bfloat16)

    residual = inputs + after(team_sum(matmul(gated_low, output_w)), up_last)
    scaled2, inverse2 = normalize(residual)
    normed2 = after(team_rows((scaled2 * gain_two).astype(jnp.bfloat16)), down_line)
    gate_pre = matmul(normed2, gate_w)
    up_pre = matmul(normed2, up_w)
    sig_gate = jax.nn.sigmoid(gate_pre)
    silu_gate = gate_pre * sig_gate
    act_low = (silu_gate * up_pre).astype(jnp.bfloat16)
    grad_act = matmul_nt(cotangent_all, down_w)
    grad_gate = (grad_act * up_pre * sig_gate * (1.0 + gate_pre * (1.0 - sig_gate))).astype(
        jnp.bfloat16
    )
    grad_up = (grad_act * silu_gate).astype(jnp.bfloat16)
    down_sum = scatter_rest(matmul_tn(act_low, cotangent_all).astype(jnp.bfloat16), count, index)
    pair_normed2 = core_sum(matmul_nt(grad_gate, gate_w) + matmul_nt(grad_up, up_w))
    normed2_late = after(normed2, pair_normed2)
    part_gate_w = matmul_tn(normed2_late, grad_gate).astype(jnp.bfloat16)
    part_up_w = matmul_tn(normed2_late, grad_up).astype(jnp.bfloat16)
    grad_normed2 = after(side_sum(pair_normed2), part_gate_w, part_up_w)
    down_held = down_sum(grad_normed2)
    grad_down = scatter_line(down_held, count)
    gate_sum = scatter_rest(after(part_gate_w, part_up_w), count, index)
    up_sum = scatter_rest(part_up_w, count, index)
    grad_resid = cotangent.astype(jnp.float32) + norm_back(
        grad_normed2 * gain_two, scaled2, inverse2
    )
    grad_attn_own = grad_resid.astype(jnp.bfloat16)
    pair_out = core_sum(matmul(after(act_low, grad_attn_own), down_w))
    gate_held = gate_sum(pair_out)
    grad_gate_w = scatter_line(gate_held, count)
    grad_attn = after(team_rows(grad_attn_own), gate_held, grad_down)
    grad_gated = matmul_nt(grad_attn, output_w)
    grad_output_cols = turn_cols(matmul_tn(gated_low, grad_attn).astype(jnp.bfloat16))
    grad_attended = (grad_gated * gate_open).astype(jnp.bfloat16)
    grad_outgate = (grad_gated * attended * gate_open * (1.0 - gate_open)).astype(jnp.bfloat16)
    grad_outgate_w = matmul_tn(normed1, grad_outgate).astype(jnp.bfloat16)
    part_second_w = jnp.concatenate([grad_outgate_w, grad_output_cols], axis=1)
    second_sum = scatter_rest(part_second_w, count, index)
    up_held = up_sum(part_second_w)
    grad_up_w = scatter_line(up_held, count)
    grad_qkv, grad_logit_rows, grad_logit_cols = attend_back(
        qkv_low,
        after(grad_attended, up_held, part_second_w),
        decay_cols,
        decay_sum,
        facts_all,
        heads,
        head_dim,
        team,
        own_rows,
    )
    second_held = second_sum(grad_qkv)
    grad_qkv = after(grad_qkv, grad_gate_w, second_held)
    sum_second = scatter_line(second_held, count)
    layer_out = (residual + side_sum(after(pair_out, grad_qkv))).astype(jnp.bfloat16)
    grad_decay = jnp.transpose(grad_logit_rows, (0, 2, 1)) - grad_logit_cols
    grad_log_forget = jnp.einsum(
        "bij,bhi->bjh", chain_float, grad_decay, precision=lax.Precision.HIGHEST
    ).reshape(row_count, heads)
    grad_forget_in = grad_log_forget * jax.nn.sigmoid(-forget_in)
    bias_sum = lax.dynamic_update_slice_in_dim(
        jnp.zeros((head_count,), jnp.float32),
        jnp.sum(grad_forget_in, axis=0),
        rank * heads,
        axis=0,
    )
    bias_near, grad_bias = sum_all(bias_sum[None, :], count, reps)
    grad_forget_low = lax.dynamic_update_slice_in_dim(
        jnp.zeros((row_count, small.shape[1]), jnp.bfloat16),
        grad_forget_in.astype(jnp.bfloat16),
        rank * heads,
        axis=1,
    )
    grad_first = jnp.concatenate([grad_qkv, grad_forget_low], axis=1)
    part_first_w = matmul_tn(normed1, grad_first).astype(jnp.bfloat16)
    first_sum = scatter_rest(after(part_first_w, bias_near), count, index)
    part_normed1 = matmul_nt(after(grad_first, part_first_w), first) + matmul_nt(
        grad_outgate, outgate_w
    )
    first_held = first_sum()
    grad_normed1 = team_sum(after(part_normed1, first_held))
    tokens_grad = grad_resid + norm_back(grad_normed1 * gain_one, scaled1, inverse1)
    sum_first = scatter_line(first_held, count)
    grad_down = after(grad_down, part_first_w)
    grad_gate_w = after(grad_gate_w, part_first_w)
    grad_up_w = after(grad_up_w, part_first_w)
    sum_second = after(sum_second, first_held)
    sum_small = sum_first[:, 3 * quarter :]
    sum_first = sum_first[:, : 3 * quarter]

    def replicas(values):
        total = values
        step = 2
        while step < reps:
            other = lax.ppermute(total, "rep", [(r, r ^ step) for r in range(reps)])
            total = add_low(total, other)
            step *= 2
        return total

    def own_of(values):
        pair = replicas(values).reshape(2, shard_rows, values.shape[1])
        sides = both(side == 0, pick(pair, side, 0), swap_side(pick(pair, 1 - side, 0)))
        cores = both(core == 0, sides, swap_core(sides))
        return jnp.transpose(cores.astype(jnp.float32), (1, 0, 2, 3))

    def whole_cols(values):
        parts = values.shape[1] // quarter
        quad = own_of(values).reshape(2, 2, shard_rows, parts, quarter)
        quad = jnp.transpose(quad, (3, 2, 0, 1, 4)).reshape(parts, shard_rows, model_width)
        return [quad[p] for p in range(parts)]

    def whole_units(values):
        quad = own_of(values).reshape(2, 2, shard_rows, count // 2, unit)
        return jnp.transpose(quad, (2, 3, 0, 1, 4)).reshape(shard_rows, team * quarter_ff)

    small_pair = replicas(sum_small).reshape(2, shard_rows, sum_small.shape[1])
    small_own = add_low(pick(small_pair, side, 0), swap_side(pick(small_pair, 1 - side, 0)))
    small_own = small_own.astype(jnp.float32) + swap_core(small_own).astype(jnp.float32)
    down_mine = replicas(grad_down)
    down_own = both(core == 0, down_mine, swap_core(down_mine)).astype(jnp.float32)
    query_g, key_g, value_g = whole_cols(sum_first)
    outgate_g, output_g = whole_cols(sum_second)
    gate_g = whole_units(grad_gate_w)
    up_g = whole_units(grad_up_w)
    forget_g = small_own[:, :head_count]

    def gain_grad(gain, *pairs):
        total = sum(jnp.sum(w.astype(jnp.float32) * grad, axis=1) for w, grad in pairs)
        return total / gain.astype(jnp.float32)

    gain_one_g = gain_grad(
        attn_gain,
        (w_query, query_g),
        (w_key, key_g),
        (w_value, value_g),
        (w_outgate, outgate_g),
        (w_forget, forget_g),
    )
    gain_two_g = gain_grad(ffn_gain, (w_gate, gate_g), (w_up, up_g))
    return (
        layer_out,
        tokens_grad,
        gain_one_g,
        query_g,
        key_g,
        value_g,
        outgate_g,
        forget_g,
        grad_bias,
        output_g,
        gain_two_g,
        gate_g,
        up_g,
        down_own.reshape(shard_ff, model_width),
    )


def solution(mesh):
    in_specs = (
        P(("rep", "shard"), None),
        P(("rep", "shard"), None),
        P(("rep", "shard"), None),
        P("shard"),
        P("shard", None),
        P("shard", None),
        P("shard", None),
        P("shard", None),
        P("shard", None),
        P(),
        P("shard", None),
        P("shard"),
        P("shard", None),
        P("shard", None),
        P("shard", None),
        P(("rep", "shard"), None),
    )
    out_specs = (
        P(("rep", "shard"), None),
        P(("rep", "shard"), None),
        P("shard"),
        P("shard", None),
        P("shard", None),
        P("shard", None),
        P("shard", None),
        P("shard", None),
        P(),
        P("shard", None),
        P("shard"),
        P("shard", None),
        P("shard", None),
        P("shard", None),
    )

    def program(*arrays):
        return local(*arrays, reps=mesh.shape["rep"], count=mesh.shape["shard"])

    return jax.shard_map(program, mesh=mesh, in_specs=in_specs, out_specs=out_specs, check_vma=False)
```

```python
import jax
import jax.numpy as jnp
from jax import lax
from jax.experimental import pallas as pl
from jax.experimental.pallas import tpu as pltpu
from jax.sharding import PartitionSpec as P

PLEN = 64
CLEN = 64
NP = 2
NC = 4


EPS = 1e-06
NEGATIVE = -1e30


def chain_mask(prompt_ids, offsets):
    positions = jnp.arange(NP * PLEN + NC * CLEN, dtype=jnp.int32)
    in_prompt = positions < NP * PLEN
    after_prompts = positions - NP * PLEN
    sequence = jnp.where(in_prompt, positions // PLEN, NP + after_prompts // CLEN)
    within = jnp.where(in_prompt, positions % PLEN, after_prompts % CLEN)
    cont_index = sequence - NP
    selector = (cont_index[:, None] == jnp.arange(NC, dtype=jnp.int32)[None, :]).astype(jnp.int32)
    owner_id = jnp.where(in_prompt, -1, jnp.sum(selector * prompt_ids[None, :], axis=1))
    reach_end = jnp.sum(selector * offsets[None, :], axis=1)
    same_seq = (sequence[:, None] == sequence[None, :]) & (within[None, :] <= within[:, None])
    from_prompt = (owner_id[:, None] == sequence[None, :]) & (within[None, :] < reach_end[:, None])
    return same_seq | from_prompt


def normalize(values):
    inverse = lax.rsqrt(jnp.mean(values * values, axis=1, keepdims=True) + EPS)
    return (values * inverse, inverse)


def norm_back(grad_scaled, scaled, inverse):
    return inverse * (grad_scaled - scaled * jnp.mean(grad_scaled * scaled, axis=1, keepdims=True))


PROMPTS = NP * PLEN


def dot_nn(left_side, right_side):
    return jnp.dot(left_side, right_side, preferred_element_type=jnp.float32)


def dot_nt(left_side, right_side):
    return lax.dot_general(
        left_side, right_side, (((1,), (1,)), ((), ())), preferred_element_type=jnp.float32
    )


def dot_tn(left_side, right_side):
    return lax.dot_general(
        left_side, right_side, (((0,), (0,)), ((), ())), preferred_element_type=jnp.float32
    )


def key_mask(facts, block, rows):
    row = lax.broadcasted_iota(jnp.int32, (PROMPTS, PROMPTS), 0)
    col = lax.broadcasted_iota(jnp.int32, (PROMPTS, PROMPTS), 1)
    parts = [(row // PLEN == col // PLEN) & (col <= row)]
    within = lax.broadcasted_iota(jnp.int32, (CLEN, PLEN + CLEN), 0)
    key = lax.broadcasted_iota(jnp.int32, (CLEN, PLEN + CLEN), 1)
    for c in range(NC):
        reach = facts[block, NC + c]
        parts.append(((key < PLEN) & (key < reach)) | ((key >= PLEN) & (key - PLEN <= within)))
    return parts


def probs_of(query, keys, decay_col, decay_row, facts, block, masks, scale):
    logits = []
    for part, mask in enumerate(masks):
        if part == 0:
            rows = slice(0, PROMPTS)
            row_decay = decay_row[:, :PROMPTS]
        else:
            start = PROMPTS + (part - 1) * CLEN
            rows = slice(start, start + CLEN)
            first = facts[block, part - 1] == 0
            prompt_decay = jnp.where(first, decay_row[:, :PLEN], decay_row[:, PLEN:PROMPTS])
            row_decay = jnp.concatenate([prompt_decay, decay_row[:, start : start + CLEN]], axis=1)
        product = dot_nt(query[rows], keys[part]) * scale
        logits.append(jnp.where(mask, product + decay_col[rows] - row_decay, NEGATIVE))
    logits = jnp.concatenate(logits, axis=0)
    shifted = jnp.exp(logits - jnp.max(logits, axis=1, keepdims=True))
    return shifted / jnp.sum(shifted, axis=1, keepdims=True)


def part_rows(part):
    if part == 0:
        return slice(0, PROMPTS)
    start = PROMPTS + (part - 1) * CLEN
    return slice(start, start + CLEN)


def part_keys(ref, lanes, facts, block):
    parts = [ref[:PROMPTS, lanes]]
    for c in range(NC):
        start = pl.multiple_of(facts[block, c] * PLEN, PLEN)
        own = part_rows(c + 1)
        parts.append(jnp.concatenate([ref[pl.ds(start, PLEN), lanes], ref[own, lanes]], axis=0))
    return parts


def attend(qkv, decay_cols, decay_rows, facts, heads, head_dim, team, rows):
    width = heads * head_dim
    scale = head_dim ** (-0.5)

    def body(facts_ref, qkv_ref, col_ref, row_ref, out_ref):
        block = pl.program_id(0)
        masks = key_mask(facts_ref, block, rows)
        for h in range(heads):
            lanes = slice(h * head_dim, (h + 1) * head_dim)
            key_lanes = slice(width + h * head_dim, width + (h + 1) * head_dim)
            value_lanes = slice(2 * width + h * head_dim, 2 * width + (h + 1) * head_dim)
            keys = part_keys(qkv_ref, key_lanes, facts_ref, block)
            values = part_keys(qkv_ref, value_lanes, facts_ref, block)
            probs = probs_of(
                qkv_ref[:, lanes], keys, col_ref[0, :, h : h + 1], row_ref[0, h : h + 1, :],
                facts_ref, block, masks, scale,
            ).astype(jnp.bfloat16)
            for part in range(NC + 1):
                at = part_rows(part)
                out_ref[at, lanes] = dot_nn(probs[at], values[part])

    return pl.pallas_call(
        body,
        grid_spec=pltpu.PrefetchScalarGridSpec(
            num_scalar_prefetch=1,
            grid=(team,),
            in_specs=[
                pl.BlockSpec((rows, qkv.shape[1]), lambda b, f: (b, 0)),
                pl.BlockSpec((1, rows, heads), lambda b, f: (b, 0, 0)),
                pl.BlockSpec((1, heads, rows), lambda b, f: (b, 0, 0)),
            ],
            out_specs=pl.BlockSpec((rows, width), lambda b, f: (b, 0)),
        ),
        out_shape=jax.ShapeDtypeStruct((team * rows, width), jnp.float32),
        cost_estimate=pl.CostEstimate(
            flops=64 * team * rows * rows * width,
            bytes_accessed=8 * team * rows * width * 2,
            transcendentals=team * rows * PROMPTS * heads,
        ),
        name="attend",
    )(facts, qkv, decay_cols, decay_rows)


def attend_back(qkv, grad_attended, decay_cols, decay_rows, facts, heads, head_dim, team, rows):
    width = heads * head_dim
    scale = head_dim ** (-0.5)

    def body(facts_ref, qkv_ref, grad_ref, col_ref, row_ref, out_ref, sum_ref, low_ref, key_acc, value_acc):
        block = pl.program_id(0)
        masks = key_mask(facts_ref, block, rows)
        for h in range(heads):
            lanes = slice(h * head_dim, (h + 1) * head_dim)
            key_lanes = slice(width + h * head_dim, width + (h + 1) * head_dim)
            value_lanes = slice(2 * width + h * head_dim, 2 * width + (h + 1) * head_dim)
            keys = part_keys(qkv_ref, key_lanes, facts_ref, block)
            values = part_keys(qkv_ref, value_lanes, facts_ref, block)
            query = qkv_ref[:, lanes]
            grad = grad_ref[:, lanes]
            probs = probs_of(
                query, keys, col_ref[0, :, h : h + 1], row_ref[0, h : h + 1, :],
                facts_ref, block, masks, scale,
            )
            grad_probs = jnp.concatenate(
                [dot_nt(grad[part_rows(p)], values[p]) for p in range(NC + 1)], axis=0
            )
            mean = jnp.sum(probs * grad_probs, axis=1, keepdims=True)
            grad_logits = probs * (grad_probs - mean)
            sum_ref[0, :, h : h + 1] = jnp.sum(grad_logits, axis=1, keepdims=True)
            probs_low = probs.astype(jnp.bfloat16)
            grad_qk = (grad_logits * scale).astype(jnp.bfloat16)
            prompt_sum = jnp.sum(grad_logits[:PROMPTS], axis=0, keepdims=True)
            for part in range(NC + 1):
                at = part_rows(part)
                out_ref[at, lanes] = dot_nn(grad_qk[at], keys[part]).astype(jnp.bfloat16)
                grad_keys = dot_tn(grad_qk[at], query[at])
                grad_values = dot_tn(probs_low[at], grad[at])
                if part == 0:
                    key_acc[...] = grad_keys
                    value_acc[...] = grad_values
                    continue
                start = pl.multiple_of(facts_ref[block, part - 1] * PLEN, PLEN)
                key_acc[pl.ds(start, PLEN), :] += grad_keys[:PLEN]
                value_acc[pl.ds(start, PLEN), :] += grad_values[:PLEN]
                out_ref[at, key_lanes] = grad_keys[PLEN:].astype(jnp.bfloat16)
                out_ref[at, value_lanes] = grad_values[PLEN:].astype(jnp.bfloat16)
                column = jnp.sum(grad_logits[at], axis=0, keepdims=True)
                first = facts_ref[block, part - 1] == 0
                nothing = jnp.zeros((1, PLEN), jnp.float32)
                prompt_sum += jnp.concatenate(
                    [
                        jnp.where(first, column[:, :PLEN], nothing),
                        jnp.where(first, nothing, column[:, :PLEN]),
                    ],
                    axis=1,
                )
                low_ref[0, h : h + 1, at] = column[:, PLEN:]
            low_ref[0, h : h + 1, :PROMPTS] = prompt_sum
            out_ref[:PROMPTS, key_lanes] = key_acc[...].astype(jnp.bfloat16)
            out_ref[:PROMPTS, value_lanes] = value_acc[...].astype(jnp.bfloat16)

    return pl.pallas_call(
        body,
        grid_spec=pltpu.PrefetchScalarGridSpec(
            num_scalar_prefetch=1,
            grid=(team,),
            in_specs=[
                pl.BlockSpec((rows, qkv.shape[1]), lambda b, f: (b, 0)),
                pl.BlockSpec((rows, width), lambda b, f: (b, 0)),
                pl.BlockSpec((1, rows, heads), lambda b, f: (b, 0, 0)),
                pl.BlockSpec((1, heads, rows), lambda b, f: (b, 0, 0)),
            ],
            out_specs=[
                pl.BlockSpec((rows, 3 * width), lambda b, f: (b, 0)),
                pl.BlockSpec((1, rows, heads), lambda b, f: (b, 0, 0)),
                pl.BlockSpec((1, heads, rows), lambda b, f: (b, 0, 0)),
            ],
            scratch_shapes=[
                pltpu.VMEM((PROMPTS, head_dim), jnp.float32),
                pltpu.VMEM((PROMPTS, head_dim), jnp.float32),
            ],
        ),
        out_shape=[
            jax.ShapeDtypeStruct((team * rows, 3 * width), jnp.bfloat16),
            jax.ShapeDtypeStruct((team, rows, heads), jnp.float32),
            jax.ShapeDtypeStruct((team, heads, rows), jnp.float32),
        ],
        cost_estimate=pl.CostEstimate(
            flops=80 * team * rows * rows * width,
            bytes_accessed=7 * team * rows * width * 2,
            transcendentals=team * rows * PROMPTS * heads,
        ),
        name="attend_back",
    )(facts, qkv, grad_attended, decay_cols, decay_rows)


def matmul(left_side, right_side):
    return jnp.dot(left_side, right_side, preferred_element_type=jnp.float32)


def matmul_tn(left_side, right_side):
    return lax.dot_general(
        left_side, right_side, (((0,), (0,)), ((), ())), preferred_element_type=jnp.float32
    )


def matmul_nt(left_side, right_side):
    return lax.dot_general(
        left_side, right_side, (((1,), (1,)), ((), ())), preferred_element_type=jnp.float32
    )


def line_groups(count):
    step = count // 4
    return [[first + step * k for k in range(4)] for first in range(step)]


def middle_strides(count):
    strides = []
    step = count // 8
    while step > 1:
        strides.append(step)
        step //= 2
    return strides


def swap_pairs(count, step):
    return [(s, s ^ step) for s in range(count)]


def both(low_first, mine, other, axis=0):
    return jnp.stack(
        [jnp.where(low_first, mine, other), jnp.where(low_first, other, mine)], axis=axis
    )


def pick(values, at, axis):
    return lax.dynamic_index_in_dim(values, at, axis, keepdims=False)


def add_low(left_side, right_side):
    return (left_side.astype(jnp.float32) + right_side.astype(jnp.float32)).astype(jnp.bfloat16)


def after(values, *others):
    return lax.optimization_barrier((values,) + others)[0]


def gather_line(block, count):
    return lax.all_gather(block, "shard", axis=0, tiled=True, axis_index_groups=line_groups(count))


def gather_rest(line, count, index, *others):
    width = line.shape[1]
    held = line.reshape(4, -1, width)
    for step in reversed(middle_strides(count)):
        other = lax.ppermute(held, "shard", swap_pairs(count, step))
        if others:
            other = after(other, *others)
        held = both((index // step) % 2 == 0, held, other, axis=1).reshape(4, -1, width)
    return held.reshape(-1, width), other


def scatter_rest(values, count, index):
    width = values.shape[1]
    held = values.reshape(4, -1, width)
    strides = middle_strides(count)
    parts = []
    for step in strides:
        if parts:
            held = add_low(*parts)
        at = (index // step) % 2
        halves = held.reshape(4, 2, -1, width)
        other = lax.ppermute(pick(halves, 1 - at, 1), "shard", swap_pairs(count, step))
        parts = [pick(halves, at, 1), other]

    def finish(*others):
        return add_low(parts[0], after(parts[1], *others)).reshape(-1, width)

    return finish


def scatter_line(values, count):
    return lax.psum_scatter(
        values, "shard", scatter_dimension=0, tiled=True, axis_index_groups=line_groups(count)
    )


def sum_all(values, count, reps):
    total = values
    for step in middle_strides(count):
        total = total + lax.ppermute(total, "shard", swap_pairs(count, step))
    near = total
    for step in (count // 2, count // 4, 1):
        total = total + lax.ppermute(total, "shard", swap_pairs(count, step))
    step = 1
    while step < reps:
        total = total + lax.ppermute(total, "rep", [(r, r ^ step) for r in range(reps)])
        step *= 2
    return near, total[0]


def local(
    tokens,
    prompt_ids,
    seq_offsets,
    attn_gain,
    w_query,
    w_key,
    w_value,
    w_outgate,
    w_forget,
    forget_bias,
    w_output,
    ffn_gain,
    w_gate,
    w_up,
    w_down,
    cotangent,
    *,
    reps,
    count,
):
    own_rows = tokens.shape[0]
    model_width = tokens.shape[1]
    head_count = w_forget.shape[1]
    head_dim = model_width // head_count
    score_scale = head_dim ** (-0.5)
    team = 4
    core = lax.axis_index("rep") % 2
    index = lax.axis_index("shard")
    side = index % 2
    rank = 2 * side + core
    quarter = model_width // team
    heads = head_count // team
    shard_rows = w_query.shape[0]
    shard_ff = w_down.shape[0]
    unit = shard_ff // 2
    quarter_ff = w_gate.shape[1] // team
    core_pairs = [(r, r ^ 1) for r in range(reps)]
    side_pairs = [(s, s ^ 1) for s in range(count)]

    def swap_core(values):
        return lax.ppermute(values, "rep", core_pairs)

    def swap_side(values):
        return lax.ppermute(values, "shard", side_pairs)

    def team_rows(values, *others):
        pair = jnp.concatenate([values, swap_side(values)], axis=0)
        if others:
            pair = after(pair, *others)
        return jnp.concatenate([pair, swap_core(pair)], axis=0)

    def core_sum(partial):
        half = 2 * own_rows
        return partial[:half] + swap_core(partial[half:].astype(jnp.bfloat16)).astype(jnp.float32)

    def side_sum(pair):
        return pair[:own_rows] + swap_side(pair[own_rows:].astype(jnp.bfloat16)).astype(jnp.float32)

    def team_sum(partial):
        return side_sum(core_sum(partial))

    def cols_of(values, who):
        return lax.dynamic_slice_in_dim(values, who * quarter, quarter, axis=1)

    def units_of(values, which_side):
        cut = values.reshape(values.shape[0], count // 2, 2, 2, unit)
        return pick(pick(cut, core, 3), which_side, 2).reshape(values.shape[0], quarter_ff)

    def pair_rows(mine, sent):
        return both(side == 0, mine, swap_side(sent)).reshape(-1, mine.shape[1])

    small = jnp.concatenate(
        [
            w_forget,
            attn_gain[:, None],
            ffn_gain[:, None],
            jnp.zeros((shard_rows, 128 - head_count - 2), jnp.bfloat16),
        ],
        axis=1,
    )
    far_rank = rank ^ 2

    def columns(who, *weights):
        return [cols_of(w, who) for w in weights]

    first_block = pair_rows(
        jnp.concatenate(columns(rank, w_query, w_key, w_value) + [small], axis=1),
        jnp.concatenate(columns(far_rank, w_query, w_key, w_value) + [small], axis=1),
    )
    rest_block = pair_rows(
        jnp.concatenate(
            columns(rank, w_outgate, w_output) + [units_of(w_gate, side), units_of(w_up, side)],
            axis=1,
        ),
        after(
            jnp.concatenate(
                columns(far_rank, w_outgate, w_output)
                + [units_of(w_gate, 1 - side), units_of(w_up, 1 - side)],
                axis=1,
            ),
            first_block,
        ),
    )
    first_line = gather_line(first_block, count)
    second_line = gather_line(after(rest_block[:, : 2 * quarter], first_line), count)
    gate_line = gather_line(
        after(rest_block[:, 2 * quarter : 2 * quarter + quarter_ff], second_line), count
    )
    up_line = gather_line(after(rest_block[:, 2 * quarter + quarter_ff :], gate_line), count)
    down_line = gather_line(
        after(lax.dynamic_slice_in_dim(w_down, core * unit, unit, axis=0), up_line), count
    )
    first, _ = gather_rest(first_line, count, index)
    gate_w, gate_last = gather_rest(gate_line, count, index)
    up_w, up_last = gather_rest(up_line, count, index)
    down_w, _ = gather_rest(down_line, count, index)

    forget_w = lax.dynamic_slice_in_dim(
        first[:, 3 * quarter : 3 * quarter + head_count], rank * heads, heads, axis=1
    )
    gain_one = first[:, 3 * quarter + head_count].astype(jnp.float32)
    gain_two = first[:, 3 * quarter + head_count + 1].astype(jnp.float32)
    def turn_rows(values):
        cut = values.reshape(2, 2, quarter, quarter)
        mine = pick(cut, side, 0)
        pair = both(side == 0, mine, swap_side(pick(cut, 1 - side, 0)))
        kept = pick(pair, core, 1)
        quad = both(core == 0, kept, swap_core(pick(pair, 1 - core, 1)))
        return jnp.transpose(quad, (2, 1, 0, 3)).reshape(quarter, model_width)

    def turn_cols(values):
        cut = values.reshape(quarter, 2, 2, quarter)
        mine = pick(cut, core, 2)
        pair = both(core == 0, mine, swap_core(pick(cut, 1 - core, 2)))
        kept = pick(pair, side, 2)
        quad = both(side == 0, kept, swap_side(pick(pair, 1 - side, 2)))
        return quad.reshape(model_width, quarter)

    tokens_all = team_rows(after(tokens, rest_block), first_line)
    cotangent_all = team_rows(after(cotangent, tokens_all))
    facts_all = team_rows(jnp.concatenate([prompt_ids[0], seq_offsets[0]])[None, :])
    chain_ok = jnp.stack([chain_mask(facts_all[b, :NC], facts_all[b, NC:]) for b in range(team)])
    chain_float = chain_ok.astype(jnp.float32)

    inputs_all = tokens_all.astype(jnp.float32)
    scaled_all, inverse_all = normalize(inputs_all)
    scaled1 = scaled_all[:own_rows]
    inverse1 = inverse_all[:own_rows]
    inputs = inputs_all[:own_rows]
    normed1 = after(
        (scaled_all * gain_one).astype(jnp.bfloat16), second_line, cotangent_all
    )
    row_count = normed1.shape[0]

    qkv_low = matmul(normed1, first[:, : 3 * quarter]).astype(jnp.bfloat16)
    second = gather_rest(second_line, count, index, qkv_low)[0]
    outgate_w = second[:, :quarter]
    output_w = turn_rows(second[:, quarter:])
    outgate_pre = matmul(normed1, outgate_w)
    bias_mine = lax.dynamic_slice_in_dim(
        forget_bias.astype(jnp.float32), rank * heads, heads, axis=0
    )
    forget_in = matmul(normed1, forget_w) + bias_mine[None, :]
    log_forget = jax.nn.log_sigmoid(forget_in).reshape(team, own_rows, heads)
    decay_sum = jnp.einsum(
        "bij,bjh->bhi", chain_float, log_forget, precision=lax.Precision.HIGHEST
    )

    decay_cols = jnp.transpose(decay_sum, (0, 2, 1))
    attended = attend(
        after(qkv_low, gate_line),
        decay_cols,
        decay_sum,
        facts_all,
        heads,
        head_dim,
        team,
        own_rows,
    )
    gate_open = jax.nn.sigmoid(outgate_pre)
    gated_low = (after(attended, up_line, gate_last) * gate_open).astype(jnp.bfloat16)

    residual = inputs + after(team_sum(matmul(gated_low, output_w)), up_last)
    scaled2, inverse2 = normalize(residual)
    normed2 = after(team_rows((scaled2 * gain_two).astype(jnp.bfloat16)), down_line)
    gate_pre = matmul(normed2, gate_w)
    up_pre = matmul(normed2, up_w)
    sig_gate = jax.nn.sigmoid(gate_pre)
    silu_gate = gate_pre * sig_gate
    act_low = (silu_gate * up_pre).astype(jnp.bfloat16)
    grad_act = matmul_nt(cotangent_all, down_w)
    grad_gate = (grad_act * up_pre * sig_gate * (1.0 + gate_pre * (1.0 - sig_gate))).astype(
        jnp.bfloat16
    )
    grad_up = (grad_act * silu_gate).astype(jnp.bfloat16)
    down_sum = scatter_rest(matmul_tn(act_low, cotangent_all).astype(jnp.bfloat16), count, index)
    pair_normed2 = core_sum(matmul_nt(grad_gate, gate_w) + matmul_nt(grad_up, up_w))
    normed2_late = after(normed2, pair_normed2)
    part_gate_w = matmul_tn(normed2_late, grad_gate).astype(jnp.bfloat16)
    part_up_w = matmul_tn(normed2_late, grad_up).astype(jnp.bfloat16)
    grad_normed2 = after(side_sum(pair_normed2), part_gate_w, part_up_w)
    down_held = down_sum(grad_normed2)
    grad_down = scatter_line(down_held, count)
    gate_sum = scatter_rest(after(part_gate_w, part_up_w), count, index)
    up_sum = scatter_rest(part_up_w, count, index)
    grad_resid = cotangent.astype(jnp.float32) + norm_back(
        grad_normed2 * gain_two, scaled2, inverse2
    )
    grad_attn_own = grad_resid.astype(jnp.bfloat16)
    pair_out = core_sum(matmul(after(act_low, grad_attn_own, down_held), down_w))
    gate_held = gate_sum()
    grad_gate_w = scatter_line(gate_held, count)
    grad_attn = after(team_rows(grad_attn_own, gate_held), grad_down)
    grad_gated = matmul_nt(grad_attn, output_w)
    grad_output_cols = turn_cols(matmul_tn(gated_low, grad_attn).astype(jnp.bfloat16))
    grad_attended = (grad_gated * gate_open).astype(jnp.bfloat16)
    grad_outgate = (grad_gated * attended * gate_open * (1.0 - gate_open)).astype(jnp.bfloat16)
    up_held = up_sum(grad_outgate)
    grad_outgate_w = matmul_tn(after(normed1, up_held), grad_outgate).astype(jnp.bfloat16)
    part_second_w = jnp.concatenate([grad_outgate_w, grad_output_cols], axis=1)
    second_sum = scatter_rest(part_second_w, count, index)
    grad_up_w = scatter_line(up_held, count)
    grad_qkv, grad_logit_rows, grad_logit_cols = attend_back(
        qkv_low,
        after(grad_attended, up_held, part_second_w),
        decay_cols,
        decay_sum,
        facts_all,
        heads,
        head_dim,
        team,
        own_rows,
    )
    second_held = second_sum(grad_qkv)
    grad_qkv = after(grad_qkv, grad_gate_w, second_held)
    sum_second = scatter_line(second_held, count)
    layer_out = (residual + side_sum(after(pair_out, grad_qkv))).astype(jnp.bfloat16)
    grad_decay = jnp.transpose(grad_logit_rows, (0, 2, 1)) - grad_logit_cols
    grad_log_forget = jnp.einsum(
        "bij,bhi->bjh", chain_float, grad_decay, precision=lax.Precision.HIGHEST
    ).reshape(row_count, heads)
    grad_forget_in = grad_log_forget * jax.nn.sigmoid(-forget_in)
    bias_sum = lax.dynamic_update_slice_in_dim(
        jnp.zeros((head_count,), jnp.float32),
        jnp.sum(grad_forget_in, axis=0),
        rank * heads,
        axis=0,
    )
    bias_near, grad_bias = sum_all(bias_sum[None, :], count, reps)
    grad_forget_low = lax.dynamic_update_slice_in_dim(
        jnp.zeros((row_count, small.shape[1]), jnp.bfloat16),
        grad_forget_in.astype(jnp.bfloat16),
        rank * heads,
        axis=1,
    )
    grad_first = jnp.concatenate([grad_qkv, grad_forget_low], axis=1)
    part_first_w = matmul_tn(normed1, grad_first).astype(jnp.bfloat16)
    first_sum = scatter_rest(after(part_first_w, bias_near), count, index)
    part_normed1 = matmul_nt(after(grad_first, part_first_w), first) + matmul_nt(
        grad_outgate, outgate_w
    )
    first_held = first_sum()
    grad_normed1 = team_sum(after(part_normed1, first_held))
    tokens_grad = grad_resid + norm_back(grad_normed1 * gain_one, scaled1, inverse1)
    sum_first = scatter_line(first_held, count)
    grad_down = after(grad_down, part_first_w)
    grad_gate_w = after(grad_gate_w, part_first_w)
    grad_up_w = after(grad_up_w, grad_normed1)
    sum_second = after(sum_second, grad_normed1)

    def replicas(values):
        total = values
        step = 2
        while step < reps:
            other = lax.ppermute(total, "rep", [(r, r ^ step) for r in range(reps)])
            total = add_low(total, other)
            step *= 2
        return total

    def own_of(values):
        pair = replicas(values).reshape(2, shard_rows, values.shape[1])
        sides = both(side == 0, pick(pair, side, 0), swap_side(pick(pair, 1 - side, 0)))
        cores = both(core == 0, sides, swap_core(sides))
        return jnp.transpose(cores.astype(jnp.float32), (1, 0, 2, 3))

    def whole_cols(own):
        parts = own.shape[3] // quarter
        quad = own.reshape(2, 2, shard_rows, parts, quarter)
        quad = jnp.transpose(quad, (3, 2, 0, 1, 4)).reshape(parts, shard_rows, model_width)
        return [quad[p] for p in range(parts)]

    def whole_units(values):
        quad = own_of(values).reshape(2, 2, shard_rows, count // 2, unit)
        return jnp.transpose(quad, (2, 3, 0, 1, 4)).reshape(shard_rows, team * quarter_ff)

    down_mine = replicas(grad_down)
    down_own = both(core == 0, down_mine, swap_core(down_mine)).astype(jnp.float32)
    first_own = own_of(sum_first)
    query_g, key_g, value_g = whole_cols(first_own[..., : 3 * quarter])
    forget_g = jnp.sum(first_own[..., 3 * quarter : 3 * quarter + head_count], axis=(0, 1))
    outgate_g, output_g = whole_cols(own_of(sum_second))
    gate_g = whole_units(grad_gate_w)
    up_g = whole_units(grad_up_w)

    def gain_grad(gain, *pairs):
        total = sum(jnp.sum(w.astype(jnp.float32) * grad, axis=1) for w, grad in pairs)
        return total / gain.astype(jnp.float32)

    gain_one_g = gain_grad(
        attn_gain,
        (w_query, query_g),
        (w_key, key_g),
        (w_value, value_g),
        (w_outgate, outgate_g),
        (w_forget, forget_g),
    )
    gain_two_g = gain_grad(ffn_gain, (w_gate, gate_g), (w_up, up_g))
    return (
        layer_out,
        tokens_grad,
        gain_one_g,
        query_g,
        key_g,
        value_g,
        outgate_g,
        forget_g,
        grad_bias,
        output_g,
        gain_two_g,
        gate_g,
        up_g,
        down_own.reshape(shard_ff, model_width),
    )


def solution(mesh):
    in_specs = (
        P(("rep", "shard"), None),
        P(("rep", "shard"), None),
        P(("rep", "shard"), None),
        P("shard"),
        P("shard", None),
        P("shard", None),
        P("shard", None),
        P("shard", None),
        P("shard", None),
        P(),
        P("shard", None),
        P("shard"),
        P("shard", None),
        P("shard", None),
        P("shard", None),
        P(("rep", "shard"), None),
    )
    out_specs = (
        P(("rep", "shard"), None),
        P(("rep", "shard"), None),
        P("shard"),
        P("shard", None),
        P("shard", None),
        P("shard", None),
        P("shard", None),
        P("shard", None),
        P(),
        P("shard", None),
        P("shard"),
        P("shard", None),
        P("shard", None),
        P("shard", None),
    )

    def program(*arrays):
        return local(*arrays, reps=mesh.shape["rep"], count=mesh.shape["shard"])

    return jax.shard_map(program, mesh=mesh, in_specs=in_specs, out_specs=out_specs, check_vma=False)
```

```python
import jax
import jax.numpy as jnp
from jax import lax
from jax.experimental import pallas as pl
from jax.experimental.pallas import tpu as pltpu
from jax.sharding import PartitionSpec as P

PLEN = 64
CLEN = 64
NP = 2
NC = 4


EPS = 1e-06
NEGATIVE = -1e30


def chain_mask(prompt_ids, offsets):
    positions = jnp.arange(NP * PLEN + NC * CLEN, dtype=jnp.int32)
    in_prompt = positions < NP * PLEN
    after_prompts = positions - NP * PLEN
    sequence = jnp.where(in_prompt, positions // PLEN, NP + after_prompts // CLEN)
    within = jnp.where(in_prompt, positions % PLEN, after_prompts % CLEN)
    cont_index = sequence - NP
    selector = (cont_index[:, None] == jnp.arange(NC, dtype=jnp.int32)[None, :]).astype(jnp.int32)
    owner_id = jnp.where(in_prompt, -1, jnp.sum(selector * prompt_ids[None, :], axis=1))
    reach_end = jnp.sum(selector * offsets[None, :], axis=1)
    same_seq = (sequence[:, None] == sequence[None, :]) & (within[None, :] <= within[:, None])
    from_prompt = (owner_id[:, None] == sequence[None, :]) & (within[None, :] < reach_end[:, None])
    return same_seq | from_prompt


def normalize(values):
    inverse = lax.rsqrt(jnp.mean(values * values, axis=1, keepdims=True) + EPS)
    return (values * inverse, inverse)


def norm_back(grad_scaled, scaled, inverse):
    return inverse * (grad_scaled - scaled * jnp.mean(grad_scaled * scaled, axis=1, keepdims=True))


PROMPTS = NP * PLEN


def dot_nn(left_side, right_side):
    return jnp.dot(left_side, right_side, preferred_element_type=jnp.float32)


def dot_nt(left_side, right_side):
    return lax.dot_general(
        left_side, right_side, (((1,), (1,)), ((), ())), preferred_element_type=jnp.float32
    )


def dot_tn(left_side, right_side):
    return lax.dot_general(
        left_side, right_side, (((0,), (0,)), ((), ())), preferred_element_type=jnp.float32
    )


def key_mask(facts, block, rows):
    row = lax.broadcasted_iota(jnp.int32, (PROMPTS, PROMPTS), 0)
    col = lax.broadcasted_iota(jnp.int32, (PROMPTS, PROMPTS), 1)
    parts = [(row // PLEN == col // PLEN) & (col <= row)]
    within = lax.broadcasted_iota(jnp.int32, (CLEN, PLEN + CLEN), 0)
    key = lax.broadcasted_iota(jnp.int32, (CLEN, PLEN + CLEN), 1)
    for c in range(NC):
        reach = facts[block, NC + c]
        parts.append(((key < PLEN) & (key < reach)) | ((key >= PLEN) & (key - PLEN <= within)))
    return parts


def probs_of(query, keys, decay_col, decay_row, facts, block, masks, scale):
    logits = []
    for part, mask in enumerate(masks):
        if part == 0:
            rows = slice(0, PROMPTS)
            row_decay = decay_row[:, :PROMPTS]
        else:
            start = PROMPTS + (part - 1) * CLEN
            rows = slice(start, start + CLEN)
            first = facts[block, part - 1] == 0
            prompt_decay = jnp.where(first, decay_row[:, :PLEN], decay_row[:, PLEN:PROMPTS])
            row_decay = jnp.concatenate([prompt_decay, decay_row[:, start : start + CLEN]], axis=1)
        product = dot_nt(query[rows], keys[part]) * scale
        logits.append(jnp.where(mask, product + decay_col[rows] - row_decay, NEGATIVE))
    logits = jnp.concatenate(logits, axis=0)
    shifted = jnp.exp(logits - jnp.max(logits, axis=1, keepdims=True))
    return shifted / jnp.sum(shifted, axis=1, keepdims=True)


def part_rows(part):
    if part == 0:
        return slice(0, PROMPTS)
    start = PROMPTS + (part - 1) * CLEN
    return slice(start, start + CLEN)


def part_keys(ref, lanes, facts, block):
    parts = [ref[:PROMPTS, lanes]]
    for c in range(NC):
        start = pl.multiple_of(facts[block, c] * PLEN, PLEN)
        own = part_rows(c + 1)
        parts.append(jnp.concatenate([ref[pl.ds(start, PLEN), lanes], ref[own, lanes]], axis=0))
    return parts


def attend(qkv, decay_cols, decay_rows, facts, heads, head_dim, team, rows):
    width = heads * head_dim
    scale = head_dim ** (-0.5)

    def body(facts_ref, qkv_ref, col_ref, row_ref, out_ref):
        block = pl.program_id(0)
        masks = key_mask(facts_ref, block, rows)
        for h in range(heads):
            lanes = slice(h * head_dim, (h + 1) * head_dim)
            key_lanes = slice(width + h * head_dim, width + (h + 1) * head_dim)
            value_lanes = slice(2 * width + h * head_dim, 2 * width + (h + 1) * head_dim)
            keys = part_keys(qkv_ref, key_lanes, facts_ref, block)
            values = part_keys(qkv_ref, value_lanes, facts_ref, block)
            probs = probs_of(
                qkv_ref[:, lanes], keys, col_ref[0, :, h : h + 1], row_ref[0, h : h + 1, :],
                facts_ref, block, masks, scale,
            ).astype(jnp.bfloat16)
            for part in range(NC + 1):
                at = part_rows(part)
                out_ref[at, lanes] = dot_nn(probs[at], values[part])

    return pl.pallas_call(
        body,
        grid_spec=pltpu.PrefetchScalarGridSpec(
            num_scalar_prefetch=1,
            grid=(team,),
            in_specs=[
                pl.BlockSpec((rows, qkv.shape[1]), lambda b, f: (b, 0)),
                pl.BlockSpec((1, rows, heads), lambda b, f: (b, 0, 0)),
                pl.BlockSpec((1, heads, rows), lambda b, f: (b, 0, 0)),
            ],
            out_specs=pl.BlockSpec((rows, width), lambda b, f: (b, 0)),
        ),
        out_shape=jax.ShapeDtypeStruct((team * rows, width), jnp.float32),
        cost_estimate=pl.CostEstimate(
            flops=64 * team * rows * rows * width,
            bytes_accessed=8 * team * rows * width * 2,
            transcendentals=team * rows * PROMPTS * heads,
        ),
        name="attend",
    )(facts, qkv, decay_cols, decay_rows)


def attend_back(qkv, grad_attended, decay_cols, decay_rows, facts, heads, head_dim, team, rows):
    width = heads * head_dim
    scale = head_dim ** (-0.5)

    def body(facts_ref, qkv_ref, grad_ref, col_ref, row_ref, out_ref, sum_ref, low_ref, key_acc, value_acc):
        block = pl.program_id(0)
        masks = key_mask(facts_ref, block, rows)
        for h in range(heads):
            lanes = slice(h * head_dim, (h + 1) * head_dim)
            key_lanes = slice(width + h * head_dim, width + (h + 1) * head_dim)
            value_lanes = slice(2 * width + h * head_dim, 2 * width + (h + 1) * head_dim)
            keys = part_keys(qkv_ref, key_lanes, facts_ref, block)
            values = part_keys(qkv_ref, value_lanes, facts_ref, block)
            query = qkv_ref[:, lanes]
            grad = grad_ref[:, lanes]
            probs = probs_of(
                query, keys, col_ref[0, :, h : h + 1], row_ref[0, h : h + 1, :],
                facts_ref, block, masks, scale,
            )
            grad_probs = jnp.concatenate(
                [dot_nt(grad[part_rows(p)], values[p]) for p in range(NC + 1)], axis=0
            )
            mean = jnp.sum(probs * grad_probs, axis=1, keepdims=True)
            grad_logits = probs * (grad_probs - mean)
            sum_ref[0, :, h : h + 1] = jnp.sum(grad_logits, axis=1, keepdims=True)
            probs_low = probs.astype(jnp.bfloat16)
            grad_qk = (grad_logits * scale).astype(jnp.bfloat16)
            prompt_sum = jnp.sum(grad_logits[:PROMPTS], axis=0, keepdims=True)
            for part in range(NC + 1):
                at = part_rows(part)
                out_ref[at, lanes] = dot_nn(grad_qk[at], keys[part]).astype(jnp.bfloat16)
                grad_keys = dot_tn(grad_qk[at], query[at])
                grad_values = dot_tn(probs_low[at], grad[at])
                if part == 0:
                    key_acc[...] = grad_keys
                    value_acc[...] = grad_values
                    continue
                start = pl.multiple_of(facts_ref[block, part - 1] * PLEN, PLEN)
                key_acc[pl.ds(start, PLEN), :] += grad_keys[:PLEN]
                value_acc[pl.ds(start, PLEN), :] += grad_values[:PLEN]
                out_ref[at, key_lanes] = grad_keys[PLEN:].astype(jnp.bfloat16)
                out_ref[at, value_lanes] = grad_values[PLEN:].astype(jnp.bfloat16)
                column = jnp.sum(grad_logits[at], axis=0, keepdims=True)
                first = facts_ref[block, part - 1] == 0
                nothing = jnp.zeros((1, PLEN), jnp.float32)
                prompt_sum += jnp.concatenate(
                    [
                        jnp.where(first, column[:, :PLEN], nothing),
                        jnp.where(first, nothing, column[:, :PLEN]),
                    ],
                    axis=1,
                )
                low_ref[0, h : h + 1, at] = column[:, PLEN:]
            low_ref[0, h : h + 1, :PROMPTS] = prompt_sum
            out_ref[:PROMPTS, key_lanes] = key_acc[...].astype(jnp.bfloat16)
            out_ref[:PROMPTS, value_lanes] = value_acc[...].astype(jnp.bfloat16)

    return pl.pallas_call(
        body,
        grid_spec=pltpu.PrefetchScalarGridSpec(
            num_scalar_prefetch=1,
            grid=(team,),
            in_specs=[
                pl.BlockSpec((rows, qkv.shape[1]), lambda b, f: (b, 0)),
                pl.BlockSpec((rows, width), lambda b, f: (b, 0)),
                pl.BlockSpec((1, rows, heads), lambda b, f: (b, 0, 0)),
                pl.BlockSpec((1, heads, rows), lambda b, f: (b, 0, 0)),
            ],
            out_specs=[
                pl.BlockSpec((rows, 3 * width), lambda b, f: (b, 0)),
                pl.BlockSpec((1, rows, heads), lambda b, f: (b, 0, 0)),
                pl.BlockSpec((1, heads, rows), lambda b, f: (b, 0, 0)),
            ],
            scratch_shapes=[
                pltpu.VMEM((PROMPTS, head_dim), jnp.float32),
                pltpu.VMEM((PROMPTS, head_dim), jnp.float32),
            ],
        ),
        out_shape=[
            jax.ShapeDtypeStruct((team * rows, 3 * width), jnp.bfloat16),
            jax.ShapeDtypeStruct((team, rows, heads), jnp.float32),
            jax.ShapeDtypeStruct((team, heads, rows), jnp.float32),
        ],
        cost_estimate=pl.CostEstimate(
            flops=80 * team * rows * rows * width,
            bytes_accessed=7 * team * rows * width * 2,
            transcendentals=team * rows * PROMPTS * heads,
        ),
        name="attend_back",
    )(facts, qkv, grad_attended, decay_cols, decay_rows)


def matmul(left_side, right_side):
    return jnp.dot(left_side, right_side, preferred_element_type=jnp.float32)


def matmul_tn(left_side, right_side):
    return lax.dot_general(
        left_side, right_side, (((0,), (0,)), ((), ())), preferred_element_type=jnp.float32
    )


def matmul_nt(left_side, right_side):
    return lax.dot_general(
        left_side, right_side, (((1,), (1,)), ((), ())), preferred_element_type=jnp.float32
    )


def line_groups(count):
    step = count // 4
    return [[first + step * k for k in range(4)] for first in range(step)]


def middle_strides(count):
    strides = []
    step = count // 8
    while step > 1:
        strides.append(step)
        step //= 2
    return strides


def swap_pairs(count, step):
    return [(s, s ^ step) for s in range(count)]


def both(low_first, mine, other, axis=0):
    return jnp.stack(
        [jnp.where(low_first, mine, other), jnp.where(low_first, other, mine)], axis=axis
    )


def pick(values, at, axis):
    return lax.dynamic_index_in_dim(values, at, axis, keepdims=False)


def add_low(left_side, right_side):
    return (left_side.astype(jnp.float32) + right_side.astype(jnp.float32)).astype(jnp.bfloat16)


def after(values, *others):
    return lax.optimization_barrier((values,) + others)[0]


def gather_line(block, count):
    return lax.all_gather(block, "shard", axis=0, tiled=True, axis_index_groups=line_groups(count))


def gather_rest(line, count, index, *others):
    width = line.shape[1]
    held = line.reshape(4, -1, width)
    for step in reversed(middle_strides(count)):
        other = lax.ppermute(held, "shard", swap_pairs(count, step))
        if others:
            other = after(other, *others)
        held = both((index // step) % 2 == 0, held, other, axis=1).reshape(4, -1, width)
    return held.reshape(-1, width), other


def scatter_rest(values, count, index):
    width = values.shape[1]
    held = values.reshape(4, -1, width)
    strides = middle_strides(count)
    parts = []
    for step in strides:
        if parts:
            held = add_low(*parts)
        at = (index // step) % 2
        halves = held.reshape(4, 2, -1, width)
        other = lax.ppermute(pick(halves, 1 - at, 1), "shard", swap_pairs(count, step))
        parts = [pick(halves, at, 1), other]

    def finish(*others):
        return add_low(parts[0], after(parts[1], *others)).reshape(-1, width)

    return finish


def scatter_line(values, count):
    return lax.psum_scatter(
        values, "shard", scatter_dimension=0, tiled=True, axis_index_groups=line_groups(count)
    )


def sum_all(values, count, reps):
    total = values
    for step in middle_strides(count):
        total = total + lax.ppermute(total, "shard", swap_pairs(count, step))
    near = total
    for step in (count // 2, count // 4, 1):
        total = total + lax.ppermute(total, "shard", swap_pairs(count, step))
    step = 1
    while step < reps:
        total = total + lax.ppermute(total, "rep", [(r, r ^ step) for r in range(reps)])
        step *= 2
    return near, total[0]


def local(
    tokens,
    prompt_ids,
    seq_offsets,
    attn_gain,
    w_query,
    w_key,
    w_value,
    w_outgate,
    w_forget,
    forget_bias,
    w_output,
    ffn_gain,
    w_gate,
    w_up,
    w_down,
    cotangent,
    *,
    reps,
    count,
):
    own_rows = tokens.shape[0]
    model_width = tokens.shape[1]
    head_count = w_forget.shape[1]
    head_dim = model_width // head_count
    score_scale = head_dim ** (-0.5)
    team = 4
    core = lax.axis_index("rep") % 2
    index = lax.axis_index("shard")
    side = index % 2
    rank = 2 * side + core
    quarter = model_width // team
    heads = head_count // team
    shard_rows = w_query.shape[0]
    shard_ff = w_down.shape[0]
    unit = shard_ff // 2
    quarter_ff = w_gate.shape[1] // team
    core_pairs = [(r, r ^ 1) for r in range(reps)]
    side_pairs = [(s, s ^ 1) for s in range(count)]

    def swap_core(values):
        return lax.ppermute(values, "rep", core_pairs)

    def swap_side(values):
        return lax.ppermute(values, "shard", side_pairs)

    def team_rows(values, *others):
        pair = jnp.concatenate([values, swap_side(values)], axis=0)
        if others:
            pair = after(pair, *others)
        return jnp.concatenate([pair, swap_core(pair)], axis=0)

    def core_sum(partial):
        half = 2 * own_rows
        return partial[:half] + swap_core(partial[half:].astype(jnp.bfloat16)).astype(jnp.float32)

    def side_sum(pair):
        return pair[:own_rows] + swap_side(pair[own_rows:].astype(jnp.bfloat16)).astype(jnp.float32)

    def team_sum(partial):
        return side_sum(core_sum(partial))

    def cols_of(values, who):
        return lax.dynamic_slice_in_dim(values, who * quarter, quarter, axis=1)

    def units_of(values, which_side):
        cut = values.reshape(values.shape[0], count // 2, 2, 2, unit)
        return pick(pick(cut, core, 3), which_side, 2).reshape(values.shape[0], quarter_ff)

    def pair_rows(mine, sent):
        return both(side == 0, mine, swap_side(sent)).reshape(-1, mine.shape[1])

    small = jnp.concatenate(
        [
            w_forget,
            attn_gain[:, None],
            ffn_gain[:, None],
            jnp.zeros((shard_rows, 128 - head_count - 2), jnp.bfloat16),
        ],
        axis=1,
    )
    far_rank = rank ^ 2

    def columns(who, *weights):
        return [cols_of(w, who) for w in weights]

    first_block = pair_rows(
        jnp.concatenate(columns(rank, w_query, w_key, w_value) + [small], axis=1),
        jnp.concatenate(columns(far_rank, w_query, w_key, w_value) + [small], axis=1),
    )
    rest_block = pair_rows(
        jnp.concatenate(
            columns(rank, w_outgate, w_output) + [units_of(w_gate, side), units_of(w_up, side)],
            axis=1,
        ),
        after(
            jnp.concatenate(
                columns(far_rank, w_outgate, w_output)
                + [units_of(w_gate, 1 - side), units_of(w_up, 1 - side)],
                axis=1,
            ),
            first_block,
        ),
    )
    first_line = gather_line(first_block, count)
    second_line = gather_line(after(rest_block[:, : 2 * quarter], first_line), count)
    gate_line = gather_line(
        after(rest_block[:, 2 * quarter : 2 * quarter + quarter_ff], second_line), count
    )
    up_line = gather_line(after(rest_block[:, 2 * quarter + quarter_ff :], gate_line), count)
    down_line = gather_line(
        after(lax.dynamic_slice_in_dim(w_down, core * unit, unit, axis=0), up_line), count
    )
    first, _ = gather_rest(first_line, count, index)
    gate_w, gate_last = gather_rest(gate_line, count, index)
    up_w, up_last = gather_rest(up_line, count, index)
    down_w, _ = gather_rest(down_line, count, index)

    forget_w = lax.dynamic_slice_in_dim(
        first[:, 3 * quarter : 3 * quarter + head_count], rank * heads, heads, axis=1
    )
    gain_one = first[:, 3 * quarter + head_count].astype(jnp.float32)
    gain_two = first[:, 3 * quarter + head_count + 1].astype(jnp.float32)
    def replicas(values):
        total = values
        step = 2
        while step < reps:
            other = lax.ppermute(total, "rep", [(r, r ^ step) for r in range(reps)])
            total = add_low(total, other)
            step *= 2
        return total

    def own_of(values):
        pair = replicas(values).reshape(2, shard_rows, values.shape[1])
        sides = both(side == 0, pick(pair, side, 0), swap_side(pick(pair, 1 - side, 0)))
        return both(core == 0, sides, swap_core(sides))

    def both_cores(values):
        mine = replicas(values)
        return both(core == 0, mine, swap_core(mine))

    def turn_rows(values):
        cut = values.reshape(2, 2, quarter, quarter)
        mine = pick(cut, side, 0)
        pair = both(side == 0, mine, swap_side(pick(cut, 1 - side, 0)))
        kept = pick(pair, core, 1)
        quad = both(core == 0, kept, swap_core(pick(pair, 1 - core, 1)))
        return jnp.transpose(quad, (2, 1, 0, 3)).reshape(quarter, model_width)

    def turn_cols(values):
        cut = values.reshape(quarter, 2, 2, quarter)
        mine = pick(cut, core, 2)
        pair = both(core == 0, mine, swap_core(pick(cut, 1 - core, 2)))
        kept = pick(pair, side, 2)
        quad = both(side == 0, kept, swap_side(pick(pair, 1 - side, 2)))
        return quad.reshape(model_width, quarter)

    tokens_all = team_rows(after(tokens, rest_block), first_line)
    cotangent_all = team_rows(after(cotangent, tokens_all))
    facts_all = team_rows(jnp.concatenate([prompt_ids[0], seq_offsets[0]])[None, :])
    chain_ok = jnp.stack([chain_mask(facts_all[b, :NC], facts_all[b, NC:]) for b in range(team)])
    chain_float = chain_ok.astype(jnp.float32)

    inputs_all = tokens_all.astype(jnp.float32)
    scaled_all, inverse_all = normalize(inputs_all)
    scaled1 = scaled_all[:own_rows]
    inverse1 = inverse_all[:own_rows]
    inputs = inputs_all[:own_rows]
    normed1 = after((scaled_all * gain_one).astype(jnp.bfloat16), second_line)
    row_count = normed1.shape[0]

    qkv_low = matmul(normed1, first[:, : 3 * quarter]).astype(jnp.bfloat16)
    second = gather_rest(second_line, count, index, qkv_low)[0]
    outgate_w = second[:, :quarter]
    output_w = turn_rows(second[:, quarter:])
    outgate_pre = matmul(normed1, outgate_w)
    bias_mine = lax.dynamic_slice_in_dim(
        forget_bias.astype(jnp.float32), rank * heads, heads, axis=0
    )
    forget_in = matmul(normed1, forget_w) + bias_mine[None, :]
    log_forget = jax.nn.log_sigmoid(forget_in).reshape(team, own_rows, heads)
    decay_sum = jnp.einsum(
        "bij,bjh->bhi", chain_float, log_forget, precision=lax.Precision.HIGHEST
    )

    decay_cols = jnp.transpose(decay_sum, (0, 2, 1))
    attended = attend(
        after(qkv_low, gate_line, cotangent_all),
        decay_cols,
        decay_sum,
        facts_all,
        heads,
        head_dim,
        team,
        own_rows,
    )
    gate_open = jax.nn.sigmoid(outgate_pre)
    gated_low = (after(attended, up_line, gate_last) * gate_open).astype(jnp.bfloat16)

    residual = inputs + after(team_sum(matmul(gated_low, output_w)), up_last)
    scaled2, inverse2 = normalize(residual)
    normed2 = after(team_rows((scaled2 * gain_two).astype(jnp.bfloat16)), down_line)
    gate_pre = matmul(normed2, gate_w)
    up_pre = matmul(normed2, up_w)
    sig_gate = jax.nn.sigmoid(gate_pre)
    silu_gate = gate_pre * sig_gate
    act_low = (silu_gate * up_pre).astype(jnp.bfloat16)
    grad_act = matmul_nt(cotangent_all, down_w)
    grad_gate = (grad_act * up_pre * sig_gate * (1.0 + gate_pre * (1.0 - sig_gate))).astype(
        jnp.bfloat16
    )
    grad_up = (grad_act * silu_gate).astype(jnp.bfloat16)
    down_sum = scatter_rest(matmul_tn(act_low, cotangent_all).astype(jnp.bfloat16), count, index)
    pair_normed2 = core_sum(matmul_nt(grad_gate, gate_w) + matmul_nt(grad_up, up_w))
    normed2_late = after(normed2, pair_normed2)
    part_gate_w = matmul_tn(normed2_late, grad_gate).astype(jnp.bfloat16)
    grad_normed2 = after(side_sum(pair_normed2), part_gate_w)
    down_held = down_sum(grad_normed2)
    grad_down = scatter_line(down_held, count)
    gate_sum = scatter_rest(part_gate_w, count, index)
    grad_resid = cotangent.astype(jnp.float32) + norm_back(
        grad_normed2 * gain_two, scaled2, inverse2
    )
    grad_attn_own = grad_resid.astype(jnp.bfloat16)
    normed2_last, act_late = lax.optimization_barrier((normed2_late, act_low, grad_attn_own))[:2]
    part_up_w = matmul_tn(normed2_last, grad_up).astype(jnp.bfloat16)
    up_sum = scatter_rest(part_up_w, count, index)
    part_out = matmul(after(act_late, down_held), down_w)
    gate_held = gate_sum(part_out, part_up_w)
    grad_gate_w = scatter_line(gate_held, count)
    grad_attn = after(team_rows(grad_attn_own, gate_held), grad_down)
    grad_gated = matmul_nt(grad_attn, output_w)
    grad_output_cols = turn_cols(matmul_tn(gated_low, grad_attn).astype(jnp.bfloat16))
    grad_attended = (grad_gated * gate_open).astype(jnp.bfloat16)
    grad_outgate = (grad_gated * attended * gate_open * (1.0 - gate_open)).astype(jnp.bfloat16)
    up_held = up_sum(grad_outgate)
    grad_outgate_w = matmul_tn(after(normed1, up_held), grad_outgate).astype(jnp.bfloat16)
    part_second_w = jnp.concatenate([grad_outgate_w, grad_output_cols], axis=1)
    second_sum = scatter_rest(part_second_w, count, index)
    grad_up_w = scatter_line(up_held, count)
    grad_qkv, grad_logit_rows, grad_logit_cols = attend_back(
        qkv_low,
        after(grad_attended, up_held, part_second_w),
        decay_cols,
        decay_sum,
        facts_all,
        heads,
        head_dim,
        team,
        own_rows,
    )
    second_held = second_sum(grad_qkv)
    grad_qkv = after(grad_qkv, grad_gate_w, second_held)
    sum_second = scatter_line(second_held, count)
    layer_out = (residual + team_sum(after(part_out, grad_qkv))).astype(jnp.bfloat16)
    grad_decay = jnp.transpose(grad_logit_rows, (0, 2, 1)) - grad_logit_cols
    grad_log_forget = jnp.einsum(
        "bij,bhi->bjh", chain_float, grad_decay, precision=lax.Precision.HIGHEST
    ).reshape(row_count, heads)
    grad_forget_in = grad_log_forget * jax.nn.sigmoid(-forget_in)
    bias_sum = lax.dynamic_update_slice_in_dim(
        jnp.zeros((head_count,), jnp.float32),
        jnp.sum(grad_forget_in, axis=0),
        rank * heads,
        axis=0,
    )
    bias_near, grad_bias = sum_all(bias_sum[None, :], count, reps)
    grad_forget_low = lax.dynamic_update_slice_in_dim(
        jnp.zeros((row_count, small.shape[1]), jnp.bfloat16),
        grad_forget_in.astype(jnp.bfloat16),
        rank * heads,
        axis=1,
    )
    grad_first = jnp.concatenate([grad_qkv, grad_forget_low], axis=1)
    part_first_w = matmul_tn(normed1, grad_first).astype(jnp.bfloat16)
    first_sum = scatter_rest(after(part_first_w, bias_near), count, index)
    part_normed1 = matmul_nt(after(grad_first, part_first_w), first) + matmul_nt(
        grad_outgate, outgate_w
    )
    down_own = both_cores(after(grad_down, part_first_w))
    first_held = first_sum(grad_bias, layer_out, down_own)
    grad_normed1 = team_sum(after(part_normed1, first_held))
    tokens_grad = grad_resid + norm_back(grad_normed1 * gain_one, scaled1, inverse1)
    sum_first = scatter_line(first_held, count)
    gate_own = own_of(after(grad_gate_w, grad_normed1))
    grad_up_w = after(grad_up_w, grad_normed1)
    sum_second = after(sum_second, grad_normed1)

    def whole_cols(own):
        parts = own.shape[3] // quarter
        quad = jnp.transpose(own.astype(jnp.float32), (1, 0, 2, 3))
        quad = quad.reshape(2, 2, shard_rows, parts, quarter)
        quad = jnp.transpose(quad, (3, 2, 0, 1, 4)).reshape(parts, shard_rows, model_width)
        return [quad[p] for p in range(parts)]

    def whole_units(own):
        quad = jnp.transpose(own.astype(jnp.float32), (1, 0, 2, 3))
        quad = quad.reshape(2, 2, shard_rows, count // 2, unit)
        return jnp.transpose(quad, (2, 3, 0, 1, 4)).reshape(shard_rows, team * quarter_ff)

    first_own = own_of(sum_first)
    query_g, key_g, value_g = whole_cols(first_own[..., : 3 * quarter])
    forget_own = first_own[..., 3 * quarter : 3 * quarter + head_count]
    forget_g = jnp.sum(forget_own.astype(jnp.float32), axis=(0, 1))
    outgate_g, output_g = whole_cols(own_of(sum_second))
    gate_g = whole_units(gate_own)
    up_g = whole_units(own_of(grad_up_w))

    def gain_grad(gain, *pairs):
        total = sum(jnp.sum(w.astype(jnp.float32) * grad, axis=1) for w, grad in pairs)
        return total / gain.astype(jnp.float32)

    gain_one_g = gain_grad(
        attn_gain,
        (w_query, query_g),
        (w_key, key_g),
        (w_value, value_g),
        (w_outgate, outgate_g),
        (w_forget, forget_g),
    )
    gain_two_g = gain_grad(ffn_gain, (w_gate, gate_g), (w_up, up_g))
    return (
        layer_out,
        tokens_grad,
        gain_one_g,
        query_g,
        key_g,
        value_g,
        outgate_g,
        forget_g,
        grad_bias,
        output_g,
        gain_two_g,
        gate_g,
        up_g,
        down_own.astype(jnp.float32).reshape(shard_ff, model_width),
    )


def solution(mesh):
    in_specs = (
        P(("rep", "shard"), None),
        P(("rep", "shard"), None),
        P(("rep", "shard"), None),
        P("shard"),
        P("shard", None),
        P("shard", None),
        P("shard", None),
        P("shard", None),
        P("shard", None),
        P(),
        P("shard", None),
        P("shard"),
        P("shard", None),
        P("shard", None),
        P("shard", None),
        P(("rep", "shard"), None),
    )
    out_specs = (
        P(("rep", "shard"), None),
        P(("rep", "shard"), None),
        P("shard"),
        P("shard", None),
        P("shard", None),
        P("shard", None),
        P("shard", None),
        P("shard", None),
        P(),
        P("shard", None),
        P("shard"),
        P("shard", None),
        P("shard", None),
        P("shard", None),
    )

    def program(*arrays):
        return local(*arrays, reps=mesh.shape["rep"], count=mesh.shape["shard"])

    return jax.shard_map(program, mesh=mesh, in_specs=in_specs, out_specs=out_specs, check_vma=False)
```

```python
import jax
import jax.numpy as jnp
from jax import lax
from jax.experimental import pallas as pl
from jax.experimental.pallas import tpu as pltpu
from jax.sharding import PartitionSpec as P

PLEN = 64
CLEN = 64
NP = 2
NC = 4


EPS = 1e-06
NEGATIVE = -1e30


def chain_mask(prompt_ids, offsets):
    positions = jnp.arange(NP * PLEN + NC * CLEN, dtype=jnp.int32)
    in_prompt = positions < NP * PLEN
    after_prompts = positions - NP * PLEN
    sequence = jnp.where(in_prompt, positions // PLEN, NP + after_prompts // CLEN)
    within = jnp.where(in_prompt, positions % PLEN, after_prompts % CLEN)
    cont_index = sequence - NP
    selector = (cont_index[:, None] == jnp.arange(NC, dtype=jnp.int32)[None, :]).astype(jnp.int32)
    owner_id = jnp.where(in_prompt, -1, jnp.sum(selector * prompt_ids[None, :], axis=1))
    reach_end = jnp.sum(selector * offsets[None, :], axis=1)
    same_seq = (sequence[:, None] == sequence[None, :]) & (within[None, :] <= within[:, None])
    from_prompt = (owner_id[:, None] == sequence[None, :]) & (within[None, :] < reach_end[:, None])
    return same_seq | from_prompt


def normalize(values):
    inverse = lax.rsqrt(jnp.mean(values * values, axis=1, keepdims=True) + EPS)
    return (values * inverse, inverse)


def norm_back(grad_scaled, scaled, inverse):
    return inverse * (grad_scaled - scaled * jnp.mean(grad_scaled * scaled, axis=1, keepdims=True))


PROMPTS = NP * PLEN


def dot_nn(left_side, right_side):
    return jnp.dot(left_side, right_side, preferred_element_type=jnp.float32)


def dot_nt(left_side, right_side):
    return lax.dot_general(
        left_side, right_side, (((1,), (1,)), ((), ())), preferred_element_type=jnp.float32
    )


def dot_tn(left_side, right_side):
    return lax.dot_general(
        left_side, right_side, (((0,), (0,)), ((), ())), preferred_element_type=jnp.float32
    )


def key_mask(facts, block, rows):
    row = lax.broadcasted_iota(jnp.int32, (PROMPTS, PROMPTS), 0)
    col = lax.broadcasted_iota(jnp.int32, (PROMPTS, PROMPTS), 1)
    parts = [(row // PLEN == col // PLEN) & (col <= row)]
    within = lax.broadcasted_iota(jnp.int32, (CLEN, PLEN + CLEN), 0)
    key = lax.broadcasted_iota(jnp.int32, (CLEN, PLEN + CLEN), 1)
    for c in range(NC):
        reach = facts[block, NC + c]
        parts.append(((key < PLEN) & (key < reach)) | ((key >= PLEN) & (key - PLEN <= within)))
    return parts


def probs_of(query, keys, decay_col, decay_row, facts, block, masks, scale):
    logits = []
    for part, mask in enumerate(masks):
        if part == 0:
            rows = slice(0, PROMPTS)
            row_decay = decay_row[:, :PROMPTS]
        else:
            start = PROMPTS + (part - 1) * CLEN
            rows = slice(start, start + CLEN)
            first = facts[block, part - 1] == 0
            prompt_decay = jnp.where(first, decay_row[:, :PLEN], decay_row[:, PLEN:PROMPTS])
            row_decay = jnp.concatenate([prompt_decay, decay_row[:, start : start + CLEN]], axis=1)
        product = dot_nt(query[rows], keys[part]) * scale
        logits.append(jnp.where(mask, product + decay_col[rows] - row_decay, NEGATIVE))
    logits = jnp.concatenate(logits, axis=0)
    shifted = jnp.exp(logits - jnp.max(logits, axis=1, keepdims=True))
    return shifted / jnp.sum(shifted, axis=1, keepdims=True)


def part_rows(part):
    if part == 0:
        return slice(0, PROMPTS)
    start = PROMPTS + (part - 1) * CLEN
    return slice(start, start + CLEN)


def part_keys(ref, lanes, facts, block):
    parts = [ref[:PROMPTS, lanes]]
    for c in range(NC):
        start = pl.multiple_of(facts[block, c] * PLEN, PLEN)
        own = part_rows(c + 1)
        parts.append(jnp.concatenate([ref[pl.ds(start, PLEN), lanes], ref[own, lanes]], axis=0))
    return parts


def attend(qkv, decay_cols, decay_rows, facts, heads, head_dim, team, rows):
    width = heads * head_dim
    scale = head_dim ** (-0.5)

    def body(facts_ref, qkv_ref, col_ref, row_ref, out_ref):
        block = pl.program_id(0)
        masks = key_mask(facts_ref, block, rows)
        for h in range(heads):
            lanes = slice(h * head_dim, (h + 1) * head_dim)
            key_lanes = slice(width + h * head_dim, width + (h + 1) * head_dim)
            value_lanes = slice(2 * width + h * head_dim, 2 * width + (h + 1) * head_dim)
            keys = part_keys(qkv_ref, key_lanes, facts_ref, block)
            values = part_keys(qkv_ref, value_lanes, facts_ref, block)
            probs = probs_of(
                qkv_ref[:, lanes], keys, col_ref[0, :, h : h + 1], row_ref[0, h : h + 1, :],
                facts_ref, block, masks, scale,
            ).astype(jnp.bfloat16)
            for part in range(NC + 1):
                at = part_rows(part)
                out_ref[at, lanes] = dot_nn(probs[at], values[part])

    return pl.pallas_call(
        body,
        grid_spec=pltpu.PrefetchScalarGridSpec(
            num_scalar_prefetch=1,
            grid=(team,),
            in_specs=[
                pl.BlockSpec((rows, qkv.shape[1]), lambda b, f: (b, 0)),
                pl.BlockSpec((1, rows, heads), lambda b, f: (b, 0, 0)),
                pl.BlockSpec((1, heads, rows), lambda b, f: (b, 0, 0)),
            ],
            out_specs=pl.BlockSpec((rows, width), lambda b, f: (b, 0)),
        ),
        out_shape=jax.ShapeDtypeStruct((team * rows, width), jnp.float32),
        cost_estimate=pl.CostEstimate(
            flops=8 * team * rows * rows * width,
            bytes_accessed=8 * team * rows * width * 2,
            transcendentals=team * rows * PROMPTS * heads,
        ),
        name="attend",
    )(facts, qkv, decay_cols, decay_rows)


def attend_back(qkv, grad_attended, decay_cols, decay_rows, facts, heads, head_dim, team, rows):
    width = heads * head_dim
    scale = head_dim ** (-0.5)

    def body(facts_ref, qkv_ref, grad_ref, col_ref, row_ref, out_ref, sum_ref, low_ref, key_acc, value_acc):
        block = pl.program_id(0)
        masks = key_mask(facts_ref, block, rows)
        for h in range(heads):
            lanes = slice(h * head_dim, (h + 1) * head_dim)
            key_lanes = slice(width + h * head_dim, width + (h + 1) * head_dim)
            value_lanes = slice(2 * width + h * head_dim, 2 * width + (h + 1) * head_dim)
            keys = part_keys(qkv_ref, key_lanes, facts_ref, block)
            values = part_keys(qkv_ref, value_lanes, facts_ref, block)
            query = qkv_ref[:, lanes]
            grad = grad_ref[:, lanes]
            probs = probs_of(
                query, keys, col_ref[0, :, h : h + 1], row_ref[0, h : h + 1, :],
                facts_ref, block, masks, scale,
            )
            grad_probs = jnp.concatenate(
                [dot_nt(grad[part_rows(p)], values[p]) for p in range(NC + 1)], axis=0
            )
            mean = jnp.sum(probs * grad_probs, axis=1, keepdims=True)
            grad_logits = probs * (grad_probs - mean)
            sum_ref[0, :, h : h + 1] = jnp.sum(grad_logits, axis=1, keepdims=True)
            probs_low = probs.astype(jnp.bfloat16)
            grad_qk = (grad_logits * scale).astype(jnp.bfloat16)
            prompt_sum = jnp.sum(grad_logits[:PROMPTS], axis=0, keepdims=True)
            for part in range(NC + 1):
                at = part_rows(part)
                out_ref[at, lanes] = dot_nn(grad_qk[at], keys[part]).astype(jnp.bfloat16)
                grad_keys = dot_tn(grad_qk[at], query[at])
                grad_values = dot_tn(probs_low[at], grad[at])
                if part == 0:
                    key_acc[...] = grad_keys
                    value_acc[...] = grad_values
                    continue
                start = pl.multiple_of(facts_ref[block, part - 1] * PLEN, PLEN)
                key_acc[pl.ds(start, PLEN), :] += grad_keys[:PLEN]
                value_acc[pl.ds(start, PLEN), :] += grad_values[:PLEN]
                out_ref[at, key_lanes] = grad_keys[PLEN:].astype(jnp.bfloat16)
                out_ref[at, value_lanes] = grad_values[PLEN:].astype(jnp.bfloat16)
                column = jnp.sum(grad_logits[at], axis=0, keepdims=True)
                first = facts_ref[block, part - 1] == 0
                nothing = jnp.zeros((1, PLEN), jnp.float32)
                prompt_sum += jnp.concatenate(
                    [
                        jnp.where(first, column[:, :PLEN], nothing),
                        jnp.where(first, nothing, column[:, :PLEN]),
                    ],
                    axis=1,
                )
                low_ref[0, h : h + 1, at] = column[:, PLEN:]
            low_ref[0, h : h + 1, :PROMPTS] = prompt_sum
            out_ref[:PROMPTS, key_lanes] = key_acc[...].astype(jnp.bfloat16)
            out_ref[:PROMPTS, value_lanes] = value_acc[...].astype(jnp.bfloat16)

    return pl.pallas_call(
        body,
        grid_spec=pltpu.PrefetchScalarGridSpec(
            num_scalar_prefetch=1,
            grid=(team,),
            in_specs=[
                pl.BlockSpec((rows, qkv.shape[1]), lambda b, f: (b, 0)),
                pl.BlockSpec((rows, width), lambda b, f: (b, 0)),
                pl.BlockSpec((1, rows, heads), lambda b, f: (b, 0, 0)),
                pl.BlockSpec((1, heads, rows), lambda b, f: (b, 0, 0)),
            ],
            out_specs=[
                pl.BlockSpec((rows, 3 * width), lambda b, f: (b, 0)),
                pl.BlockSpec((1, rows, heads), lambda b, f: (b, 0, 0)),
                pl.BlockSpec((1, heads, rows), lambda b, f: (b, 0, 0)),
            ],
            scratch_shapes=[
                pltpu.VMEM((PROMPTS, head_dim), jnp.float32),
                pltpu.VMEM((PROMPTS, head_dim), jnp.float32),
            ],
        ),
        out_shape=[
            jax.ShapeDtypeStruct((team * rows, 3 * width), jnp.bfloat16),
            jax.ShapeDtypeStruct((team, rows, heads), jnp.float32),
            jax.ShapeDtypeStruct((team, heads, rows), jnp.float32),
        ],
        cost_estimate=pl.CostEstimate(
            flops=80 * team * rows * rows * width,
            bytes_accessed=7 * team * rows * width * 2,
            transcendentals=team * rows * PROMPTS * heads,
        ),
        name="attend_back",
    )(facts, qkv, grad_attended, decay_cols, decay_rows)


def matmul(left_side, right_side):
    return jnp.dot(left_side, right_side, preferred_element_type=jnp.float32)


def matmul_tn(left_side, right_side):
    return lax.dot_general(
        left_side, right_side, (((0,), (0,)), ((), ())), preferred_element_type=jnp.float32
    )


def matmul_nt(left_side, right_side):
    return lax.dot_general(
        left_side, right_side, (((1,), (1,)), ((), ())), preferred_element_type=jnp.float32
    )


def line_groups(count):
    step = count // 4
    return [[first + step * k for k in range(4)] for first in range(step)]


def middle_strides(count):
    strides = []
    step = count // 8
    while step > 1:
        strides.append(step)
        step //= 2
    return strides


def swap_pairs(count, step):
    return [(s, s ^ step) for s in range(count)]


def both(low_first, mine, other, axis=0):
    return jnp.stack(
        [jnp.where(low_first, mine, other), jnp.where(low_first, other, mine)], axis=axis
    )


def pick(values, at, axis):
    return lax.dynamic_index_in_dim(values, at, axis, keepdims=False)


def add_low(left_side, right_side):
    return (left_side.astype(jnp.float32) + right_side.astype(jnp.float32)).astype(jnp.bfloat16)


def after(values, *others):
    return lax.optimization_barrier((values,) + others)[0]


def gather_line(block, count):
    return lax.all_gather(block, "shard", axis=0, tiled=True, axis_index_groups=line_groups(count))


def gather_rest(line, count, index, *others):
    width = line.shape[1]
    held = line.reshape(4, -1, width)
    for step in reversed(middle_strides(count)):
        other = lax.ppermute(held, "shard", swap_pairs(count, step))
        if others:
            other = after(other, *others)
        held = both((index // step) % 2 == 0, held, other, axis=1).reshape(4, -1, width)
    return held.reshape(-1, width), other


def scatter_rest(values, count, index):
    width = values.shape[1]
    held = values.reshape(4, -1, width)
    strides = middle_strides(count)
    parts = []
    for step in strides:
        if parts:
            held = add_low(*parts)
        at = (index // step) % 2
        halves = held.reshape(4, 2, -1, width)
        other = lax.ppermute(pick(halves, 1 - at, 1), "shard", swap_pairs(count, step))
        parts = [pick(halves, at, 1), other]

    def finish(*others):
        return add_low(parts[0], after(parts[1], *others)).reshape(-1, width)

    return finish


def scatter_line(values, count):
    return lax.psum_scatter(
        values, "shard", scatter_dimension=0, tiled=True, axis_index_groups=line_groups(count)
    )


def sum_near(values, count):
    total = values
    for step in middle_strides(count):
        total = total + lax.ppermute(total, "shard", swap_pairs(count, step))
    return total


def sum_far(near, count, reps):
    total = near
    for step in (count // 2, count // 4, 1):
        total = total + lax.ppermute(total, "shard", swap_pairs(count, step))
    step = 1
    while step < reps:
        total = total + lax.ppermute(total, "rep", [(r, r ^ step) for r in range(reps)])
        step *= 2
    return total[0]


def local(
    tokens,
    prompt_ids,
    seq_offsets,
    attn_gain,
    w_query,
    w_key,
    w_value,
    w_outgate,
    w_forget,
    forget_bias,
    w_output,
    ffn_gain,
    w_gate,
    w_up,
    w_down,
    cotangent,
    *,
    reps,
    count,
):
    own_rows = tokens.shape[0]
    model_width = tokens.shape[1]
    head_count = w_forget.shape[1]
    head_dim = model_width // head_count
    score_scale = head_dim ** (-0.5)
    team = 4
    core = lax.axis_index("rep") % 2
    index = lax.axis_index("shard")
    side = index % 2
    rank = 2 * side + core
    quarter = model_width // team
    heads = head_count // team
    shard_rows = w_query.shape[0]
    shard_ff = w_down.shape[0]
    unit = shard_ff // 2
    quarter_ff = w_gate.shape[1] // team
    core_pairs = [(r, r ^ 1) for r in range(reps)]
    side_pairs = [(s, s ^ 1) for s in range(count)]

    def swap_core(values):
        return lax.ppermute(values, "rep", core_pairs)

    def swap_side(values):
        return lax.ppermute(values, "shard", side_pairs)

    def team_rows(values, *others):
        pair = jnp.concatenate([values, swap_side(values)], axis=0)
        if others:
            pair = after(pair, *others)
        return jnp.concatenate([pair, swap_core(pair)], axis=0)

    def core_sum(partial):
        half = 2 * own_rows
        return partial[:half] + swap_core(partial[half:].astype(jnp.bfloat16)).astype(jnp.float32)

    def side_sum(pair):
        return pair[:own_rows] + swap_side(pair[own_rows:].astype(jnp.bfloat16)).astype(jnp.float32)

    def team_sum(partial):
        return side_sum(core_sum(partial))

    def cols_of(values, who):
        return lax.dynamic_slice_in_dim(values, who * quarter, quarter, axis=1)

    def units_of(values, which_side):
        cut = values.reshape(values.shape[0], count // 2, 2, 2, unit)
        return pick(pick(cut, core, 3), which_side, 2).reshape(values.shape[0], quarter_ff)

    def pair_rows(mine, sent):
        return both(side == 0, mine, swap_side(sent)).reshape(-1, mine.shape[1])

    small = jnp.concatenate(
        [
            w_forget,
            attn_gain[:, None],
            ffn_gain[:, None],
            jnp.zeros((shard_rows, 128 - head_count - 2), jnp.bfloat16),
        ],
        axis=1,
    )
    far_rank = rank ^ 2

    def columns(who, *weights):
        return [cols_of(w, who) for w in weights]

    first_block = pair_rows(
        jnp.concatenate(columns(rank, w_query, w_key, w_value) + [small], axis=1),
        jnp.concatenate(columns(far_rank, w_query, w_key, w_value) + [small], axis=1),
    )
    rest_block = pair_rows(
        jnp.concatenate(
            columns(rank, w_outgate, w_output) + [units_of(w_gate, side), units_of(w_up, side)],
            axis=1,
        ),
        after(
            jnp.concatenate(
                columns(far_rank, w_outgate, w_output)
                + [units_of(w_gate, 1 - side), units_of(w_up, 1 - side)],
                axis=1,
            ),
            first_block,
        ),
    )
    first_line = gather_line(first_block, count)
    second_line = gather_line(after(rest_block[:, : 2 * quarter], first_line), count)
    gate_line = gather_line(
        after(rest_block[:, 2 * quarter : 2 * quarter + quarter_ff], second_line), count
    )
    up_line = gather_line(after(rest_block[:, 2 * quarter + quarter_ff :], gate_line), count)
    down_line = gather_line(
        after(lax.dynamic_slice_in_dim(w_down, core * unit, unit, axis=0), up_line), count
    )
    first, _ = gather_rest(first_line, count, index)
    gate_w, gate_last = gather_rest(gate_line, count, index)
    up_w, up_last = gather_rest(up_line, count, index)
    down_w, _ = gather_rest(down_line, count, index)

    forget_w = lax.dynamic_slice_in_dim(
        first[:, 3 * quarter : 3 * quarter + head_count], rank * heads, heads, axis=1
    )
    gain_one = first[:, 3 * quarter + head_count].astype(jnp.float32)
    gain_two = first[:, 3 * quarter + head_count + 1].astype(jnp.float32)
    def replicas(values):
        total = values
        step = 2
        while step < reps:
            other = lax.ppermute(total, "rep", [(r, r ^ step) for r in range(reps)])
            total = add_low(total, other)
            step *= 2
        return total

    def own_of(values):
        pair = replicas(values).reshape(2, shard_rows, values.shape[1])
        sides = both(side == 0, pick(pair, side, 0), swap_side(pick(pair, 1 - side, 0)))
        return both(core == 0, sides, swap_core(sides))

    def both_cores(values):
        mine = replicas(values)
        return both(core == 0, mine, swap_core(mine))

    def turn_rows(values):
        cut = values.reshape(2, 2, quarter, quarter)
        mine = pick(cut, side, 0)
        pair = both(side == 0, mine, swap_side(pick(cut, 1 - side, 0)))
        kept = pick(pair, core, 1)
        quad = both(core == 0, kept, swap_core(pick(pair, 1 - core, 1)))
        return jnp.transpose(quad, (2, 1, 0, 3)).reshape(quarter, model_width)

    def turn_cols(values):
        cut = values.reshape(quarter, 2, 2, quarter)
        mine = pick(cut, core, 2)
        pair = both(core == 0, mine, swap_core(pick(cut, 1 - core, 2)))
        kept = pick(pair, side, 2)
        quad = both(side == 0, kept, swap_side(pick(pair, 1 - side, 2)))
        return quad.reshape(model_width, quarter)

    tokens_all = team_rows(after(tokens, rest_block), first_line)
    facts_all = team_rows(jnp.concatenate([prompt_ids[0], seq_offsets[0]])[None, :])
    chain_ok = jnp.stack([chain_mask(facts_all[b, :NC], facts_all[b, NC:]) for b in range(team)])
    chain_float = chain_ok.astype(jnp.float32)

    inputs_all = tokens_all.astype(jnp.float32)
    scaled_all, inverse_all = normalize(inputs_all)
    scaled1 = scaled_all[:own_rows]
    inverse1 = inverse_all[:own_rows]
    inputs = inputs_all[:own_rows]
    normed1 = after((scaled_all * gain_one).astype(jnp.bfloat16), gate_line)
    row_count = normed1.shape[0]

    qkv_low = matmul(normed1, first[:, : 3 * quarter]).astype(jnp.bfloat16)
    cotangent_all = team_rows(after(cotangent, first_line), qkv_low)
    second = gather_rest(second_line, count, index, qkv_low)[0]
    outgate_w = second[:, :quarter]
    output_w = turn_rows(second[:, quarter:])
    outgate_pre = matmul(normed1, outgate_w)
    bias_mine = lax.dynamic_slice_in_dim(
        forget_bias.astype(jnp.float32), rank * heads, heads, axis=0
    )
    forget_in = matmul(normed1, forget_w) + bias_mine[None, :]
    log_forget = jax.nn.log_sigmoid(forget_in).reshape(team, own_rows, heads)
    decay_sum = jnp.einsum(
        "bij,bjh->bhi", chain_float, log_forget, precision=lax.Precision.HIGHEST
    )

    decay_cols = jnp.transpose(decay_sum, (0, 2, 1))
    attended = attend(
        qkv_low,
        decay_cols,
        decay_sum,
        facts_all,
        heads,
        head_dim,
        team,
        own_rows,
    )
    gate_open = jax.nn.sigmoid(outgate_pre)
    gated_low = (after(attended, up_line, gate_last, cotangent_all) * gate_open).astype(jnp.bfloat16)

    residual = inputs + after(team_sum(matmul(gated_low, output_w)), up_last)
    scaled2, inverse2 = normalize(residual)
    normed2 = after(team_rows((scaled2 * gain_two).astype(jnp.bfloat16)), down_line)
    gate_pre = matmul(normed2, gate_w)
    up_pre = matmul(normed2, up_w)
    sig_gate = jax.nn.sigmoid(gate_pre)
    silu_gate = gate_pre * sig_gate
    act_low = (silu_gate * up_pre).astype(jnp.bfloat16)
    grad_act = matmul_nt(cotangent_all, down_w)
    grad_gate = (grad_act * up_pre * sig_gate * (1.0 + gate_pre * (1.0 - sig_gate))).astype(
        jnp.bfloat16
    )
    grad_up = (grad_act * silu_gate).astype(jnp.bfloat16)
    down_sum = scatter_rest(matmul_tn(act_low, cotangent_all).astype(jnp.bfloat16), count, index)
    pair_normed2 = core_sum(matmul_nt(grad_gate, gate_w) + matmul_nt(grad_up, up_w))
    normed2_late = after(normed2, pair_normed2)
    part_gate_w = matmul_tn(normed2_late, grad_gate).astype(jnp.bfloat16)
    grad_normed2 = after(side_sum(pair_normed2), part_gate_w)
    down_held = down_sum(grad_normed2)
    grad_down = scatter_line(down_held, count)
    gate_sum = scatter_rest(part_gate_w, count, index)
    grad_resid = cotangent.astype(jnp.float32) + norm_back(
        grad_normed2 * gain_two, scaled2, inverse2
    )
    grad_attn_own = grad_resid.astype(jnp.bfloat16)
    normed2_last, act_late = lax.optimization_barrier((normed2_late, act_low, grad_attn_own))[:2]
    part_up_w = matmul_tn(normed2_last, grad_up).astype(jnp.bfloat16)
    up_sum = scatter_rest(part_up_w, count, index)
    part_out = matmul(after(act_late, down_held), down_w)
    gate_held = gate_sum(part_out, part_up_w)
    grad_gate_w = scatter_line(gate_held, count)
    grad_attn = after(team_rows(grad_attn_own, gate_held), grad_down)
    grad_gated = matmul_nt(grad_attn, output_w)
    grad_output_cols = turn_cols(matmul_tn(gated_low, grad_attn).astype(jnp.bfloat16))
    grad_attended = (grad_gated * gate_open).astype(jnp.bfloat16)
    grad_outgate = (grad_gated * attended * gate_open * (1.0 - gate_open)).astype(jnp.bfloat16)
    up_held = up_sum(grad_outgate)
    grad_outgate_w = matmul_tn(after(normed1, up_held), grad_outgate).astype(jnp.bfloat16)
    part_second_w = jnp.concatenate([grad_outgate_w, grad_output_cols], axis=1)
    second_sum = scatter_rest(part_second_w, count, index)
    grad_up_w = scatter_line(up_held, count)
    grad_qkv, grad_logit_rows, grad_logit_cols = attend_back(
        qkv_low,
        after(grad_attended, up_held, part_second_w),
        decay_cols,
        decay_sum,
        facts_all,
        heads,
        head_dim,
        team,
        own_rows,
    )
    second_held = second_sum(grad_qkv)
    grad_qkv = after(grad_qkv, grad_gate_w, second_held, grad_up_w)
    sum_second = scatter_line(second_held, count)
    layer_out = (residual + team_sum(after(part_out, grad_qkv))).astype(jnp.bfloat16)
    grad_decay = jnp.transpose(grad_logit_rows, (0, 2, 1)) - grad_logit_cols
    grad_log_forget = jnp.einsum(
        "bij,bhi->bjh", chain_float, grad_decay, precision=lax.Precision.HIGHEST
    ).reshape(row_count, heads)
    grad_forget_in = grad_log_forget * jax.nn.sigmoid(-forget_in)
    bias_sum = lax.dynamic_update_slice_in_dim(
        jnp.zeros((head_count,), jnp.float32),
        jnp.sum(grad_forget_in, axis=0),
        rank * heads,
        axis=0,
    )
    bias_near = sum_near(bias_sum[None, :], count)
    grad_forget_low = lax.dynamic_update_slice_in_dim(
        jnp.zeros((row_count, small.shape[1]), jnp.bfloat16),
        grad_forget_in.astype(jnp.bfloat16),
        rank * heads,
        axis=1,
    )
    grad_first = jnp.concatenate([grad_qkv, grad_forget_low], axis=1)
    part_first_w = matmul_tn(normed1, grad_first).astype(jnp.bfloat16)
    first_sum = scatter_rest(after(part_first_w, bias_near), count, index)
    part_normed1 = matmul_nt(after(grad_first, part_first_w), first) + matmul_nt(
        grad_outgate, outgate_w
    )
    down_own = both_cores(after(grad_down, part_first_w))
    grad_bias = sum_far(after(bias_near, part_first_w), count, reps)
    first_held = first_sum(grad_bias, layer_out, down_own, sum_second)
    grad_normed1 = team_sum(after(part_normed1, first_held))
    tokens_grad = grad_resid + norm_back(grad_normed1 * gain_one, scaled1, inverse1)
    sum_first = scatter_line(first_held, count)
    gate_own = own_of(after(grad_gate_w, grad_normed1))
    grad_up_w = after(grad_up_w, grad_normed1)
    sum_second = after(sum_second, grad_normed1)

    def whole_cols(own):
        parts = own.shape[3] // quarter
        quad = jnp.transpose(own.astype(jnp.float32), (1, 0, 2, 3))
        quad = quad.reshape(2, 2, shard_rows, parts, quarter)
        quad = jnp.transpose(quad, (3, 2, 0, 1, 4)).reshape(parts, shard_rows, model_width)
        return [quad[p] for p in range(parts)]

    def whole_units(own):
        quad = jnp.transpose(own.astype(jnp.float32), (1, 0, 2, 3))
        quad = quad.reshape(2, 2, shard_rows, count // 2, unit)
        return jnp.transpose(quad, (2, 3, 0, 1, 4)).reshape(shard_rows, team * quarter_ff)

    first_own = own_of(sum_first)
    query_g, key_g, value_g = whole_cols(first_own[..., : 3 * quarter])
    forget_own = first_own[..., 3 * quarter : 3 * quarter + head_count]
    forget_g = jnp.sum(forget_own.astype(jnp.float32), axis=(0, 1))
    outgate_g, output_g = whole_cols(own_of(sum_second))
    gate_g = whole_units(gate_own)
    up_g = whole_units(own_of(grad_up_w))

    def gain_grad(gain, *pairs):
        total = sum(jnp.sum(w.astype(jnp.float32) * grad, axis=1) for w, grad in pairs)
        return total / gain.astype(jnp.float32)

    gain_one_g = gain_grad(
        attn_gain,
        (w_query, query_g),
        (w_key, key_g),
        (w_value, value_g),
        (w_outgate, outgate_g),
        (w_forget, forget_g),
    )
    gain_two_g = gain_grad(ffn_gain, (w_gate, gate_g), (w_up, up_g))
    return (
        layer_out,
        tokens_grad,
        gain_one_g,
        query_g,
        key_g,
        value_g,
        outgate_g,
        forget_g,
        grad_bias,
        output_g,
        gain_two_g,
        gate_g,
        up_g,
        down_own.astype(jnp.float32).reshape(shard_ff, model_width),
    )


def solution(mesh):
    in_specs = (
        P(("rep", "shard"), None),
        P(("rep", "shard"), None),
        P(("rep", "shard"), None),
        P("shard"),
        P("shard", None),
        P("shard", None),
        P("shard", None),
        P("shard", None),
        P("shard", None),
        P(),
        P("shard", None),
        P("shard"),
        P("shard", None),
        P("shard", None),
        P("shard", None),
        P(("rep", "shard"), None),
    )
    out_specs = (
        P(("rep", "shard"), None),
        P(("rep", "shard"), None),
        P("shard"),
        P("shard", None),
        P("shard", None),
        P("shard", None),
        P("shard", None),
        P("shard", None),
        P(),
        P("shard", None),
        P("shard"),
        P("shard", None),
        P("shard", None),
        P("shard", None),
    )

    def program(*arrays):
        return local(*arrays, reps=mesh.shape["rep"], count=mesh.shape["shard"])

    return jax.shard_map(program, mesh=mesh, in_specs=in_specs, out_specs=out_specs, check_vma=False)
```

```python
import jax
import jax.numpy as jnp
from jax import lax
from jax.experimental import pallas as pl
from jax.experimental.pallas import tpu as pltpu
from jax.sharding import PartitionSpec as P

PLEN = 64
CLEN = 64
NP = 2
NC = 4


EPS = 1e-06
NEGATIVE = -1e30


def chain_mask(prompt_ids, offsets):
    positions = jnp.arange(NP * PLEN + NC * CLEN, dtype=jnp.int32)
    in_prompt = positions < NP * PLEN
    after_prompts = positions - NP * PLEN
    sequence = jnp.where(in_prompt, positions // PLEN, NP + after_prompts // CLEN)
    within = jnp.where(in_prompt, positions % PLEN, after_prompts % CLEN)
    cont_index = sequence - NP
    selector = (cont_index[:, None] == jnp.arange(NC, dtype=jnp.int32)[None, :]).astype(jnp.int32)
    owner_id = jnp.where(in_prompt, -1, jnp.sum(selector * prompt_ids[None, :], axis=1))
    reach_end = jnp.sum(selector * offsets[None, :], axis=1)
    same_seq = (sequence[:, None] == sequence[None, :]) & (within[None, :] <= within[:, None])
    from_prompt = (owner_id[:, None] == sequence[None, :]) & (within[None, :] < reach_end[:, None])
    return same_seq | from_prompt


def normalize(values):
    inverse = lax.rsqrt(jnp.mean(values * values, axis=1, keepdims=True) + EPS)
    return (values * inverse, inverse)


def norm_back(grad_scaled, scaled, inverse):
    return inverse * (grad_scaled - scaled * jnp.mean(grad_scaled * scaled, axis=1, keepdims=True))


PROMPTS = NP * PLEN


def dot_nn(left_side, right_side):
    return jnp.dot(left_side, right_side, preferred_element_type=jnp.float32)


def dot_nt(left_side, right_side):
    return lax.dot_general(
        left_side, right_side, (((1,), (1,)), ((), ())), preferred_element_type=jnp.float32
    )


def dot_tn(left_side, right_side):
    return lax.dot_general(
        left_side, right_side, (((0,), (0,)), ((), ())), preferred_element_type=jnp.float32
    )


def key_mask(facts, block, rows):
    row = lax.broadcasted_iota(jnp.int32, (PROMPTS, PROMPTS), 0)
    col = lax.broadcasted_iota(jnp.int32, (PROMPTS, PROMPTS), 1)
    parts = [(row // PLEN == col // PLEN) & (col <= row)]
    within = lax.broadcasted_iota(jnp.int32, (CLEN, PLEN + CLEN), 0)
    key = lax.broadcasted_iota(jnp.int32, (CLEN, PLEN + CLEN), 1)
    for c in range(NC):
        reach = facts[block, NC + c]
        parts.append(((key < PLEN) & (key < reach)) | ((key >= PLEN) & (key - PLEN <= within)))
    return parts


def probs_of(query, keys, decay_col, decay_row, facts, block, masks, scale):
    logits = []
    for part, mask in enumerate(masks):
        if part == 0:
            rows = slice(0, PROMPTS)
            row_decay = decay_row[:, :PROMPTS]
        else:
            start = PROMPTS + (part - 1) * CLEN
            rows = slice(start, start + CLEN)
            first = facts[block, part - 1] == 0
            prompt_decay = jnp.where(first, decay_row[:, :PLEN], decay_row[:, PLEN:PROMPTS])
            row_decay = jnp.concatenate([prompt_decay, decay_row[:, start : start + CLEN]], axis=1)
        product = dot_nt(query[rows], keys[part]) * scale
        logits.append(jnp.where(mask, product + decay_col[rows] - row_decay, NEGATIVE))
    logits = jnp.concatenate(logits, axis=0)
    shifted = jnp.exp(logits - jnp.max(logits, axis=1, keepdims=True))
    return shifted / jnp.sum(shifted, axis=1, keepdims=True)


def part_rows(part):
    if part == 0:
        return slice(0, PROMPTS)
    start = PROMPTS + (part - 1) * CLEN
    return slice(start, start + CLEN)


def part_keys(ref, lanes, facts, block):
    parts = [ref[:PROMPTS, lanes]]
    for c in range(NC):
        start = pl.multiple_of(facts[block, c] * PLEN, PLEN)
        own = part_rows(c + 1)
        parts.append(jnp.concatenate([ref[pl.ds(start, PLEN), lanes], ref[own, lanes]], axis=0))
    return parts


def attend(qkv, decay_cols, decay_rows, facts, heads, head_dim, team, rows):
    width = heads * head_dim
    scale = head_dim ** (-0.5)

    def body(facts_ref, qkv_ref, col_ref, row_ref, out_ref):
        block = pl.program_id(0)
        masks = key_mask(facts_ref, block, rows)
        for h in range(heads):
            lanes = slice(h * head_dim, (h + 1) * head_dim)
            key_lanes = slice(width + h * head_dim, width + (h + 1) * head_dim)
            value_lanes = slice(2 * width + h * head_dim, 2 * width + (h + 1) * head_dim)
            keys = part_keys(qkv_ref, key_lanes, facts_ref, block)
            values = part_keys(qkv_ref, value_lanes, facts_ref, block)
            probs = probs_of(
                qkv_ref[:, lanes], keys, col_ref[0, :, h : h + 1], row_ref[0, h : h + 1, :],
                facts_ref, block, masks, scale,
            ).astype(jnp.bfloat16)
            for part in range(NC + 1):
                at = part_rows(part)
                out_ref[at, lanes] = dot_nn(probs[at], values[part])

    return pl.pallas_call(
        body,
        grid_spec=pltpu.PrefetchScalarGridSpec(
            num_scalar_prefetch=1,
            grid=(team,),
            in_specs=[
                pl.BlockSpec((rows, qkv.shape[1]), lambda b, f: (b, 0)),
                pl.BlockSpec((1, rows, heads), lambda b, f: (b, 0, 0)),
                pl.BlockSpec((1, heads, rows), lambda b, f: (b, 0, 0)),
            ],
            out_specs=pl.BlockSpec((rows, width), lambda b, f: (b, 0)),
        ),
        out_shape=jax.ShapeDtypeStruct((team * rows, width), jnp.float32),
        cost_estimate=pl.CostEstimate(
            flops=8 * team * rows * rows * width,
            bytes_accessed=8 * team * rows * width * 2,
            transcendentals=team * rows * PROMPTS * heads,
        ),
        name="attend",
    )(facts, qkv, decay_cols, decay_rows)


def attend_back(qkv, grad_attended, decay_cols, decay_rows, facts, heads, head_dim, team, rows):
    width = heads * head_dim
    scale = head_dim ** (-0.5)

    def body(facts_ref, qkv_ref, grad_ref, col_ref, row_ref, out_ref, sum_ref, low_ref, key_acc, value_acc):
        block = pl.program_id(0)
        masks = key_mask(facts_ref, block, rows)
        for h in range(heads):
            lanes = slice(h * head_dim, (h + 1) * head_dim)
            key_lanes = slice(width + h * head_dim, width + (h + 1) * head_dim)
            value_lanes = slice(2 * width + h * head_dim, 2 * width + (h + 1) * head_dim)
            keys = part_keys(qkv_ref, key_lanes, facts_ref, block)
            values = part_keys(qkv_ref, value_lanes, facts_ref, block)
            query = qkv_ref[:, lanes]
            grad = grad_ref[:, lanes]
            probs = probs_of(
                query, keys, col_ref[0, :, h : h + 1], row_ref[0, h : h + 1, :],
                facts_ref, block, masks, scale,
            )
            grad_probs = jnp.concatenate(
                [dot_nt(grad[part_rows(p)], values[p]) for p in range(NC + 1)], axis=0
            )
            mean = jnp.sum(probs * grad_probs, axis=1, keepdims=True)
            grad_logits = probs * (grad_probs - mean)
            sum_ref[0, :, h : h + 1] = jnp.sum(grad_logits, axis=1, keepdims=True)
            probs_low = probs.astype(jnp.bfloat16)
            grad_qk = (grad_logits * scale).astype(jnp.bfloat16)
            prompt_sum = jnp.sum(grad_logits[:PROMPTS], axis=0, keepdims=True)
            for part in range(NC + 1):
                at = part_rows(part)
                out_ref[at, lanes] = dot_nn(grad_qk[at], keys[part]).astype(jnp.bfloat16)
                grad_keys = dot_tn(grad_qk[at], query[at])
                grad_values = dot_tn(probs_low[at], grad[at])
                if part == 0:
                    key_acc[...] = grad_keys
                    value_acc[...] = grad_values
                    continue
                start = pl.multiple_of(facts_ref[block, part - 1] * PLEN, PLEN)
                key_acc[pl.ds(start, PLEN), :] += grad_keys[:PLEN]
                value_acc[pl.ds(start, PLEN), :] += grad_values[:PLEN]
                out_ref[at, key_lanes] = grad_keys[PLEN:].astype(jnp.bfloat16)
                out_ref[at, value_lanes] = grad_values[PLEN:].astype(jnp.bfloat16)
                column = jnp.sum(grad_logits[at], axis=0, keepdims=True)
                first = facts_ref[block, part - 1] == 0
                nothing = jnp.zeros((1, PLEN), jnp.float32)
                prompt_sum += jnp.concatenate(
                    [
                        jnp.where(first, column[:, :PLEN], nothing),
                        jnp.where(first, nothing, column[:, :PLEN]),
                    ],
                    axis=1,
                )
                low_ref[0, h : h + 1, at] = column[:, PLEN:]
            low_ref[0, h : h + 1, :PROMPTS] = prompt_sum
            out_ref[:PROMPTS, key_lanes] = key_acc[...].astype(jnp.bfloat16)
            out_ref[:PROMPTS, value_lanes] = value_acc[...].astype(jnp.bfloat16)

    return pl.pallas_call(
        body,
        grid_spec=pltpu.PrefetchScalarGridSpec(
            num_scalar_prefetch=1,
            grid=(team,),
            in_specs=[
                pl.BlockSpec((rows, qkv.shape[1]), lambda b, f: (b, 0)),
                pl.BlockSpec((rows, width), lambda b, f: (b, 0)),
                pl.BlockSpec((1, rows, heads), lambda b, f: (b, 0, 0)),
                pl.BlockSpec((1, heads, rows), lambda b, f: (b, 0, 0)),
            ],
            out_specs=[
                pl.BlockSpec((rows, 3 * width), lambda b, f: (b, 0)),
                pl.BlockSpec((1, rows, heads), lambda b, f: (b, 0, 0)),
                pl.BlockSpec((1, heads, rows), lambda b, f: (b, 0, 0)),
            ],
            scratch_shapes=[
                pltpu.VMEM((PROMPTS, head_dim), jnp.float32),
                pltpu.VMEM((PROMPTS, head_dim), jnp.float32),
            ],
        ),
        out_shape=[
            jax.ShapeDtypeStruct((team * rows, 3 * width), jnp.bfloat16),
            jax.ShapeDtypeStruct((team, rows, heads), jnp.float32),
            jax.ShapeDtypeStruct((team, heads, rows), jnp.float32),
        ],
        cost_estimate=pl.CostEstimate(
            flops=80 * team * rows * rows * width,
            bytes_accessed=7 * team * rows * width * 2,
            transcendentals=team * rows * PROMPTS * heads,
        ),
        name="attend_back",
    )(facts, qkv, grad_attended, decay_cols, decay_rows)


def matmul(left_side, right_side):
    return jnp.dot(left_side, right_side, preferred_element_type=jnp.float32)


def matmul_tn(left_side, right_side):
    return lax.dot_general(
        left_side, right_side, (((0,), (0,)), ((), ())), preferred_element_type=jnp.float32
    )


def matmul_nt(left_side, right_side):
    return lax.dot_general(
        left_side, right_side, (((1,), (1,)), ((), ())), preferred_element_type=jnp.float32
    )


def line_groups(count):
    step = count // 4
    return [[first + step * k for k in range(4)] for first in range(step)]


def middle_strides(count):
    strides = []
    step = count // 8
    while step > 1:
        strides.append(step)
        step //= 2
    return strides


def swap_pairs(count, step):
    return [(s, s ^ step) for s in range(count)]


def both(low_first, mine, other, axis=0):
    return jnp.stack(
        [jnp.where(low_first, mine, other), jnp.where(low_first, other, mine)], axis=axis
    )


def pick(values, at, axis):
    return lax.dynamic_index_in_dim(values, at, axis, keepdims=False)


def add_low(left_side, right_side):
    return (left_side.astype(jnp.float32) + right_side.astype(jnp.float32)).astype(jnp.bfloat16)


def after(values, *others):
    return lax.optimization_barrier((values,) + others)[0]


def gather_line(block, count):
    return lax.all_gather(block, "shard", axis=0, tiled=True, axis_index_groups=line_groups(count))


def gather_rest(line, count, index, *others):
    width = line.shape[1]
    held = line.reshape(4, -1, width)
    for step in reversed(middle_strides(count)):
        other = lax.ppermute(held, "shard", swap_pairs(count, step))
        if others:
            other = after(other, *others)
        held = both((index // step) % 2 == 0, held, other, axis=1).reshape(4, -1, width)
    return held.reshape(-1, width), other


def scatter_rest(values, count, index):
    width = values.shape[1]
    held = values.reshape(4, -1, width)
    strides = middle_strides(count)
    parts = []
    for step in strides:
        if parts:
            held = add_low(*parts)
        at = (index // step) % 2
        halves = held.reshape(4, 2, -1, width)
        other = lax.ppermute(pick(halves, 1 - at, 1), "shard", swap_pairs(count, step))
        parts = [pick(halves, at, 1), other]

    def finish(*others):
        return add_low(parts[0], after(parts[1], *others)).reshape(-1, width)

    return finish


def scatter_line(values, count):
    return lax.psum_scatter(
        values, "shard", scatter_dimension=0, tiled=True, axis_index_groups=line_groups(count)
    )


def sum_near(values, count):
    total = values
    for step in middle_strides(count):
        total = total + lax.ppermute(total, "shard", swap_pairs(count, step))
    return total


def sum_far(near, count, reps):
    total = near
    for step in (count // 2, count // 4, 1):
        total = total + lax.ppermute(total, "shard", swap_pairs(count, step))
    step = 1
    while step < reps:
        total = total + lax.ppermute(total, "rep", [(r, r ^ step) for r in range(reps)])
        step *= 2
    return total[0]


def local(
    tokens,
    prompt_ids,
    seq_offsets,
    attn_gain,
    w_query,
    w_key,
    w_value,
    w_outgate,
    w_forget,
    forget_bias,
    w_output,
    ffn_gain,
    w_gate,
    w_up,
    w_down,
    cotangent,
    *,
    reps,
    count,
):
    own_rows = tokens.shape[0]
    model_width = tokens.shape[1]
    head_count = w_forget.shape[1]
    head_dim = model_width // head_count
    score_scale = head_dim ** (-0.5)
    team = 4
    core = lax.axis_index("rep") % 2
    index = lax.axis_index("shard")
    side = index % 2
    rank = 2 * side + core
    quarter = model_width // team
    heads = head_count // team
    shard_rows = w_query.shape[0]
    shard_ff = w_down.shape[0]
    unit = shard_ff // 2
    quarter_ff = w_gate.shape[1] // team
    core_pairs = [(r, r ^ 1) for r in range(reps)]
    side_pairs = [(s, s ^ 1) for s in range(count)]

    def swap_core(values):
        return lax.ppermute(values, "rep", core_pairs)

    def swap_side(values):
        return lax.ppermute(values, "shard", side_pairs)

    def team_rows(values, *others):
        pair = jnp.concatenate([values, swap_side(values)], axis=0)
        if others:
            pair = after(pair, *others)
        return jnp.concatenate([pair, swap_core(pair)], axis=0)

    def core_sum(partial):
        half = 2 * own_rows
        return partial[:half] + swap_core(partial[half:].astype(jnp.bfloat16)).astype(jnp.float32)

    def side_sum(pair):
        return pair[:own_rows] + swap_side(pair[own_rows:].astype(jnp.bfloat16)).astype(jnp.float32)

    def team_sum(partial):
        return side_sum(core_sum(partial))

    def cols_of(values, who):
        return lax.dynamic_slice_in_dim(values, who * quarter, quarter, axis=1)

    def units_of(values, which_side):
        cut = values.reshape(values.shape[0], count // 2, 2, 2, unit)
        return pick(pick(cut, core, 3), which_side, 2).reshape(values.shape[0], quarter_ff)

    def pair_rows(mine, sent):
        return both(side == 0, mine, swap_side(sent)).reshape(-1, mine.shape[1])

    small = jnp.concatenate(
        [
            w_forget,
            attn_gain[:, None],
            ffn_gain[:, None],
            jnp.zeros((shard_rows, 128 - head_count - 2), jnp.bfloat16),
        ],
        axis=1,
    )
    far_rank = rank ^ 2

    def columns(who, *weights):
        return [cols_of(w, who) for w in weights]

    first_block = pair_rows(
        jnp.concatenate(columns(rank, w_query, w_key, w_value) + [small], axis=1),
        jnp.concatenate(columns(far_rank, w_query, w_key, w_value) + [small], axis=1),
    )
    rest_block = pair_rows(
        jnp.concatenate(
            columns(rank, w_outgate, w_output) + [units_of(w_gate, side), units_of(w_up, side)],
            axis=1,
        ),
        after(
            jnp.concatenate(
                columns(far_rank, w_outgate, w_output)
                + [units_of(w_gate, 1 - side), units_of(w_up, 1 - side)],
                axis=1,
            ),
            first_block,
        ),
    )
    first_line = gather_line(first_block, count)
    second_line = gather_line(after(rest_block[:, : 2 * quarter], first_line), count)
    gate_line = gather_line(
        after(rest_block[:, 2 * quarter : 2 * quarter + quarter_ff], second_line), count
    )
    up_line = gather_line(after(rest_block[:, 2 * quarter + quarter_ff :], gate_line), count)
    down_line = gather_line(
        after(lax.dynamic_slice_in_dim(w_down, core * unit, unit, axis=0), up_line), count
    )
    first, _ = gather_rest(first_line, count, index)
    gate_w, gate_last = gather_rest(gate_line, count, index)
    up_w, up_last = gather_rest(up_line, count, index)
    down_w, _ = gather_rest(down_line, count, index)

    forget_w = lax.dynamic_slice_in_dim(
        first[:, 3 * quarter : 3 * quarter + head_count], rank * heads, heads, axis=1
    )
    gain_one = first[:, 3 * quarter + head_count].astype(jnp.float32)
    gain_two = first[:, 3 * quarter + head_count + 1].astype(jnp.float32)
    def replicas(values):
        total = values
        step = 2
        while step < reps:
            other = lax.ppermute(total, "rep", [(r, r ^ step) for r in range(reps)])
            total = add_low(total, other)
            step *= 2
        return total

    def own_of(values):
        pair = replicas(values).reshape(2, shard_rows, values.shape[1])
        sides = both(side == 0, pick(pair, side, 0), swap_side(pick(pair, 1 - side, 0)))
        return both(core == 0, sides, swap_core(sides))

    def both_cores(values):
        mine = replicas(values)
        return both(core == 0, mine, swap_core(mine))

    def turn_rows(values):
        cut = values.reshape(2, 2, quarter, quarter)
        mine = pick(cut, side, 0)
        pair = both(side == 0, mine, swap_side(pick(cut, 1 - side, 0)))
        kept = pick(pair, core, 1)
        quad = both(core == 0, kept, swap_core(pick(pair, 1 - core, 1)))
        return jnp.transpose(quad, (2, 1, 0, 3)).reshape(quarter, model_width)

    def turn_cols(values):
        cut = values.reshape(quarter, 2, 2, quarter)
        mine = pick(cut, core, 2)
        pair = both(core == 0, mine, swap_core(pick(cut, 1 - core, 2)))
        kept = pick(pair, side, 2)
        quad = both(side == 0, kept, swap_side(pick(pair, 1 - side, 2)))
        return quad.reshape(model_width, quarter)

    tokens_all = team_rows(after(tokens, rest_block), first_line)
    facts_all = team_rows(jnp.concatenate([prompt_ids[0], seq_offsets[0]])[None, :])
    chain_ok = jnp.stack([chain_mask(facts_all[b, :NC], facts_all[b, NC:]) for b in range(team)])
    chain_float = chain_ok.astype(jnp.float32)

    inputs_all = tokens_all.astype(jnp.float32)
    scaled_all, inverse_all = normalize(inputs_all)
    scaled1 = scaled_all[:own_rows]
    inverse1 = inverse_all[:own_rows]
    inputs = inputs_all[:own_rows]
    normed1 = after((scaled_all * gain_one).astype(jnp.bfloat16), gate_line)
    row_count = normed1.shape[0]

    qkv_low = matmul(normed1, first[:, : 3 * quarter]).astype(jnp.bfloat16)
    cotangent_all = team_rows(after(cotangent, first_line), qkv_low)
    second = gather_rest(second_line, count, index, qkv_low)[0]
    outgate_w = second[:, :quarter]
    output_w = turn_rows(second[:, quarter:])
    outgate_pre = matmul(normed1, outgate_w)
    bias_mine = lax.dynamic_slice_in_dim(
        forget_bias.astype(jnp.float32), rank * heads, heads, axis=0
    )
    forget_in = matmul(normed1, forget_w) + bias_mine[None, :]
    log_forget = jax.nn.log_sigmoid(forget_in).reshape(team, own_rows, heads)
    decay_sum = jnp.einsum(
        "bij,bjh->bhi", chain_float, log_forget, precision=lax.Precision.HIGHEST
    )

    decay_cols = jnp.transpose(decay_sum, (0, 2, 1))
    attended = attend(
        qkv_low,
        decay_cols,
        decay_sum,
        facts_all,
        heads,
        head_dim,
        team,
        own_rows,
    )
    gate_open = jax.nn.sigmoid(outgate_pre)
    gated_low = (after(attended, up_line, gate_last, cotangent_all) * gate_open).astype(jnp.bfloat16)

    residual = inputs + after(team_sum(matmul(gated_low, output_w)), up_last)
    scaled2, inverse2 = normalize(residual)
    normed2 = after(team_rows((scaled2 * gain_two).astype(jnp.bfloat16)), down_line)
    gate_pre = matmul(normed2, gate_w)
    up_pre = matmul(normed2, up_w)
    sig_gate = jax.nn.sigmoid(gate_pre)
    silu_gate = gate_pre * sig_gate
    act_low = (silu_gate * up_pre).astype(jnp.bfloat16)
    grad_act = matmul_nt(cotangent_all, down_w)
    grad_gate = (grad_act * up_pre * sig_gate * (1.0 + gate_pre * (1.0 - sig_gate))).astype(
        jnp.bfloat16
    )
    grad_up = (grad_act * silu_gate).astype(jnp.bfloat16)
    down_sum = scatter_rest(matmul_tn(act_low, cotangent_all).astype(jnp.bfloat16), count, index)
    pair_normed2 = core_sum(matmul_nt(grad_gate, gate_w) + matmul_nt(grad_up, up_w))
    normed2_late = after(normed2, pair_normed2)
    part_gate_w = matmul_tn(normed2_late, grad_gate).astype(jnp.bfloat16)
    grad_normed2 = after(side_sum(pair_normed2), part_gate_w)
    down_held = down_sum(grad_normed2)
    grad_down = scatter_line(down_held, count)
    gate_sum = scatter_rest(part_gate_w, count, index)
    grad_resid = cotangent.astype(jnp.float32) + norm_back(
        grad_normed2 * gain_two, scaled2, inverse2
    )
    grad_attn_own = grad_resid.astype(jnp.bfloat16)
    normed2_last, act_late = lax.optimization_barrier((normed2_late, act_low, grad_attn_own))[:2]
    part_up_w = matmul_tn(normed2_last, grad_up).astype(jnp.bfloat16)
    up_sum = scatter_rest(part_up_w, count, index)
    part_out = matmul(after(act_late, down_held), down_w)
    gate_held = gate_sum(part_out, part_up_w)
    grad_gate_w = scatter_line(gate_held, count)
    grad_attn = after(team_rows(grad_attn_own, gate_held), grad_down)
    grad_gated = matmul_nt(grad_attn, output_w)
    grad_output_cols = turn_cols(matmul_tn(gated_low, grad_attn).astype(jnp.bfloat16))
    grad_attended = (grad_gated * gate_open).astype(jnp.bfloat16)
    grad_outgate = (grad_gated * attended * gate_open * (1.0 - gate_open)).astype(jnp.bfloat16)
    grad_qkv, grad_logit_rows, grad_logit_cols = attend_back(
        qkv_low, grad_attended, decay_cols, decay_sum, facts_all, heads, head_dim, team, own_rows
    )
    up_held = up_sum(grad_qkv)
    grad_up_w = scatter_line(up_held, count)
    grad_outgate_w = matmul_tn(after(normed1, grad_qkv), grad_outgate).astype(jnp.bfloat16)
    part_second_w = jnp.concatenate([grad_outgate_w, after(grad_output_cols, grad_qkv)], axis=1)
    second_sum = scatter_rest(part_second_w, count, index)
    grad_qkv = after(grad_qkv, grad_gate_w, part_second_w)
    grad_decay = jnp.transpose(grad_logit_rows, (0, 2, 1)) - grad_logit_cols
    grad_log_forget = jnp.einsum(
        "bij,bhi->bjh", chain_float, grad_decay, precision=lax.Precision.HIGHEST
    ).reshape(row_count, heads)
    grad_forget_in = grad_log_forget * jax.nn.sigmoid(-forget_in)
    bias_sum = lax.dynamic_update_slice_in_dim(
        jnp.zeros((head_count,), jnp.float32),
        jnp.sum(grad_forget_in, axis=0),
        rank * heads,
        axis=0,
    )
    bias_near = sum_near(bias_sum[None, :], count)
    grad_forget_low = lax.dynamic_update_slice_in_dim(
        jnp.zeros((row_count, small.shape[1]), jnp.bfloat16),
        grad_forget_in.astype(jnp.bfloat16),
        rank * heads,
        axis=1,
    )
    grad_first = jnp.concatenate([grad_qkv, grad_forget_low], axis=1)
    part_first_w = matmul_tn(normed1, grad_first).astype(jnp.bfloat16)
    second_held = second_sum(part_first_w)
    sum_second = scatter_line(second_held, count)
    part_first_w = after(part_first_w, bias_near, second_held)
    first_sum = scatter_rest(part_first_w, count, index)
    part_normed1 = matmul_nt(after(grad_first, part_first_w, grad_up_w), first) + matmul_nt(
        grad_outgate, outgate_w
    )
    down_own = both_cores(after(grad_down, part_first_w))
    grad_bias = sum_far(after(bias_near, part_first_w), count, reps)
    layer_out = (residual + team_sum(after(part_out, grad_qkv))).astype(jnp.bfloat16)
    first_held = first_sum(grad_bias, layer_out, down_own, sum_second)
    grad_normed1 = team_sum(after(part_normed1, first_held))
    tokens_grad = grad_resid + norm_back(grad_normed1 * gain_one, scaled1, inverse1)
    sum_first = scatter_line(first_held, count)
    gate_own = own_of(after(grad_gate_w, grad_normed1))
    grad_up_w = after(grad_up_w, grad_normed1)
    sum_second = after(sum_second, grad_normed1)

    def whole_cols(own):
        parts = own.shape[3] // quarter
        quad = jnp.transpose(own.astype(jnp.float32), (1, 0, 2, 3))
        quad = quad.reshape(2, 2, shard_rows, parts, quarter)
        quad = jnp.transpose(quad, (3, 2, 0, 1, 4)).reshape(parts, shard_rows, model_width)
        return [quad[p] for p in range(parts)]

    def whole_units(own):
        quad = jnp.transpose(own.astype(jnp.float32), (1, 0, 2, 3))
        quad = quad.reshape(2, 2, shard_rows, count // 2, unit)
        return jnp.transpose(quad, (2, 3, 0, 1, 4)).reshape(shard_rows, team * quarter_ff)

    first_own = own_of(sum_first)
    query_g, key_g, value_g = whole_cols(first_own[..., : 3 * quarter])
    forget_own = first_own[..., 3 * quarter : 3 * quarter + head_count]
    forget_g = jnp.sum(forget_own.astype(jnp.float32), axis=(0, 1))
    outgate_g, output_g = whole_cols(own_of(sum_second))
    gate_g = whole_units(gate_own)
    up_g = whole_units(own_of(grad_up_w))

    def gain_grad(gain, *pairs):
        total = sum(jnp.sum(w.astype(jnp.float32) * grad, axis=1) for w, grad in pairs)
        return total / gain.astype(jnp.float32)

    gain_one_g = gain_grad(
        attn_gain,
        (w_query, query_g),
        (w_key, key_g),
        (w_value, value_g),
        (w_outgate, outgate_g),
        (w_forget, forget_g),
    )
    gain_two_g = gain_grad(ffn_gain, (w_gate, gate_g), (w_up, up_g))
    return (
        layer_out,
        tokens_grad,
        gain_one_g,
        query_g,
        key_g,
        value_g,
        outgate_g,
        forget_g,
        grad_bias,
        output_g,
        gain_two_g,
        gate_g,
        up_g,
        down_own.astype(jnp.float32).reshape(shard_ff, model_width),
    )


def solution(mesh):
    in_specs = (
        P(("rep", "shard"), None),
        P(("rep", "shard"), None),
        P(("rep", "shard"), None),
        P("shard"),
        P("shard", None),
        P("shard", None),
        P("shard", None),
        P("shard", None),
        P("shard", None),
        P(),
        P("shard", None),
        P("shard"),
        P("shard", None),
        P("shard", None),
        P("shard", None),
        P(("rep", "shard"), None),
    )
    out_specs = (
        P(("rep", "shard"), None),
        P(("rep", "shard"), None),
        P("shard"),
        P("shard", None),
        P("shard", None),
        P("shard", None),
        P("shard", None),
        P("shard", None),
        P(),
        P("shard", None),
        P("shard"),
        P("shard", None),
        P("shard", None),
        P("shard", None),
    )

    def program(*arrays):
        return local(*arrays, reps=mesh.shape["rep"], count=mesh.shape["shard"])

    return jax.shard_map(program, mesh=mesh, in_specs=in_specs, out_specs=out_specs, check_vma=False)
```

```python
import jax
import jax.numpy as jnp
from jax import lax
from jax.experimental import pallas as pl
from jax.experimental.pallas import tpu as pltpu
from jax.sharding import PartitionSpec as P

PLEN = 64
CLEN = 64
NP = 2
NC = 4


EPS = 1e-06
NEGATIVE = -1e30


def chain_mask(prompt_ids, offsets):
    positions = jnp.arange(NP * PLEN + NC * CLEN, dtype=jnp.int32)
    in_prompt = positions < NP * PLEN
    after_prompts = positions - NP * PLEN
    sequence = jnp.where(in_prompt, positions // PLEN, NP + after_prompts // CLEN)
    within = jnp.where(in_prompt, positions % PLEN, after_prompts % CLEN)
    cont_index = sequence - NP
    selector = (cont_index[:, None] == jnp.arange(NC, dtype=jnp.int32)[None, :]).astype(jnp.int32)
    owner_id = jnp.where(in_prompt, -1, jnp.sum(selector * prompt_ids[None, :], axis=1))
    reach_end = jnp.sum(selector * offsets[None, :], axis=1)
    same_seq = (sequence[:, None] == sequence[None, :]) & (within[None, :] <= within[:, None])
    from_prompt = (owner_id[:, None] == sequence[None, :]) & (within[None, :] < reach_end[:, None])
    return same_seq | from_prompt


def normalize(values):
    inverse = lax.rsqrt(jnp.mean(values * values, axis=1, keepdims=True) + EPS)
    return (values * inverse, inverse)


def norm_back(grad_scaled, scaled, inverse):
    return inverse * (grad_scaled - scaled * jnp.mean(grad_scaled * scaled, axis=1, keepdims=True))


PROMPTS = NP * PLEN


def dot_nn(left_side, right_side):
    return jnp.dot(left_side, right_side, preferred_element_type=jnp.float32)


def dot_nt(left_side, right_side):
    return lax.dot_general(
        left_side, right_side, (((1,), (1,)), ((), ())), preferred_element_type=jnp.float32
    )


def dot_tn(left_side, right_side):
    return lax.dot_general(
        left_side, right_side, (((0,), (0,)), ((), ())), preferred_element_type=jnp.float32
    )


def key_mask(facts, block, rows):
    row = lax.broadcasted_iota(jnp.int32, (PROMPTS, PROMPTS), 0)
    col = lax.broadcasted_iota(jnp.int32, (PROMPTS, PROMPTS), 1)
    parts = [(row // PLEN == col // PLEN) & (col <= row)]
    within = lax.broadcasted_iota(jnp.int32, (CLEN, PLEN + CLEN), 0)
    key = lax.broadcasted_iota(jnp.int32, (CLEN, PLEN + CLEN), 1)
    for c in range(NC):
        reach = facts[block, NC + c]
        parts.append(((key < PLEN) & (key < reach)) | ((key >= PLEN) & (key - PLEN <= within)))
    return parts


def probs_of(query, keys, decay_col, decay_row, facts, block, masks, scale):
    logits = []
    for part, mask in enumerate(masks):
        if part == 0:
            rows = slice(0, PROMPTS)
            row_decay = decay_row[:, :PROMPTS]
        else:
            start = PROMPTS + (part - 1) * CLEN
            rows = slice(start, start + CLEN)
            first = facts[block, part - 1] == 0
            prompt_decay = jnp.where(first, decay_row[:, :PLEN], decay_row[:, PLEN:PROMPTS])
            row_decay = jnp.concatenate([prompt_decay, decay_row[:, start : start + CLEN]], axis=1)
        product = dot_nt(query[rows], keys[part]) * scale
        logits.append(jnp.where(mask, product + decay_col[rows] - row_decay, NEGATIVE))
    logits = jnp.concatenate(logits, axis=0)
    shifted = jnp.exp(logits - jnp.max(logits, axis=1, keepdims=True))
    return shifted / jnp.sum(shifted, axis=1, keepdims=True)


def part_rows(part):
    if part == 0:
        return slice(0, PROMPTS)
    start = PROMPTS + (part - 1) * CLEN
    return slice(start, start + CLEN)


def part_keys(ref, lanes, facts, block):
    parts = [ref[:PROMPTS, lanes]]
    for c in range(NC):
        start = pl.multiple_of(facts[block, c] * PLEN, PLEN)
        own = part_rows(c + 1)
        parts.append(jnp.concatenate([ref[pl.ds(start, PLEN), lanes], ref[own, lanes]], axis=0))
    return parts


def attend(qkv, decay_cols, decay_rows, facts, heads, head_dim, team, rows):
    width = heads * head_dim
    scale = head_dim ** (-0.5)

    def body(facts_ref, qkv_ref, col_ref, row_ref, out_ref):
        block = pl.program_id(0)
        masks = key_mask(facts_ref, block, rows)
        for h in range(heads):
            lanes = slice(h * head_dim, (h + 1) * head_dim)
            key_lanes = slice(width + h * head_dim, width + (h + 1) * head_dim)
            value_lanes = slice(2 * width + h * head_dim, 2 * width + (h + 1) * head_dim)
            keys = part_keys(qkv_ref, key_lanes, facts_ref, block)
            values = part_keys(qkv_ref, value_lanes, facts_ref, block)
            probs = probs_of(
                qkv_ref[:, lanes], keys, col_ref[0, :, h : h + 1], row_ref[0, h : h + 1, :],
                facts_ref, block, masks, scale,
            ).astype(jnp.bfloat16)
            for part in range(NC + 1):
                at = part_rows(part)
                out_ref[at, lanes] = dot_nn(probs[at], values[part])

    return pl.pallas_call(
        body,
        grid_spec=pltpu.PrefetchScalarGridSpec(
            num_scalar_prefetch=1,
            grid=(team,),
            in_specs=[
                pl.BlockSpec((rows, qkv.shape[1]), lambda b, f: (b, 0)),
                pl.BlockSpec((1, rows, heads), lambda b, f: (b, 0, 0)),
                pl.BlockSpec((1, heads, rows), lambda b, f: (b, 0, 0)),
            ],
            out_specs=pl.BlockSpec((rows, width), lambda b, f: (b, 0)),
        ),
        out_shape=jax.ShapeDtypeStruct((team * rows, width), jnp.float32),
        cost_estimate=pl.CostEstimate(
            flops=8 * team * rows * rows * width,
            bytes_accessed=8 * team * rows * width * 2,
            transcendentals=team * rows * PROMPTS * heads,
        ),
        name="attend",
    )(facts, qkv, decay_cols, decay_rows)


def attend_back(qkv, grad_attended, decay_cols, decay_rows, facts, heads, head_dim, team, rows):
    width = heads * head_dim
    scale = head_dim ** (-0.5)

    def body(facts_ref, qkv_ref, grad_ref, col_ref, row_ref, out_ref, sum_ref, low_ref, key_acc, value_acc):
        block = pl.program_id(0)
        masks = key_mask(facts_ref, block, rows)
        for h in range(heads):
            lanes = slice(h * head_dim, (h + 1) * head_dim)
            key_lanes = slice(width + h * head_dim, width + (h + 1) * head_dim)
            value_lanes = slice(2 * width + h * head_dim, 2 * width + (h + 1) * head_dim)
            keys = part_keys(qkv_ref, key_lanes, facts_ref, block)
            values = part_keys(qkv_ref, value_lanes, facts_ref, block)
            query = qkv_ref[:, lanes]
            grad = grad_ref[:, lanes]
            probs = probs_of(
                query, keys, col_ref[0, :, h : h + 1], row_ref[0, h : h + 1, :],
                facts_ref, block, masks, scale,
            )
            grad_probs = jnp.concatenate(
                [dot_nt(grad[part_rows(p)], values[p]) for p in range(NC + 1)], axis=0
            )
            mean = jnp.sum(probs * grad_probs, axis=1, keepdims=True)
            grad_logits = probs * (grad_probs - mean)
            sum_ref[0, :, h : h + 1] = jnp.sum(grad_logits, axis=1, keepdims=True)
            probs_low = probs.astype(jnp.bfloat16)
            grad_qk = (grad_logits * scale).astype(jnp.bfloat16)
            prompt_sum = jnp.sum(grad_logits[:PROMPTS], axis=0, keepdims=True)
            for part in range(NC + 1):
                at = part_rows(part)
                out_ref[at, lanes] = dot_nn(grad_qk[at], keys[part]).astype(jnp.bfloat16)
                grad_keys = dot_tn(grad_qk[at], query[at])
                grad_values = dot_tn(probs_low[at], grad[at])
                if part == 0:
                    key_acc[...] = grad_keys
                    value_acc[...] = grad_values
                    continue
                start = pl.multiple_of(facts_ref[block, part - 1] * PLEN, PLEN)
                key_acc[pl.ds(start, PLEN), :] += grad_keys[:PLEN]
                value_acc[pl.ds(start, PLEN), :] += grad_values[:PLEN]
                out_ref[at, key_lanes] = grad_keys[PLEN:].astype(jnp.bfloat16)
                out_ref[at, value_lanes] = grad_values[PLEN:].astype(jnp.bfloat16)
                column = jnp.sum(grad_logits[at], axis=0, keepdims=True)
                first = facts_ref[block, part - 1] == 0
                nothing = jnp.zeros((1, PLEN), jnp.float32)
                prompt_sum += jnp.concatenate(
                    [
                        jnp.where(first, column[:, :PLEN], nothing),
                        jnp.where(first, nothing, column[:, :PLEN]),
                    ],
                    axis=1,
                )
                low_ref[0, h : h + 1, at] = column[:, PLEN:]
            low_ref[0, h : h + 1, :PROMPTS] = prompt_sum
            out_ref[:PROMPTS, key_lanes] = key_acc[...].astype(jnp.bfloat16)
            out_ref[:PROMPTS, value_lanes] = value_acc[...].astype(jnp.bfloat16)

    return pl.pallas_call(
        body,
        grid_spec=pltpu.PrefetchScalarGridSpec(
            num_scalar_prefetch=1,
            grid=(team,),
            in_specs=[
                pl.BlockSpec((rows, qkv.shape[1]), lambda b, f: (b, 0)),
                pl.BlockSpec((rows, width), lambda b, f: (b, 0)),
                pl.BlockSpec((1, rows, heads), lambda b, f: (b, 0, 0)),
                pl.BlockSpec((1, heads, rows), lambda b, f: (b, 0, 0)),
            ],
            out_specs=[
                pl.BlockSpec((rows, 3 * width), lambda b, f: (b, 0)),
                pl.BlockSpec((1, rows, heads), lambda b, f: (b, 0, 0)),
                pl.BlockSpec((1, heads, rows), lambda b, f: (b, 0, 0)),
            ],
            scratch_shapes=[
                pltpu.VMEM((PROMPTS, head_dim), jnp.float32),
                pltpu.VMEM((PROMPTS, head_dim), jnp.float32),
            ],
        ),
        out_shape=[
            jax.ShapeDtypeStruct((team * rows, 3 * width), jnp.bfloat16),
            jax.ShapeDtypeStruct((team, rows, heads), jnp.float32),
            jax.ShapeDtypeStruct((team, heads, rows), jnp.float32),
        ],
        cost_estimate=pl.CostEstimate(
            flops=80 * team * rows * rows * width,
            bytes_accessed=7 * team * rows * width * 2,
            transcendentals=team * rows * PROMPTS * heads,
        ),
        name="attend_back",
    )(facts, qkv, grad_attended, decay_cols, decay_rows)


def matmul(left_side, right_side):
    return jnp.dot(left_side, right_side, preferred_element_type=jnp.float32)


def matmul_tn(left_side, right_side):
    return lax.dot_general(
        left_side, right_side, (((0,), (0,)), ((), ())), preferred_element_type=jnp.float32
    )


def matmul_nt(left_side, right_side):
    return lax.dot_general(
        left_side, right_side, (((1,), (1,)), ((), ())), preferred_element_type=jnp.float32
    )


def line_groups(count):
    step = count // 4
    return [[first + step * k for k in range(4)] for first in range(step)]


def middle_strides(count):
    strides = []
    step = count // 8
    while step > 1:
        strides.append(step)
        step //= 2
    return strides


def swap_pairs(count, step):
    return [(s, s ^ step) for s in range(count)]


def both(low_first, mine, other, axis=0):
    return jnp.stack(
        [jnp.where(low_first, mine, other), jnp.where(low_first, other, mine)], axis=axis
    )


def pick(values, at, axis):
    return lax.dynamic_index_in_dim(values, at, axis, keepdims=False)


def add_low(left_side, right_side):
    return (left_side.astype(jnp.float32) + right_side.astype(jnp.float32)).astype(jnp.bfloat16)


def after(values, *others):
    return lax.optimization_barrier((values,) + others)[0]


def gather_line(block, count):
    return lax.all_gather(block, "shard", axis=0, tiled=True, axis_index_groups=line_groups(count))


def gather_rest(line, count, index, *others):
    width = line.shape[1]
    held = line.reshape(4, -1, width)
    for step in reversed(middle_strides(count)):
        other = lax.ppermute(held, "shard", swap_pairs(count, step))
        if others:
            other = after(other, *others)
        held = both((index // step) % 2 == 0, held, other, axis=1).reshape(4, -1, width)
    return held.reshape(-1, width), other


def scatter_rest(values, count, index):
    width = values.shape[1]
    held = values.reshape(4, -1, width)
    strides = middle_strides(count)
    parts = []
    for step in strides:
        if parts:
            held = add_low(*parts)
        at = (index // step) % 2
        halves = held.reshape(4, 2, -1, width)
        other = lax.ppermute(pick(halves, 1 - at, 1), "shard", swap_pairs(count, step))
        parts = [pick(halves, at, 1), other]

    def finish(*others):
        return add_low(parts[0], after(parts[1], *others)).reshape(-1, width)

    return finish


def scatter_line(values, count):
    return lax.psum_scatter(
        values, "shard", scatter_dimension=0, tiled=True, axis_index_groups=line_groups(count)
    )


def sum_near(values, count):
    total = values
    for step in middle_strides(count):
        total = total + lax.ppermute(total, "shard", swap_pairs(count, step))
    return total


def sum_far(near, count, reps):
    total = near
    for step in (count // 2, count // 4, 1):
        total = total + lax.ppermute(total, "shard", swap_pairs(count, step))
    step = 1
    while step < reps:
        total = total + lax.ppermute(total, "rep", [(r, r ^ step) for r in range(reps)])
        step *= 2
    return total[0]


def local(
    tokens,
    prompt_ids,
    seq_offsets,
    attn_gain,
    w_query,
    w_key,
    w_value,
    w_outgate,
    w_forget,
    forget_bias,
    w_output,
    ffn_gain,
    w_gate,
    w_up,
    w_down,
    cotangent,
    *,
    reps,
    count,
):
    own_rows = tokens.shape[0]
    model_width = tokens.shape[1]
    head_count = w_forget.shape[1]
    head_dim = model_width // head_count
    score_scale = head_dim ** (-0.5)
    team = 4
    core = lax.axis_index("rep") % 2
    index = lax.axis_index("shard")
    side = index % 2
    rank = 2 * side + core
    quarter = model_width // team
    heads = head_count // team
    shard_rows = w_query.shape[0]
    shard_ff = w_down.shape[0]
    unit = shard_ff // 2
    quarter_ff = w_gate.shape[1] // team
    core_pairs = [(r, r ^ 1) for r in range(reps)]
    side_pairs = [(s, s ^ 1) for s in range(count)]

    def swap_core(values):
        return lax.ppermute(values, "rep", core_pairs)

    def swap_side(values):
        return lax.ppermute(values, "shard", side_pairs)

    def team_rows(values, *others):
        pair = jnp.concatenate([values, swap_side(values)], axis=0)
        if others:
            pair = after(pair, *others)
        return jnp.concatenate([pair, swap_core(pair)], axis=0)

    def core_sum(partial):
        half = 2 * own_rows
        return partial[:half] + swap_core(partial[half:].astype(jnp.bfloat16)).astype(jnp.float32)

    def side_sum(pair):
        return pair[:own_rows] + swap_side(pair[own_rows:].astype(jnp.bfloat16)).astype(jnp.float32)

    def team_sum(partial):
        return side_sum(core_sum(partial))

    def cols_of(values, who):
        return lax.dynamic_slice_in_dim(values, who * quarter, quarter, axis=1)

    def units_of(values, which_side):
        cut = values.reshape(values.shape[0], count // 2, 2, 2, unit)
        return pick(pick(cut, core, 3), which_side, 2).reshape(values.shape[0], quarter_ff)

    def pair_rows(mine, sent):
        return both(side == 0, mine, swap_side(sent)).reshape(-1, mine.shape[1])

    small = jnp.concatenate(
        [
            w_forget,
            attn_gain[:, None],
            ffn_gain[:, None],
            jnp.zeros((shard_rows, 128 - head_count - 2), jnp.bfloat16),
        ],
        axis=1,
    )
    far_rank = rank ^ 2

    def columns(who, *weights):
        return [cols_of(w, who) for w in weights]

    first_block = pair_rows(
        jnp.concatenate(columns(rank, w_query, w_key, w_value) + [small], axis=1),
        jnp.concatenate(columns(far_rank, w_query, w_key, w_value) + [small], axis=1),
    )
    rest_block = pair_rows(
        jnp.concatenate(
            columns(rank, w_outgate, w_output) + [units_of(w_gate, side), units_of(w_up, side)],
            axis=1,
        ),
        after(
            jnp.concatenate(
                columns(far_rank, w_outgate, w_output)
                + [units_of(w_gate, 1 - side), units_of(w_up, 1 - side)],
                axis=1,
            ),
            first_block,
        ),
    )
    first_line = gather_line(first_block, count)
    second_line = gather_line(after(rest_block[:, : 2 * quarter], first_line), count)
    gate_line = gather_line(
        after(rest_block[:, 2 * quarter : 2 * quarter + quarter_ff], second_line), count
    )
    up_line = gather_line(after(rest_block[:, 2 * quarter + quarter_ff :], gate_line), count)
    down_line = gather_line(
        after(lax.dynamic_slice_in_dim(w_down, core * unit, unit, axis=0), up_line), count
    )
    first, _ = gather_rest(first_line, count, index)
    gate_w, gate_last = gather_rest(gate_line, count, index)
    up_w, up_last = gather_rest(up_line, count, index)
    down_w, _ = gather_rest(down_line, count, index)

    forget_w = lax.dynamic_slice_in_dim(
        first[:, 3 * quarter : 3 * quarter + head_count], rank * heads, heads, axis=1
    )
    gain_one = first[:, 3 * quarter + head_count].astype(jnp.float32)
    gain_two = first[:, 3 * quarter + head_count + 1].astype(jnp.float32)
    def replicas(values):
        total = values
        step = 2
        while step < reps:
            other = lax.ppermute(total, "rep", [(r, r ^ step) for r in range(reps)])
            total = add_low(total, other)
            step *= 2
        return total

    def own_of(values):
        pair = replicas(values).reshape(2, shard_rows, values.shape[1])
        sides = both(side == 0, pick(pair, side, 0), swap_side(pick(pair, 1 - side, 0)))
        return both(core == 0, sides, swap_core(sides))

    def both_cores(values):
        mine = replicas(values)
        return both(core == 0, mine, swap_core(mine))

    def turn_rows(values):
        cut = values.reshape(2, 2, quarter, quarter)
        mine = pick(cut, side, 0)
        pair = both(side == 0, mine, swap_side(pick(cut, 1 - side, 0)))
        kept = pick(pair, core, 1)
        quad = both(core == 0, kept, swap_core(pick(pair, 1 - core, 1)))
        return jnp.transpose(quad, (2, 1, 0, 3)).reshape(quarter, model_width)

    def turn_cols(values):
        cut = values.reshape(quarter, 2, 2, quarter)
        mine = pick(cut, core, 2)
        pair = both(core == 0, mine, swap_core(pick(cut, 1 - core, 2)))
        kept = pick(pair, side, 2)
        quad = both(side == 0, kept, swap_side(pick(pair, 1 - side, 2)))
        return quad.reshape(model_width, quarter)

    tokens_all = team_rows(after(tokens, rest_block), first_line)
    facts_all = team_rows(jnp.concatenate([prompt_ids[0], seq_offsets[0]])[None, :])
    chain_ok = jnp.stack([chain_mask(facts_all[b, :NC], facts_all[b, NC:]) for b in range(team)])
    chain_float = chain_ok.astype(jnp.float32)

    inputs_all = tokens_all.astype(jnp.float32)
    scaled_all, inverse_all = normalize(inputs_all)
    scaled1 = scaled_all[:own_rows]
    inverse1 = inverse_all[:own_rows]
    inputs = inputs_all[:own_rows]
    normed1 = after((scaled_all * gain_one).astype(jnp.bfloat16), gate_line)
    row_count = normed1.shape[0]

    qkv_low = matmul(normed1, first[:, : 3 * quarter]).astype(jnp.bfloat16)
    cotangent_all = team_rows(after(cotangent, first_line), qkv_low)
    second = gather_rest(second_line, count, index, qkv_low)[0]
    outgate_w = second[:, :quarter]
    output_w = turn_rows(second[:, quarter:])
    outgate_pre = matmul(normed1, outgate_w)
    bias_mine = lax.dynamic_slice_in_dim(
        forget_bias.astype(jnp.float32), rank * heads, heads, axis=0
    )
    forget_in = matmul(normed1, forget_w) + bias_mine[None, :]
    log_forget = jax.nn.log_sigmoid(forget_in).reshape(team, own_rows, heads)
    decay_sum = jnp.einsum(
        "bij,bjh->bhi", chain_float, log_forget, precision=lax.Precision.HIGHEST
    )

    decay_cols = jnp.transpose(decay_sum, (0, 2, 1))
    attended = attend(
        qkv_low,
        decay_cols,
        decay_sum,
        facts_all,
        heads,
        head_dim,
        team,
        own_rows,
    )
    gate_open = jax.nn.sigmoid(outgate_pre)
    gated_low = (after(attended, up_line, gate_last, cotangent_all) * gate_open).astype(jnp.bfloat16)

    residual = inputs + after(team_sum(matmul(gated_low, output_w)), up_last)
    scaled2, inverse2 = normalize(residual)
    normed2 = after(team_rows((scaled2 * gain_two).astype(jnp.bfloat16)), down_line)
    gate_pre = matmul(normed2, gate_w)
    up_pre = matmul(normed2, up_w)
    sig_gate = jax.nn.sigmoid(gate_pre)
    silu_gate = gate_pre * sig_gate
    act_low = (silu_gate * up_pre).astype(jnp.bfloat16)
    grad_act = matmul_nt(cotangent_all, down_w)
    grad_gate = (grad_act * up_pre * sig_gate * (1.0 + gate_pre * (1.0 - sig_gate))).astype(
        jnp.bfloat16
    )
    grad_up = (grad_act * silu_gate).astype(jnp.bfloat16)
    down_sum = scatter_rest(matmul_tn(act_low, cotangent_all).astype(jnp.bfloat16), count, index)
    pair_normed2 = core_sum(matmul_nt(grad_gate, gate_w) + matmul_nt(grad_up, up_w))
    normed2_late = after(normed2, pair_normed2)
    part_gate_w = matmul_tn(normed2_late, grad_gate).astype(jnp.bfloat16)
    grad_normed2 = after(side_sum(pair_normed2), part_gate_w)
    down_held = down_sum(grad_normed2)
    grad_down = scatter_line(down_held, count)
    gate_sum = scatter_rest(part_gate_w, count, index)
    grad_resid = cotangent.astype(jnp.float32) + norm_back(
        grad_normed2 * gain_two, scaled2, inverse2
    )
    grad_attn_own = grad_resid.astype(jnp.bfloat16)
    normed2_last, act_late = lax.optimization_barrier((normed2_late, act_low, grad_attn_own))[:2]
    part_up_w = matmul_tn(normed2_last, grad_up).astype(jnp.bfloat16)
    up_sum = scatter_rest(part_up_w, count, index)
    part_out = matmul(after(act_late, down_held), down_w)
    gate_held = gate_sum(part_out, part_up_w)
    grad_gate_w = scatter_line(gate_held, count)
    grad_attn = after(team_rows(grad_attn_own, gate_held), grad_down)
    grad_gated = matmul_nt(grad_attn, output_w)
    grad_output_cols = turn_cols(matmul_tn(gated_low, grad_attn).astype(jnp.bfloat16))
    grad_attended = (grad_gated * gate_open).astype(jnp.bfloat16)
    grad_outgate = (grad_gated * attended * gate_open * (1.0 - gate_open)).astype(jnp.bfloat16)
    grad_qkv, grad_logit_rows, grad_logit_cols = attend_back(
        qkv_low, grad_attended, decay_cols, decay_sum, facts_all, heads, head_dim, team, own_rows
    )
    up_held = up_sum(grad_qkv)
    grad_up_w = scatter_line(up_held, count)
    grad_qkv = after(grad_qkv, grad_gate_w)
    grad_decay = jnp.transpose(grad_logit_rows, (0, 2, 1)) - grad_logit_cols
    grad_log_forget = jnp.einsum(
        "bij,bhi->bjh", chain_float, grad_decay, precision=lax.Precision.HIGHEST
    ).reshape(row_count, heads)
    grad_forget_in = grad_log_forget * jax.nn.sigmoid(-forget_in)
    bias_sum = lax.dynamic_update_slice_in_dim(
        jnp.zeros((head_count,), jnp.float32),
        jnp.sum(grad_forget_in, axis=0),
        rank * heads,
        axis=0,
    )
    bias_near = sum_near(bias_sum[None, :], count)
    grad_forget_low = lax.dynamic_update_slice_in_dim(
        jnp.zeros((row_count, small.shape[1]), jnp.bfloat16),
        grad_forget_in.astype(jnp.bfloat16),
        rank * heads,
        axis=1,
    )
    grad_first = jnp.concatenate([grad_qkv, grad_forget_low], axis=1)
    part_first_w = matmul_tn(normed1, grad_first).astype(jnp.bfloat16)
    first_sum = scatter_rest(after(part_first_w, bias_near), count, index)
    grad_outgate_w = matmul_tn(after(normed1, part_first_w), grad_outgate).astype(jnp.bfloat16)
    part_second_w = jnp.concatenate([grad_outgate_w, grad_output_cols], axis=1)
    second_sum = scatter_rest(part_second_w, count, index)
    down_own = both_cores(after(grad_down, part_first_w))
    grad_bias = sum_far(after(bias_near, part_second_w), count, reps)
    layer_out = (residual + team_sum(after(part_out, grad_qkv))).astype(jnp.bfloat16)
    first_held = first_sum(grad_bias, layer_out, down_own, part_second_w)
    part_normed1 = matmul_nt(after(grad_first, first_held, grad_up_w), first) + matmul_nt(
        grad_outgate, outgate_w
    )
    second_held = second_sum(first_held)
    sum_first = scatter_line(first_held, count)
    grad_normed1 = after(team_sum(after(part_normed1, second_held)), sum_first)
    tokens_grad = grad_resid + norm_back(grad_normed1 * gain_one, scaled1, inverse1)
    sum_second = after(scatter_line(second_held, count), sum_first)
    gate_own = own_of(after(grad_gate_w, part_normed1))
    grad_up_w = after(grad_up_w, grad_normed1)

    def whole_cols(own):
        parts = own.shape[3] // quarter
        quad = jnp.transpose(own.astype(jnp.float32), (1, 0, 2, 3))
        quad = quad.reshape(2, 2, shard_rows, parts, quarter)
        quad = jnp.transpose(quad, (3, 2, 0, 1, 4)).reshape(parts, shard_rows, model_width)
        return [quad[p] for p in range(parts)]

    def whole_units(own):
        quad = jnp.transpose(own.astype(jnp.float32), (1, 0, 2, 3))
        quad = quad.reshape(2, 2, shard_rows, count // 2, unit)
        return jnp.transpose(quad, (2, 3, 0, 1, 4)).reshape(shard_rows, team * quarter_ff)

    first_own = own_of(sum_first)
    query_g, key_g, value_g = whole_cols(first_own[..., : 3 * quarter])
    forget_own = first_own[..., 3 * quarter : 3 * quarter + head_count]
    forget_g = jnp.sum(forget_own.astype(jnp.float32), axis=(0, 1))
    outgate_g, output_g = whole_cols(own_of(sum_second))
    gate_g = whole_units(gate_own)
    up_g = whole_units(own_of(grad_up_w))

    def gain_grad(gain, *pairs):
        total = sum(jnp.sum(w.astype(jnp.float32) * grad, axis=1) for w, grad in pairs)
        return total / gain.astype(jnp.float32)

    gain_one_g = gain_grad(
        attn_gain,
        (w_query, query_g),
        (w_key, key_g),
        (w_value, value_g),
        (w_outgate, outgate_g),
        (w_forget, forget_g),
    )
    gain_two_g = gain_grad(ffn_gain, (w_gate, gate_g), (w_up, up_g))
    return (
        layer_out,
        tokens_grad,
        gain_one_g,
        query_g,
        key_g,
        value_g,
        outgate_g,
        forget_g,
        grad_bias,
        output_g,
        gain_two_g,
        gate_g,
        up_g,
        down_own.astype(jnp.float32).reshape(shard_ff, model_width),
    )


def solution(mesh):
    in_specs = (
        P(("rep", "shard"), None),
        P(("rep", "shard"), None),
        P(("rep", "shard"), None),
        P("shard"),
        P("shard", None),
        P("shard", None),
        P("shard", None),
        P("shard", None),
        P("shard", None),
        P(),
        P("shard", None),
        P("shard"),
        P("shard", None),
        P("shard", None),
        P("shard", None),
        P(("rep", "shard"), None),
    )
    out_specs = (
        P(("rep", "shard"), None),
        P(("rep", "shard"), None),
        P("shard"),
        P("shard", None),
        P("shard", None),
        P("shard", None),
        P("shard", None),
        P("shard", None),
        P(),
        P("shard", None),
        P("shard"),
        P("shard", None),
        P("shard", None),
        P("shard", None),
    )

    def program(*arrays):
        return local(*arrays, reps=mesh.shape["rep"], count=mesh.shape["shard"])

    return jax.shard_map(program, mesh=mesh, in_specs=in_specs, out_specs=out_specs, check_vma=False)
```

```python
import jax
import jax.numpy as jnp
from jax import lax
from jax.experimental import pallas as pl
from jax.experimental.pallas import tpu as pltpu
from jax.sharding import PartitionSpec as P

PLEN = 64
CLEN = 64
NP = 2
NC = 4


EPS = 1e-06
NEGATIVE = -1e30


def chain_mask(prompt_ids, offsets):
    positions = jnp.arange(NP * PLEN + NC * CLEN, dtype=jnp.int32)
    in_prompt = positions < NP * PLEN
    after_prompts = positions - NP * PLEN
    sequence = jnp.where(in_prompt, positions // PLEN, NP + after_prompts // CLEN)
    within = jnp.where(in_prompt, positions % PLEN, after_prompts % CLEN)
    cont_index = sequence - NP
    selector = (cont_index[:, None] == jnp.arange(NC, dtype=jnp.int32)[None, :]).astype(jnp.int32)
    owner_id = jnp.where(in_prompt, -1, jnp.sum(selector * prompt_ids[None, :], axis=1))
    reach_end = jnp.sum(selector * offsets[None, :], axis=1)
    same_seq = (sequence[:, None] == sequence[None, :]) & (within[None, :] <= within[:, None])
    from_prompt = (owner_id[:, None] == sequence[None, :]) & (within[None, :] < reach_end[:, None])
    return same_seq | from_prompt


def normalize(values):
    inverse = lax.rsqrt(jnp.mean(values * values, axis=1, keepdims=True) + EPS)
    return (values * inverse, inverse)


def norm_back(grad_scaled, scaled, inverse):
    return inverse * (grad_scaled - scaled * jnp.mean(grad_scaled * scaled, axis=1, keepdims=True))


PROMPTS = NP * PLEN


def dot_nn(left_side, right_side):
    return jnp.dot(left_side, right_side, preferred_element_type=jnp.float32)


def dot_nt(left_side, right_side):
    return lax.dot_general(
        left_side, right_side, (((1,), (1,)), ((), ())), preferred_element_type=jnp.float32
    )


def dot_tn(left_side, right_side):
    return lax.dot_general(
        left_side, right_side, (((0,), (0,)), ((), ())), preferred_element_type=jnp.float32
    )


def key_mask(facts, block, rows):
    row = lax.broadcasted_iota(jnp.int32, (PROMPTS, PROMPTS), 0)
    col = lax.broadcasted_iota(jnp.int32, (PROMPTS, PROMPTS), 1)
    parts = [(row // PLEN == col // PLEN) & (col <= row)]
    within = lax.broadcasted_iota(jnp.int32, (CLEN, PLEN + CLEN), 0)
    key = lax.broadcasted_iota(jnp.int32, (CLEN, PLEN + CLEN), 1)
    for c in range(NC):
        reach = facts[block, NC + c]
        parts.append(((key < PLEN) & (key < reach)) | ((key >= PLEN) & (key - PLEN <= within)))
    return parts


def probs_of(query, keys, decay_col, decay_row, facts, block, masks, scale):
    logits = []
    for part, mask in enumerate(masks):
        if part == 0:
            rows = slice(0, PROMPTS)
            row_decay = decay_row[:, :PROMPTS]
        else:
            start = PROMPTS + (part - 1) * CLEN
            rows = slice(start, start + CLEN)
            first = facts[block, part - 1] == 0
            prompt_decay = jnp.where(first, decay_row[:, :PLEN], decay_row[:, PLEN:PROMPTS])
            row_decay = jnp.concatenate([prompt_decay, decay_row[:, start : start + CLEN]], axis=1)
        product = dot_nt(query[rows], keys[part]) * scale
        logits.append(jnp.where(mask, product + decay_col[rows] - row_decay, NEGATIVE))
    logits = jnp.concatenate(logits, axis=0)
    shifted = jnp.exp(logits - jnp.max(logits, axis=1, keepdims=True))
    return shifted / jnp.sum(shifted, axis=1, keepdims=True)


def part_rows(part):
    if part == 0:
        return slice(0, PROMPTS)
    start = PROMPTS + (part - 1) * CLEN
    return slice(start, start + CLEN)


def part_keys(ref, lanes, facts, block):
    parts = [ref[:PROMPTS, lanes]]
    for c in range(NC):
        start = pl.multiple_of(facts[block, c] * PLEN, PLEN)
        own = part_rows(c + 1)
        parts.append(jnp.concatenate([ref[pl.ds(start, PLEN), lanes], ref[own, lanes]], axis=0))
    return parts


def attend(qkv, decay_cols, decay_rows, facts, heads, head_dim, team, rows):
    width = heads * head_dim
    scale = head_dim ** (-0.5)

    def body(facts_ref, qkv_ref, col_ref, row_ref, out_ref):
        block = pl.program_id(0)
        masks = key_mask(facts_ref, block, rows)
        for h in range(heads):
            lanes = slice(h * head_dim, (h + 1) * head_dim)
            key_lanes = slice(width + h * head_dim, width + (h + 1) * head_dim)
            value_lanes = slice(2 * width + h * head_dim, 2 * width + (h + 1) * head_dim)
            keys = part_keys(qkv_ref, key_lanes, facts_ref, block)
            values = part_keys(qkv_ref, value_lanes, facts_ref, block)
            probs = probs_of(
                qkv_ref[:, lanes], keys, col_ref[0, :, h : h + 1], row_ref[0, h : h + 1, :],
                facts_ref, block, masks, scale,
            ).astype(jnp.bfloat16)
            for part in range(NC + 1):
                at = part_rows(part)
                out_ref[at, lanes] = dot_nn(probs[at], values[part])

    return pl.pallas_call(
        body,
        grid_spec=pltpu.PrefetchScalarGridSpec(
            num_scalar_prefetch=1,
            grid=(team,),
            in_specs=[
                pl.BlockSpec((rows, qkv.shape[1]), lambda b, f: (b, 0)),
                pl.BlockSpec((1, rows, heads), lambda b, f: (b, 0, 0)),
                pl.BlockSpec((1, heads, rows), lambda b, f: (b, 0, 0)),
            ],
            out_specs=pl.BlockSpec((rows, width), lambda b, f: (b, 0)),
        ),
        out_shape=jax.ShapeDtypeStruct((team * rows, width), jnp.float32),
        cost_estimate=pl.CostEstimate(
            flops=8 * team * rows * rows * width,
            bytes_accessed=8 * team * rows * width * 2,
            transcendentals=team * rows * PROMPTS * heads,
        ),
        name="attend",
    )(facts, qkv, decay_cols, decay_rows)


def attend_back(qkv, grad_attended, decay_cols, decay_rows, facts, heads, head_dim, team, rows):
    width = heads * head_dim
    scale = head_dim ** (-0.5)

    def body(facts_ref, qkv_ref, grad_ref, col_ref, row_ref, out_ref, sum_ref, low_ref, key_acc, value_acc):
        block = pl.program_id(0)
        masks = key_mask(facts_ref, block, rows)
        for h in range(heads):
            lanes = slice(h * head_dim, (h + 1) * head_dim)
            key_lanes = slice(width + h * head_dim, width + (h + 1) * head_dim)
            value_lanes = slice(2 * width + h * head_dim, 2 * width + (h + 1) * head_dim)
            keys = part_keys(qkv_ref, key_lanes, facts_ref, block)
            values = part_keys(qkv_ref, value_lanes, facts_ref, block)
            query = qkv_ref[:, lanes]
            grad = grad_ref[:, lanes]
            probs = probs_of(
                query, keys, col_ref[0, :, h : h + 1], row_ref[0, h : h + 1, :],
                facts_ref, block, masks, scale,
            )
            grad_probs = jnp.concatenate(
                [dot_nt(grad[part_rows(p)], values[p]) for p in range(NC + 1)], axis=0
            )
            mean = jnp.sum(probs * grad_probs, axis=1, keepdims=True)
            grad_logits = probs * (grad_probs - mean)
            sum_ref[0, :, h : h + 1] = jnp.sum(grad_logits, axis=1, keepdims=True)
            probs_low = probs.astype(jnp.bfloat16)
            grad_qk = (grad_logits * scale).astype(jnp.bfloat16)
            prompt_sum = jnp.sum(grad_logits[:PROMPTS], axis=0, keepdims=True)
            for part in range(NC + 1):
                at = part_rows(part)
                out_ref[at, lanes] = dot_nn(grad_qk[at], keys[part]).astype(jnp.bfloat16)
                grad_keys = dot_tn(grad_qk[at], query[at])
                grad_values = dot_tn(probs_low[at], grad[at])
                if part == 0:
                    key_acc[...] = grad_keys
                    value_acc[...] = grad_values
                    continue
                start = pl.multiple_of(facts_ref[block, part - 1] * PLEN, PLEN)
                key_acc[pl.ds(start, PLEN), :] += grad_keys[:PLEN]
                value_acc[pl.ds(start, PLEN), :] += grad_values[:PLEN]
                out_ref[at, key_lanes] = grad_keys[PLEN:].astype(jnp.bfloat16)
                out_ref[at, value_lanes] = grad_values[PLEN:].astype(jnp.bfloat16)
                column = jnp.sum(grad_logits[at], axis=0, keepdims=True)
                first = facts_ref[block, part - 1] == 0
                nothing = jnp.zeros((1, PLEN), jnp.float32)
                prompt_sum += jnp.concatenate(
                    [
                        jnp.where(first, column[:, :PLEN], nothing),
                        jnp.where(first, nothing, column[:, :PLEN]),
                    ],
                    axis=1,
                )
                low_ref[0, h : h + 1, at] = column[:, PLEN:]
            low_ref[0, h : h + 1, :PROMPTS] = prompt_sum
            out_ref[:PROMPTS, key_lanes] = key_acc[...].astype(jnp.bfloat16)
            out_ref[:PROMPTS, value_lanes] = value_acc[...].astype(jnp.bfloat16)

    return pl.pallas_call(
        body,
        grid_spec=pltpu.PrefetchScalarGridSpec(
            num_scalar_prefetch=1,
            grid=(team,),
            in_specs=[
                pl.BlockSpec((rows, qkv.shape[1]), lambda b, f: (b, 0)),
                pl.BlockSpec((rows, width), lambda b, f: (b, 0)),
                pl.BlockSpec((1, rows, heads), lambda b, f: (b, 0, 0)),
                pl.BlockSpec((1, heads, rows), lambda b, f: (b, 0, 0)),
            ],
            out_specs=[
                pl.BlockSpec((rows, 3 * width), lambda b, f: (b, 0)),
                pl.BlockSpec((1, rows, heads), lambda b, f: (b, 0, 0)),
                pl.BlockSpec((1, heads, rows), lambda b, f: (b, 0, 0)),
            ],
            scratch_shapes=[
                pltpu.VMEM((PROMPTS, head_dim), jnp.float32),
                pltpu.VMEM((PROMPTS, head_dim), jnp.float32),
            ],
        ),
        out_shape=[
            jax.ShapeDtypeStruct((team * rows, 3 * width), jnp.bfloat16),
            jax.ShapeDtypeStruct((team, rows, heads), jnp.float32),
            jax.ShapeDtypeStruct((team, heads, rows), jnp.float32),
        ],
        cost_estimate=pl.CostEstimate(
            flops=80 * team * rows * rows * width,
            bytes_accessed=7 * team * rows * width * 2,
            transcendentals=team * rows * PROMPTS * heads,
        ),
        name="attend_back",
    )(facts, qkv, grad_attended, decay_cols, decay_rows)


def matmul(left_side, right_side):
    return jnp.dot(left_side, right_side, preferred_element_type=jnp.float32)


def matmul_tn(left_side, right_side):
    return lax.dot_general(
        left_side, right_side, (((0,), (0,)), ((), ())), preferred_element_type=jnp.float32
    )


def matmul_nt(left_side, right_side):
    return lax.dot_general(
        left_side, right_side, (((1,), (1,)), ((), ())), preferred_element_type=jnp.float32
    )


def line_groups(count):
    step = count // 4
    return [[first + step * k for k in range(4)] for first in range(step)]


def middle_strides(count):
    strides = []
    step = count // 8
    while step > 1:
        strides.append(step)
        step //= 2
    return strides


def swap_pairs(count, step):
    return [(s, s ^ step) for s in range(count)]


def both(low_first, mine, other, axis=0):
    return jnp.stack(
        [jnp.where(low_first, mine, other), jnp.where(low_first, other, mine)], axis=axis
    )


def pick(values, at, axis):
    return lax.dynamic_index_in_dim(values, at, axis, keepdims=False)


def add_low(left_side, right_side):
    return (left_side.astype(jnp.float32) + right_side.astype(jnp.float32)).astype(jnp.bfloat16)


def after(values, *others):
    return lax.optimization_barrier((values,) + others)[0]


def gather_line(block, count):
    return lax.all_gather(block, "shard", axis=0, tiled=True, axis_index_groups=line_groups(count))


def gather_rest(line, count, index, *others):
    width = line.shape[1]
    held = line.reshape(4, -1, width)
    for step in reversed(middle_strides(count)):
        other = lax.ppermute(held, "shard", swap_pairs(count, step))
        if others:
            other = after(other, *others)
        held = both((index // step) % 2 == 0, held, other, axis=1).reshape(4, -1, width)
    return held.reshape(-1, width), other


def scatter_rest(values, count, index):
    width = values.shape[1]
    held = values.reshape(4, -1, width)
    strides = middle_strides(count)
    parts = []
    for step in strides:
        if parts:
            held = add_low(*parts)
        at = (index // step) % 2
        halves = held.reshape(4, 2, -1, width)
        other = lax.ppermute(pick(halves, 1 - at, 1), "shard", swap_pairs(count, step))
        parts = [pick(halves, at, 1), other]

    def finish(*others):
        return add_low(parts[0], after(parts[1], *others)).reshape(-1, width)

    return finish


def scatter_line(values, count):
    return lax.psum_scatter(
        values, "shard", scatter_dimension=0, tiled=True, axis_index_groups=line_groups(count)
    )


def sum_near(values, count):
    total = values
    for step in middle_strides(count):
        total = total + lax.ppermute(total, "shard", swap_pairs(count, step))
    return total


def sum_far(near, count, reps):
    total = near
    for step in (count // 2, count // 4, 1):
        total = total + lax.ppermute(total, "shard", swap_pairs(count, step))
    step = 1
    while step < reps:
        total = total + lax.ppermute(total, "rep", [(r, r ^ step) for r in range(reps)])
        step *= 2
    return total[0]


def local(
    tokens,
    prompt_ids,
    seq_offsets,
    attn_gain,
    w_query,
    w_key,
    w_value,
    w_outgate,
    w_forget,
    forget_bias,
    w_output,
    ffn_gain,
    w_gate,
    w_up,
    w_down,
    cotangent,
    *,
    reps,
    count,
):
    own_rows = tokens.shape[0]
    model_width = tokens.shape[1]
    head_count = w_forget.shape[1]
    head_dim = model_width // head_count
    score_scale = head_dim ** (-0.5)
    team = 4
    core = lax.axis_index("rep") % 2
    index = lax.axis_index("shard")
    side = index % 2
    rank = 2 * side + core
    quarter = model_width // team
    heads = head_count // team
    shard_rows = w_query.shape[0]
    shard_ff = w_down.shape[0]
    unit = shard_ff // 2
    quarter_ff = w_gate.shape[1] // team
    core_pairs = [(r, r ^ 1) for r in range(reps)]
    side_pairs = [(s, s ^ 1) for s in range(count)]

    def swap_core(values):
        return lax.ppermute(values, "rep", core_pairs)

    def swap_side(values):
        return lax.ppermute(values, "shard", side_pairs)

    def team_rows(values, *others):
        pair = jnp.concatenate([values, swap_side(values)], axis=0)
        if others:
            pair = after(pair, *others)
        return jnp.concatenate([pair, swap_core(pair)], axis=0)

    def core_sum(partial):
        half = 2 * own_rows
        return partial[:half] + swap_core(partial[half:].astype(jnp.bfloat16)).astype(jnp.float32)

    def side_sum(pair):
        return pair[:own_rows] + swap_side(pair[own_rows:].astype(jnp.bfloat16)).astype(jnp.float32)

    def team_sum(partial):
        return side_sum(core_sum(partial))

    def cols_of(values, who):
        return lax.dynamic_slice_in_dim(values, who * quarter, quarter, axis=1)

    def units_of(values, which_side):
        cut = values.reshape(values.shape[0], count // 2, 2, 2, unit)
        return pick(pick(cut, core, 3), which_side, 2).reshape(values.shape[0], quarter_ff)

    def pair_rows(mine, sent):
        return both(side == 0, mine, swap_side(sent)).reshape(-1, mine.shape[1])

    small = jnp.concatenate(
        [
            w_forget,
            attn_gain[:, None],
            ffn_gain[:, None],
            jnp.zeros((shard_rows, 128 - head_count - 2), jnp.bfloat16),
        ],
        axis=1,
    )
    far_rank = rank ^ 2

    def columns(who, *weights):
        return [cols_of(w, who) for w in weights]

    first_block = pair_rows(
        jnp.concatenate(columns(rank, w_query, w_key, w_value) + [small], axis=1),
        jnp.concatenate(columns(far_rank, w_query, w_key, w_value) + [small], axis=1),
    )
    rest_block = pair_rows(
        jnp.concatenate(
            columns(rank, w_outgate, w_output) + [units_of(w_gate, side), units_of(w_up, side)],
            axis=1,
        ),
        after(
            jnp.concatenate(
                columns(far_rank, w_outgate, w_output)
                + [units_of(w_gate, 1 - side), units_of(w_up, 1 - side)],
                axis=1,
            ),
            first_block,
        ),
    )
    first_line = gather_line(first_block, count)
    second_line = gather_line(after(rest_block[:, : 2 * quarter], first_line), count)
    gate_line = gather_line(
        after(rest_block[:, 2 * quarter : 2 * quarter + quarter_ff], second_line), count
    )
    up_line = gather_line(after(rest_block[:, 2 * quarter + quarter_ff :], gate_line), count)
    down_line = gather_line(
        after(lax.dynamic_slice_in_dim(w_down, core * unit, unit, axis=0), up_line), count
    )
    first, _ = gather_rest(first_line, count, index)
    gate_w, gate_last = gather_rest(gate_line, count, index)
    up_w, up_last = gather_rest(up_line, count, index)
    down_w, _ = gather_rest(down_line, count, index)

    forget_w = lax.dynamic_slice_in_dim(
        first[:, 3 * quarter : 3 * quarter + head_count], rank * heads, heads, axis=1
    )
    gain_one = first[:, 3 * quarter + head_count].astype(jnp.float32)
    gain_two = first[:, 3 * quarter + head_count + 1].astype(jnp.float32)
    def replicas(values):
        total = values
        step = 2
        while step < reps:
            other = lax.ppermute(total, "rep", [(r, r ^ step) for r in range(reps)])
            total = add_low(total, other)
            step *= 2
        return total

    def own_of(values):
        pair = replicas(values).reshape(2, shard_rows, values.shape[1])
        sides = both(side == 0, pick(pair, side, 0), swap_side(pick(pair, 1 - side, 0)))
        return both(core == 0, sides, swap_core(sides))

    def both_cores(values):
        mine = replicas(values)
        return both(core == 0, mine, swap_core(mine))

    def turn_rows(values):
        cut = values.reshape(2, 2, quarter, quarter)
        mine = pick(cut, side, 0)
        pair = both(side == 0, mine, swap_side(pick(cut, 1 - side, 0)))
        kept = pick(pair, core, 1)
        quad = both(core == 0, kept, swap_core(pick(pair, 1 - core, 1)))
        return jnp.transpose(quad, (2, 1, 0, 3)).reshape(quarter, model_width)

    def turn_cols(values):
        cut = values.reshape(quarter, 2, 2, quarter)
        mine = pick(cut, core, 2)
        pair = both(core == 0, mine, swap_core(pick(cut, 1 - core, 2)))
        kept = pick(pair, side, 2)
        quad = both(side == 0, kept, swap_side(pick(pair, 1 - side, 2)))
        return quad.reshape(model_width, quarter)

    tokens_all = team_rows(after(tokens, rest_block), first_line)
    facts_all = team_rows(jnp.concatenate([prompt_ids[0], seq_offsets[0]])[None, :])
    chain_ok = jnp.stack([chain_mask(facts_all[b, :NC], facts_all[b, NC:]) for b in range(team)])
    chain_float = chain_ok.astype(jnp.float32)

    inputs_all = tokens_all.astype(jnp.float32)
    scaled_all, inverse_all = normalize(inputs_all)
    scaled1 = scaled_all[:own_rows]
    inverse1 = inverse_all[:own_rows]
    inputs = inputs_all[:own_rows]
    normed1 = after((scaled_all * gain_one).astype(jnp.bfloat16), gate_line)
    row_count = normed1.shape[0]

    qkv_low = matmul(normed1, first[:, : 3 * quarter]).astype(jnp.bfloat16)
    cotangent_all = team_rows(after(cotangent, first_line), qkv_low)
    second = gather_rest(second_line, count, index, qkv_low)[0]
    outgate_w = second[:, :quarter]
    output_w = turn_rows(second[:, quarter:])
    outgate_pre = matmul(normed1, outgate_w)
    bias_mine = lax.dynamic_slice_in_dim(
        forget_bias.astype(jnp.float32), rank * heads, heads, axis=0
    )
    forget_in = matmul(normed1, forget_w) + bias_mine[None, :]
    log_forget = jax.nn.log_sigmoid(forget_in).reshape(team, own_rows, heads)
    decay_sum = jnp.einsum(
        "bij,bjh->bhi", chain_float, log_forget, precision=lax.Precision.HIGHEST
    )

    decay_cols = jnp.transpose(decay_sum, (0, 2, 1))
    attended = attend(
        qkv_low,
        decay_cols,
        decay_sum,
        facts_all,
        heads,
        head_dim,
        team,
        own_rows,
    )
    gate_open = jax.nn.sigmoid(outgate_pre)
    gated_low = (after(attended, up_line, gate_last, cotangent_all) * gate_open).astype(jnp.bfloat16)

    residual = inputs + after(team_sum(matmul(gated_low, output_w)), up_last)
    scaled2, inverse2 = normalize(residual)
    normed2 = after(team_rows((scaled2 * gain_two).astype(jnp.bfloat16)), down_line)
    gate_pre = matmul(normed2, gate_w)
    up_pre = matmul(normed2, up_w)
    sig_gate = jax.nn.sigmoid(gate_pre)
    silu_gate = gate_pre * sig_gate
    act_low = (silu_gate * up_pre).astype(jnp.bfloat16)
    grad_act = matmul_nt(cotangent_all, down_w)
    grad_gate = (grad_act * up_pre * sig_gate * (1.0 + gate_pre * (1.0 - sig_gate))).astype(
        jnp.bfloat16
    )
    grad_up = (grad_act * silu_gate).astype(jnp.bfloat16)
    down_sum = scatter_rest(matmul_tn(act_low, cotangent_all).astype(jnp.bfloat16), count, index)
    pair_normed2 = core_sum(matmul_nt(grad_gate, gate_w) + matmul_nt(grad_up, up_w))
    normed2_late = after(normed2, pair_normed2)
    part_gate_w = matmul_tn(normed2_late, grad_gate).astype(jnp.bfloat16)
    grad_normed2 = after(side_sum(pair_normed2), part_gate_w)
    down_held = down_sum(grad_normed2)
    grad_down = scatter_line(down_held, count)
    gate_sum = scatter_rest(part_gate_w, count, index)
    grad_resid = cotangent.astype(jnp.float32) + norm_back(
        grad_normed2 * gain_two, scaled2, inverse2
    )
    grad_attn_own = grad_resid.astype(jnp.bfloat16)
    normed2_last, act_late = lax.optimization_barrier((normed2_late, act_low, grad_attn_own))[:2]
    part_up_w = matmul_tn(normed2_last, grad_up).astype(jnp.bfloat16)
    up_sum = scatter_rest(part_up_w, count, index)
    part_out = matmul(after(act_late, down_held), down_w)
    gate_held = gate_sum(part_out, part_up_w)
    grad_gate_w = scatter_line(gate_held, count)
    grad_attn = after(team_rows(grad_attn_own, gate_held), grad_down)
    grad_gated = matmul_nt(grad_attn, output_w)
    grad_output_cols = turn_cols(matmul_tn(gated_low, grad_attn).astype(jnp.bfloat16))
    grad_attended = (grad_gated * gate_open).astype(jnp.bfloat16)
    grad_outgate = (grad_gated * attended * gate_open * (1.0 - gate_open)).astype(jnp.bfloat16)
    up_held = up_sum(grad_outgate)
    grad_outgate_w = matmul_tn(after(normed1, up_held), grad_outgate).astype(jnp.bfloat16)
    part_second_w = jnp.concatenate([grad_outgate_w, grad_output_cols], axis=1)
    second_sum = scatter_rest(part_second_w, count, index)
    grad_up_w = scatter_line(up_held, count)
    grad_qkv, grad_logit_rows, grad_logit_cols = attend_back(
        qkv_low,
        after(grad_attended, up_held, part_second_w),
        decay_cols,
        decay_sum,
        facts_all,
        heads,
        head_dim,
        team,
        own_rows,
    )
    second_held = second_sum(grad_qkv)
    grad_qkv = after(grad_qkv, grad_gate_w, second_held, grad_up_w)
    sum_second = scatter_line(second_held, count)
    layer_out = (residual + team_sum(after(part_out, grad_qkv))).astype(jnp.bfloat16)
    grad_decay = jnp.transpose(grad_logit_rows, (0, 2, 1)) - grad_logit_cols
    grad_log_forget = jnp.einsum(
        "bij,bhi->bjh", chain_float, grad_decay, precision=lax.Precision.HIGHEST
    ).reshape(row_count, heads)
    grad_forget_in = grad_log_forget * jax.nn.sigmoid(-forget_in)
    bias_sum = lax.dynamic_update_slice_in_dim(
        jnp.zeros((head_count,), jnp.float32),
        jnp.sum(grad_forget_in, axis=0),
        rank * heads,
        axis=0,
    )
    bias_near = sum_near(bias_sum[None, :], count)
    grad_forget_low = lax.dynamic_update_slice_in_dim(
        jnp.zeros((row_count, small.shape[1]), jnp.bfloat16),
        grad_forget_in.astype(jnp.bfloat16),
        rank * heads,
        axis=1,
    )
    grad_first = jnp.concatenate([grad_qkv, grad_forget_low], axis=1)
    part_first_w = matmul_tn(normed1, grad_first).astype(jnp.bfloat16)
    first_sum = scatter_rest(after(part_first_w, bias_near), count, index)
    part_normed1 = matmul_nt(after(grad_first, part_first_w), first) + matmul_nt(
        grad_outgate, outgate_w
    )
    down_own = both_cores(after(grad_down, part_first_w))
    grad_bias = sum_far(after(bias_near, part_first_w), count, reps)
    first_held = first_sum(grad_bias, layer_out, down_own, sum_second)
    sum_first = scatter_line(first_held, count)
    grad_normed1 = after(team_sum(after(part_normed1, first_held)), sum_first)
    tokens_grad = grad_resid + norm_back(grad_normed1 * gain_one, scaled1, inverse1)
    gate_own = own_of(after(grad_gate_w, first_held))
    grad_up_w = after(grad_up_w, grad_normed1)
    sum_second = after(sum_second, grad_normed1)

    def whole_cols(own):
        parts = own.shape[3] // quarter
        quad = jnp.transpose(own.astype(jnp.float32), (1, 0, 2, 3))
        quad = quad.reshape(2, 2, shard_rows, parts, quarter)
        quad = jnp.transpose(quad, (3, 2, 0, 1, 4)).reshape(parts, shard_rows, model_width)
        return [quad[p] for p in range(parts)]

    def whole_units(own):
        quad = jnp.transpose(own.astype(jnp.float32), (1, 0, 2, 3))
        quad = quad.reshape(2, 2, shard_rows, count // 2, unit)
        return jnp.transpose(quad, (2, 3, 0, 1, 4)).reshape(shard_rows, team * quarter_ff)

    first_own = own_of(sum_first)
    query_g, key_g, value_g = whole_cols(first_own[..., : 3 * quarter])
    forget_own = first_own[..., 3 * quarter : 3 * quarter + head_count]
    forget_g = jnp.sum(forget_own.astype(jnp.float32), axis=(0, 1))
    outgate_g, output_g = whole_cols(own_of(sum_second))
    gate_g = whole_units(gate_own)
    up_g = whole_units(own_of(grad_up_w))

    def gain_grad(gain, *pairs):
        total = sum(jnp.sum(w.astype(jnp.float32) * grad, axis=1) for w, grad in pairs)
        return total / gain.astype(jnp.float32)

    gain_one_g = gain_grad(
        attn_gain,
        (w_query, query_g),
        (w_key, key_g),
        (w_value, value_g),
        (w_outgate, outgate_g),
        (w_forget, forget_g),
    )
    gain_two_g = gain_grad(ffn_gain, (w_gate, gate_g), (w_up, up_g))
    return (
        layer_out,
        tokens_grad,
        gain_one_g,
        query_g,
        key_g,
        value_g,
        outgate_g,
        forget_g,
        grad_bias,
        output_g,
        gain_two_g,
        gate_g,
        up_g,
        down_own.astype(jnp.float32).reshape(shard_ff, model_width),
    )


def solution(mesh):
    in_specs = (
        P(("rep", "shard"), None),
        P(("rep", "shard"), None),
        P(("rep", "shard"), None),
        P("shard"),
        P("shard", None),
        P("shard", None),
        P("shard", None),
        P("shard", None),
        P("shard", None),
        P(),
        P("shard", None),
        P("shard"),
        P("shard", None),
        P("shard", None),
        P("shard", None),
        P(("rep", "shard"), None),
    )
    out_specs = (
        P(("rep", "shard"), None),
        P(("rep", "shard"), None),
        P("shard"),
        P("shard", None),
        P("shard", None),
        P("shard", None),
        P("shard", None),
        P("shard", None),
        P(),
        P("shard", None),
        P("shard"),
        P("shard", None),
        P("shard", None),
        P("shard", None),
    )

    def program(*arrays):
        return local(*arrays, reps=mesh.shape["rep"], count=mesh.shape["shard"])

    return jax.shard_map(program, mesh=mesh, in_specs=in_specs, out_specs=out_specs, check_vma=False)
```

```python
import jax
import jax.numpy as jnp
from jax import lax
from jax.experimental import pallas as pl
from jax.experimental.pallas import tpu as pltpu
from jax.sharding import PartitionSpec as P

PLEN = 64
CLEN = 64
NP = 2
NC = 4


EPS = 1e-06
NEGATIVE = -1e30


def chain_mask(prompt_ids, offsets):
    positions = jnp.arange(NP * PLEN + NC * CLEN, dtype=jnp.int32)
    in_prompt = positions < NP * PLEN
    after_prompts = positions - NP * PLEN
    sequence = jnp.where(in_prompt, positions // PLEN, NP + after_prompts // CLEN)
    within = jnp.where(in_prompt, positions % PLEN, after_prompts % CLEN)
    cont_index = sequence - NP
    selector = (cont_index[:, None] == jnp.arange(NC, dtype=jnp.int32)[None, :]).astype(jnp.int32)
    owner_id = jnp.where(in_prompt, -1, jnp.sum(selector * prompt_ids[None, :], axis=1))
    reach_end = jnp.sum(selector * offsets[None, :], axis=1)
    same_seq = (sequence[:, None] == sequence[None, :]) & (within[None, :] <= within[:, None])
    from_prompt = (owner_id[:, None] == sequence[None, :]) & (within[None, :] < reach_end[:, None])
    return same_seq | from_prompt


def normalize(values):
    inverse = lax.rsqrt(jnp.mean(values * values, axis=1, keepdims=True) + EPS)
    return (values * inverse, inverse)


def norm_back(grad_scaled, scaled, inverse):
    return inverse * (grad_scaled - scaled * jnp.mean(grad_scaled * scaled, axis=1, keepdims=True))


PROMPTS = NP * PLEN


def dot_nn(left_side, right_side):
    return jnp.dot(left_side, right_side, preferred_element_type=jnp.float32)


def dot_nt(left_side, right_side):
    return lax.dot_general(
        left_side, right_side, (((1,), (1,)), ((), ())), preferred_element_type=jnp.float32
    )


def dot_tn(left_side, right_side):
    return lax.dot_general(
        left_side, right_side, (((0,), (0,)), ((), ())), preferred_element_type=jnp.float32
    )


def key_mask(facts, block, rows):
    row = lax.broadcasted_iota(jnp.int32, (PROMPTS, PROMPTS), 0)
    col = lax.broadcasted_iota(jnp.int32, (PROMPTS, PROMPTS), 1)
    parts = [(row // PLEN == col // PLEN) & (col <= row)]
    within = lax.broadcasted_iota(jnp.int32, (CLEN, PLEN + CLEN), 0)
    key = lax.broadcasted_iota(jnp.int32, (CLEN, PLEN + CLEN), 1)
    for c in range(NC):
        reach = facts[block, NC + c]
        parts.append(((key < PLEN) & (key < reach)) | ((key >= PLEN) & (key - PLEN <= within)))
    return parts


def probs_of(query, keys, decay_col, decay_row, facts, block, masks, scale):
    logits = []
    for part, mask in enumerate(masks):
        if part == 0:
            rows = slice(0, PROMPTS)
            row_decay = decay_row[:, :PROMPTS]
        else:
            start = PROMPTS + (part - 1) * CLEN
            rows = slice(start, start + CLEN)
            first = facts[block, part - 1] == 0
            prompt_decay = jnp.where(first, decay_row[:, :PLEN], decay_row[:, PLEN:PROMPTS])
            row_decay = jnp.concatenate([prompt_decay, decay_row[:, start : start + CLEN]], axis=1)
        product = dot_nt(query[rows], keys[part]) * scale
        logits.append(jnp.where(mask, product + decay_col[rows] - row_decay, NEGATIVE))
    logits = jnp.concatenate(logits, axis=0)
    shifted = jnp.exp(logits - jnp.max(logits, axis=1, keepdims=True))
    return shifted / jnp.sum(shifted, axis=1, keepdims=True)


def part_rows(part):
    if part == 0:
        return slice(0, PROMPTS)
    start = PROMPTS + (part - 1) * CLEN
    return slice(start, start + CLEN)


def part_keys(ref, lanes, facts, block):
    parts = [ref[:PROMPTS, lanes]]
    for c in range(NC):
        start = pl.multiple_of(facts[block, c] * PLEN, PLEN)
        own = part_rows(c + 1)
        parts.append(jnp.concatenate([ref[pl.ds(start, PLEN), lanes], ref[own, lanes]], axis=0))
    return parts


def attend(qkv, decay_cols, decay_rows, facts, heads, head_dim, team, rows):
    width = heads * head_dim
    scale = head_dim ** (-0.5)

    def body(facts_ref, qkv_ref, col_ref, row_ref, out_ref):
        block = pl.program_id(0)
        masks = key_mask(facts_ref, block, rows)
        for h in range(heads):
            lanes = slice(h * head_dim, (h + 1) * head_dim)
            key_lanes = slice(width + h * head_dim, width + (h + 1) * head_dim)
            value_lanes = slice(2 * width + h * head_dim, 2 * width + (h + 1) * head_dim)
            keys = part_keys(qkv_ref, key_lanes, facts_ref, block)
            values = part_keys(qkv_ref, value_lanes, facts_ref, block)
            probs = probs_of(
                qkv_ref[:, lanes], keys, col_ref[0, :, h : h + 1], row_ref[0, h : h + 1, :],
                facts_ref, block, masks, scale,
            ).astype(jnp.bfloat16)
            for part in range(NC + 1):
                at = part_rows(part)
                out_ref[at, lanes] = dot_nn(probs[at], values[part])

    return pl.pallas_call(
        body,
        grid_spec=pltpu.PrefetchScalarGridSpec(
            num_scalar_prefetch=1,
            grid=(team,),
            in_specs=[
                pl.BlockSpec((rows, qkv.shape[1]), lambda b, f: (b, 0)),
                pl.BlockSpec((1, rows, heads), lambda b, f: (b, 0, 0)),
                pl.BlockSpec((1, heads, rows), lambda b, f: (b, 0, 0)),
            ],
            out_specs=pl.BlockSpec((rows, width), lambda b, f: (b, 0)),
        ),
        out_shape=jax.ShapeDtypeStruct((team * rows, width), jnp.float32),
        cost_estimate=pl.CostEstimate(
            flops=8 * team * rows * rows * width,
            bytes_accessed=8 * team * rows * width * 2,
            transcendentals=team * rows * PROMPTS * heads,
        ),
        name="attend",
    )(facts, qkv, decay_cols, decay_rows)


def attend_back(qkv, grad_attended, decay_cols, decay_rows, facts, heads, head_dim, team, rows):
    width = heads * head_dim
    scale = head_dim ** (-0.5)

    def body(facts_ref, qkv_ref, grad_ref, col_ref, row_ref, out_ref, sum_ref, low_ref, key_acc, value_acc):
        block = pl.program_id(0)
        masks = key_mask(facts_ref, block, rows)
        for h in range(heads):
            lanes = slice(h * head_dim, (h + 1) * head_dim)
            key_lanes = slice(width + h * head_dim, width + (h + 1) * head_dim)
            value_lanes = slice(2 * width + h * head_dim, 2 * width + (h + 1) * head_dim)
            keys = part_keys(qkv_ref, key_lanes, facts_ref, block)
            values = part_keys(qkv_ref, value_lanes, facts_ref, block)
            query = qkv_ref[:, lanes]
            grad = grad_ref[:, lanes]
            probs = probs_of(
                query, keys, col_ref[0, :, h : h + 1], row_ref[0, h : h + 1, :],
                facts_ref, block, masks, scale,
            )
            grad_probs = jnp.concatenate(
                [dot_nt(grad[part_rows(p)], values[p]) for p in range(NC + 1)], axis=0
            )
            mean = jnp.sum(probs * grad_probs, axis=1, keepdims=True)
            grad_logits = probs * (grad_probs - mean)
            sum_ref[0, :, h : h + 1] = jnp.sum(grad_logits, axis=1, keepdims=True)
            probs_low = probs.astype(jnp.bfloat16)
            grad_qk = (grad_logits * scale).astype(jnp.bfloat16)
            prompt_sum = jnp.sum(grad_logits[:PROMPTS], axis=0, keepdims=True)
            for part in range(NC + 1):
                at = part_rows(part)
                out_ref[at, lanes] = dot_nn(grad_qk[at], keys[part]).astype(jnp.bfloat16)
                grad_keys = dot_tn(grad_qk[at], query[at])
                grad_values = dot_tn(probs_low[at], grad[at])
                if part == 0:
                    key_acc[...] = grad_keys
                    value_acc[...] = grad_values
                    continue
                start = pl.multiple_of(facts_ref[block, part - 1] * PLEN, PLEN)
                key_acc[pl.ds(start, PLEN), :] += grad_keys[:PLEN]
                value_acc[pl.ds(start, PLEN), :] += grad_values[:PLEN]
                out_ref[at, key_lanes] = grad_keys[PLEN:].astype(jnp.bfloat16)
                out_ref[at, value_lanes] = grad_values[PLEN:].astype(jnp.bfloat16)
                column = jnp.sum(grad_logits[at], axis=0, keepdims=True)
                first = facts_ref[block, part - 1] == 0
                nothing = jnp.zeros((1, PLEN), jnp.float32)
                prompt_sum += jnp.concatenate(
                    [
                        jnp.where(first, column[:, :PLEN], nothing),
                        jnp.where(first, nothing, column[:, :PLEN]),
                    ],
                    axis=1,
                )
                low_ref[0, h : h + 1, at] = column[:, PLEN:]
            low_ref[0, h : h + 1, :PROMPTS] = prompt_sum
            out_ref[:PROMPTS, key_lanes] = key_acc[...].astype(jnp.bfloat16)
            out_ref[:PROMPTS, value_lanes] = value_acc[...].astype(jnp.bfloat16)

    return pl.pallas_call(
        body,
        grid_spec=pltpu.PrefetchScalarGridSpec(
            num_scalar_prefetch=1,
            grid=(team,),
            in_specs=[
                pl.BlockSpec((rows, qkv.shape[1]), lambda b, f: (b, 0)),
                pl.BlockSpec((rows, width), lambda b, f: (b, 0)),
                pl.BlockSpec((1, rows, heads), lambda b, f: (b, 0, 0)),
                pl.BlockSpec((1, heads, rows), lambda b, f: (b, 0, 0)),
            ],
            out_specs=[
                pl.BlockSpec((rows, 3 * width), lambda b, f: (b, 0)),
                pl.BlockSpec((1, rows, heads), lambda b, f: (b, 0, 0)),
                pl.BlockSpec((1, heads, rows), lambda b, f: (b, 0, 0)),
            ],
            scratch_shapes=[
                pltpu.VMEM((PROMPTS, head_dim), jnp.float32),
                pltpu.VMEM((PROMPTS, head_dim), jnp.float32),
            ],
        ),
        out_shape=[
            jax.ShapeDtypeStruct((team * rows, 3 * width), jnp.bfloat16),
            jax.ShapeDtypeStruct((team, rows, heads), jnp.float32),
            jax.ShapeDtypeStruct((team, heads, rows), jnp.float32),
        ],
        cost_estimate=pl.CostEstimate(
            flops=80 * team * rows * rows * width,
            bytes_accessed=7 * team * rows * width * 2,
            transcendentals=team * rows * PROMPTS * heads,
        ),
        name="attend_back",
    )(facts, qkv, grad_attended, decay_cols, decay_rows)


def matmul(left_side, right_side):
    return jnp.dot(left_side, right_side, preferred_element_type=jnp.float32)


def matmul_tn(left_side, right_side):
    return lax.dot_general(
        left_side, right_side, (((0,), (0,)), ((), ())), preferred_element_type=jnp.float32
    )


def matmul_nt(left_side, right_side):
    return lax.dot_general(
        left_side, right_side, (((1,), (1,)), ((), ())), preferred_element_type=jnp.float32
    )


def line_groups(count):
    step = count // 4
    return [[first + step * k for k in range(4)] for first in range(step)]


def middle_strides(count):
    strides = []
    step = count // 8
    while step > 1:
        strides.append(step)
        step //= 2
    return strides


def swap_pairs(count, step):
    return [(s, s ^ step) for s in range(count)]


def both(low_first, mine, other, axis=0):
    return jnp.stack(
        [jnp.where(low_first, mine, other), jnp.where(low_first, other, mine)], axis=axis
    )


def pick(values, at, axis):
    return lax.dynamic_index_in_dim(values, at, axis, keepdims=False)


def add_low(left_side, right_side):
    return (left_side.astype(jnp.float32) + right_side.astype(jnp.float32)).astype(jnp.bfloat16)


def after(values, *others):
    return lax.optimization_barrier((values,) + others)[0]


def gather_line(block, count):
    return lax.all_gather(block, "shard", axis=0, tiled=True, axis_index_groups=line_groups(count))


def gather_rest(line, count, index, *others):
    width = line.shape[1]
    held = line.reshape(4, -1, width)
    for step in reversed(middle_strides(count)):
        other = lax.ppermute(held, "shard", swap_pairs(count, step))
        if others:
            other = after(other, *others)
        held = both((index // step) % 2 == 0, held, other, axis=1).reshape(4, -1, width)
    return held.reshape(-1, width), other


def scatter_rest(values, count, index):
    width = values.shape[1]
    held = values.reshape(4, -1, width)
    strides = middle_strides(count)
    parts = []
    for step in strides:
        if parts:
            held = add_low(*parts)
        at = (index // step) % 2
        halves = held.reshape(4, 2, -1, width)
        other = lax.ppermute(pick(halves, 1 - at, 1), "shard", swap_pairs(count, step))
        parts = [pick(halves, at, 1), other]

    def finish(*others):
        return add_low(parts[0], after(parts[1], *others)).reshape(-1, width)

    return finish


def scatter_line(values, count):
    return lax.psum_scatter(
        values, "shard", scatter_dimension=0, tiled=True, axis_index_groups=line_groups(count)
    )


def sum_near(values, count):
    total = values
    for step in middle_strides(count):
        total = total + lax.ppermute(total, "shard", swap_pairs(count, step))
    return total


def sum_far(near, count, reps):
    total = near
    for step in (count // 2, count // 4, 1):
        total = total + lax.ppermute(total, "shard", swap_pairs(count, step))
    step = 1
    while step < reps:
        total = total + lax.ppermute(total, "rep", [(r, r ^ step) for r in range(reps)])
        step *= 2
    return total[0]


def local(
    tokens,
    prompt_ids,
    seq_offsets,
    attn_gain,
    w_query,
    w_key,
    w_value,
    w_outgate,
    w_forget,
    forget_bias,
    w_output,
    ffn_gain,
    w_gate,
    w_up,
    w_down,
    cotangent,
    *,
    reps,
    count,
):
    own_rows = tokens.shape[0]
    model_width = tokens.shape[1]
    head_count = w_forget.shape[1]
    head_dim = model_width // head_count
    score_scale = head_dim ** (-0.5)
    team = 4
    core = lax.axis_index("rep") % 2
    index = lax.axis_index("shard")
    side = index % 2
    rank = 2 * side + core
    quarter = model_width // team
    heads = head_count // team
    shard_rows = w_query.shape[0]
    shard_ff = w_down.shape[0]
    unit = shard_ff // 2
    quarter_ff = w_gate.shape[1] // team
    core_pairs = [(r, r ^ 1) for r in range(reps)]
    side_pairs = [(s, s ^ 1) for s in range(count)]

    def swap_core(values):
        return lax.ppermute(values, "rep", core_pairs)

    def swap_side(values):
        return lax.ppermute(values, "shard", side_pairs)

    def team_rows(values, *others):
        pair = jnp.concatenate([values, swap_side(values)], axis=0)
        if others:
            pair = after(pair, *others)
        return jnp.concatenate([pair, swap_core(pair)], axis=0)

    def core_sum(partial):
        half = 2 * own_rows
        return partial[:half] + swap_core(partial[half:].astype(jnp.bfloat16)).astype(jnp.float32)

    def side_sum(pair):
        return pair[:own_rows] + swap_side(pair[own_rows:].astype(jnp.bfloat16)).astype(jnp.float32)

    def team_sum(partial):
        return side_sum(core_sum(partial))

    def cols_of(values, who):
        return lax.dynamic_slice_in_dim(values, who * quarter, quarter, axis=1)

    def units_of(values, which_side):
        cut = values.reshape(values.shape[0], count // 2, 2, 2, unit)
        return pick(pick(cut, core, 3), which_side, 2).reshape(values.shape[0], quarter_ff)

    def pair_rows(mine, sent):
        return both(side == 0, mine, swap_side(sent)).reshape(-1, mine.shape[1])

    small = jnp.concatenate(
        [
            w_forget,
            attn_gain[:, None],
            ffn_gain[:, None],
            jnp.zeros((shard_rows, 128 - head_count - 2), jnp.bfloat16),
        ],
        axis=1,
    )
    far_rank = rank ^ 2

    def columns(who, *weights):
        return [cols_of(w, who) for w in weights]

    first_block = pair_rows(
        jnp.concatenate(columns(rank, w_query, w_key, w_value) + [small], axis=1),
        jnp.concatenate(columns(far_rank, w_query, w_key, w_value) + [small], axis=1),
    )
    rest_block = pair_rows(
        jnp.concatenate(
            columns(rank, w_outgate, w_output) + [units_of(w_gate, side), units_of(w_up, side)],
            axis=1,
        ),
        after(
            jnp.concatenate(
                columns(far_rank, w_outgate, w_output)
                + [units_of(w_gate, 1 - side), units_of(w_up, 1 - side)],
                axis=1,
            ),
            first_block,
        ),
    )
    first_line = gather_line(first_block, count)
    second_line = gather_line(after(rest_block[:, : 2 * quarter], first_line), count)
    gate_line = gather_line(
        after(rest_block[:, 2 * quarter : 2 * quarter + quarter_ff], second_line), count
    )
    up_line = gather_line(after(rest_block[:, 2 * quarter + quarter_ff :], gate_line), count)
    down_line = gather_line(
        after(lax.dynamic_slice_in_dim(w_down, core * unit, unit, axis=0), up_line), count
    )
    first, _ = gather_rest(first_line, count, index)
    gate_w, gate_last = gather_rest(gate_line, count, index)
    up_w, up_last = gather_rest(up_line, count, index)
    down_w, _ = gather_rest(down_line, count, index)

    forget_w = lax.dynamic_slice_in_dim(
        first[:, 3 * quarter : 3 * quarter + head_count], rank * heads, heads, axis=1
    )
    gain_one = first[:, 3 * quarter + head_count].astype(jnp.float32)
    gain_two = first[:, 3 * quarter + head_count + 1].astype(jnp.float32)
    def replicas(values):
        total = values
        step = 2
        while step < reps:
            other = lax.ppermute(total, "rep", [(r, r ^ step) for r in range(reps)])
            total = add_low(total, other)
            step *= 2
        return total

    def own_of(values):
        pair = replicas(values).reshape(2, shard_rows, values.shape[1])
        sides = both(side == 0, pick(pair, side, 0), swap_side(pick(pair, 1 - side, 0)))
        return both(core == 0, sides, swap_core(sides))

    def both_cores(values):
        mine = replicas(values)
        return both(core == 0, mine, swap_core(mine))

    def turn_rows(values):
        cut = values.reshape(2, 2, quarter, quarter)
        mine = pick(cut, side, 0)
        pair = both(side == 0, mine, swap_side(pick(cut, 1 - side, 0)))
        kept = pick(pair, core, 1)
        quad = both(core == 0, kept, swap_core(pick(pair, 1 - core, 1)))
        return jnp.transpose(quad, (2, 1, 0, 3)).reshape(quarter, model_width)

    def turn_cols(values):
        cut = values.reshape(quarter, 2, 2, quarter)
        mine = pick(cut, core, 2)
        pair = both(core == 0, mine, swap_core(pick(cut, 1 - core, 2)))
        kept = pick(pair, side, 2)
        quad = both(side == 0, kept, swap_side(pick(pair, 1 - side, 2)))
        return quad.reshape(model_width, quarter)

    tokens_all = team_rows(after(tokens, rest_block), first_line)
    facts_all = team_rows(jnp.concatenate([prompt_ids[0], seq_offsets[0]])[None, :])
    chain_ok = jnp.stack([chain_mask(facts_all[b, :NC], facts_all[b, NC:]) for b in range(team)])
    chain_float = chain_ok.astype(jnp.float32)

    inputs_all = tokens_all.astype(jnp.float32)
    scaled_all, inverse_all = normalize(inputs_all)
    scaled1 = scaled_all[:own_rows]
    inverse1 = inverse_all[:own_rows]
    inputs = inputs_all[:own_rows]
    normed1 = after((scaled_all * gain_one).astype(jnp.bfloat16), gate_line)
    row_count = normed1.shape[0]

    qkv_low = matmul(normed1, first[:, : 3 * quarter]).astype(jnp.bfloat16)
    cotangent_all = team_rows(after(cotangent, first_line), qkv_low)
    second = gather_rest(second_line, count, index, qkv_low)[0]
    outgate_w = second[:, :quarter]
    output_w = turn_rows(second[:, quarter:])
    outgate_pre = matmul(normed1, outgate_w)
    bias_mine = lax.dynamic_slice_in_dim(
        forget_bias.astype(jnp.float32), rank * heads, heads, axis=0
    )
    forget_in = matmul(normed1, forget_w) + bias_mine[None, :]
    log_forget = jax.nn.log_sigmoid(forget_in).reshape(team, own_rows, heads)
    decay_sum = jnp.einsum(
        "bij,bjh->bhi", chain_float, log_forget, precision=lax.Precision.HIGHEST
    )

    decay_cols = jnp.transpose(decay_sum, (0, 2, 1))
    attended = attend(
        qkv_low,
        decay_cols,
        decay_sum,
        facts_all,
        heads,
        head_dim,
        team,
        own_rows,
    )
    gate_open = jax.nn.sigmoid(outgate_pre)
    gated_low = (after(attended, up_line, gate_last, cotangent_all) * gate_open).astype(jnp.bfloat16)

    residual = inputs + after(team_sum(matmul(gated_low, output_w)), up_last)
    scaled2, inverse2 = normalize(residual)
    normed2 = after(team_rows((scaled2 * gain_two).astype(jnp.bfloat16)), down_line)
    gate_pre = matmul(normed2, gate_w)
    up_pre = matmul(normed2, up_w)
    sig_gate = jax.nn.sigmoid(gate_pre)
    silu_gate = gate_pre * sig_gate
    act_low = (silu_gate * up_pre).astype(jnp.bfloat16)
    grad_act = matmul_nt(cotangent_all, down_w)
    grad_gate = (grad_act * up_pre * sig_gate * (1.0 + gate_pre * (1.0 - sig_gate))).astype(
        jnp.bfloat16
    )
    grad_up = (grad_act * silu_gate).astype(jnp.bfloat16)
    down_sum = scatter_rest(matmul_tn(act_low, cotangent_all).astype(jnp.bfloat16), count, index)
    pair_normed2 = core_sum(matmul_nt(grad_gate, gate_w) + matmul_nt(grad_up, up_w))
    normed2_late = after(normed2, pair_normed2)
    part_gate_w = matmul_tn(normed2_late, grad_gate).astype(jnp.bfloat16)
    grad_normed2 = after(side_sum(pair_normed2), part_gate_w)
    down_held = down_sum(grad_normed2)
    grad_down = scatter_line(down_held, count)
    gate_sum = scatter_rest(part_gate_w, count, index)
    grad_resid = cotangent.astype(jnp.float32) + norm_back(
        grad_normed2 * gain_two, scaled2, inverse2
    )
    grad_attn_own = grad_resid.astype(jnp.bfloat16)
    normed2_last, act_late = lax.optimization_barrier((normed2_late, act_low, grad_attn_own))[:2]
    part_up_w = matmul_tn(normed2_last, grad_up).astype(jnp.bfloat16)
    up_sum = scatter_rest(part_up_w, count, index)
    part_out = matmul(after(act_late, down_held), down_w)
    gate_held = gate_sum(part_out, part_up_w)
    grad_gate_w = scatter_line(gate_held, count)
    grad_attn = after(team_rows(grad_attn_own, gate_held), grad_down)
    grad_gated = matmul_nt(grad_attn, output_w)
    grad_output_cols = turn_cols(matmul_tn(gated_low, grad_attn).astype(jnp.bfloat16))
    grad_attended = (grad_gated * gate_open).astype(jnp.bfloat16)
    grad_outgate = (grad_gated * attended * gate_open * (1.0 - gate_open)).astype(jnp.bfloat16)
    up_held = up_sum(grad_outgate)
    grad_outgate_w = matmul_tn(after(normed1, up_held), grad_outgate).astype(jnp.bfloat16)
    part_second_w = jnp.concatenate([grad_outgate_w, grad_output_cols], axis=1)
    second_sum = scatter_rest(part_second_w, count, index)
    grad_up_w = scatter_line(up_held, count)
    grad_qkv, grad_logit_rows, grad_logit_cols = attend_back(
        qkv_low,
        after(grad_attended, up_held, part_second_w),
        decay_cols,
        decay_sum,
        facts_all,
        heads,
        head_dim,
        team,
        own_rows,
    )
    second_held = second_sum(grad_qkv)
    grad_qkv = after(grad_qkv, grad_gate_w, second_held, grad_up_w)
    sum_second = scatter_line(second_held, count)
    layer_out = (residual + team_sum(after(part_out, grad_qkv))).astype(jnp.bfloat16)
    grad_decay = jnp.transpose(grad_logit_rows, (0, 2, 1)) - grad_logit_cols
    grad_log_forget = jnp.einsum(
        "bij,bhi->bjh", chain_float, grad_decay, precision=lax.Precision.HIGHEST
    ).reshape(row_count, heads)
    grad_forget_in = grad_log_forget * jax.nn.sigmoid(-forget_in)
    bias_sum = lax.dynamic_update_slice_in_dim(
        jnp.zeros((head_count,), jnp.float32),
        jnp.sum(grad_forget_in, axis=0),
        rank * heads,
        axis=0,
    )
    bias_near = sum_near(bias_sum[None, :], count)
    grad_forget_low = lax.dynamic_update_slice_in_dim(
        jnp.zeros((row_count, small.shape[1]), jnp.bfloat16),
        grad_forget_in.astype(jnp.bfloat16),
        rank * heads,
        axis=1,
    )
    grad_first = jnp.concatenate([grad_qkv, grad_forget_low], axis=1)
    part_first_w = matmul_tn(normed1, grad_first).astype(jnp.bfloat16)
    first_sum = scatter_rest(after(part_first_w, bias_near), count, index)
    part_normed1 = matmul_nt(after(grad_first, part_first_w), first) + matmul_nt(
        grad_outgate, outgate_w
    )
    down_own = both_cores(after(grad_down, part_first_w))
    grad_bias = sum_far(after(bias_near, part_first_w), count, reps)
    first_held = first_sum(grad_bias, layer_out, down_own, sum_second)
    sum_first = scatter_line(first_held, count)
    grad_normed1 = after(team_sum(after(part_normed1, first_held)), sum_first)
    tokens_grad = grad_resid + norm_back(grad_normed1 * gain_one, scaled1, inverse1)
    gate_own = own_of(after(grad_gate_w, first_held))
    grad_up_w = after(grad_up_w, first_held)
    sum_second = after(sum_second, grad_normed1)

    def whole_cols(own):
        parts = own.shape[3] // quarter
        quad = jnp.transpose(own.astype(jnp.float32), (1, 0, 2, 3))
        quad = quad.reshape(2, 2, shard_rows, parts, quarter)
        quad = jnp.transpose(quad, (3, 2, 0, 1, 4)).reshape(parts, shard_rows, model_width)
        return [quad[p] for p in range(parts)]

    def whole_units(own):
        quad = jnp.transpose(own.astype(jnp.float32), (1, 0, 2, 3))
        quad = quad.reshape(2, 2, shard_rows, count // 2, unit)
        return jnp.transpose(quad, (2, 3, 0, 1, 4)).reshape(shard_rows, team * quarter_ff)

    first_own = own_of(sum_first)
    query_g, key_g, value_g = whole_cols(first_own[..., : 3 * quarter])
    forget_own = first_own[..., 3 * quarter : 3 * quarter + head_count]
    forget_g = jnp.sum(forget_own.astype(jnp.float32), axis=(0, 1))
    outgate_g, output_g = whole_cols(own_of(sum_second))
    gate_g = whole_units(gate_own)
    up_g = whole_units(own_of(grad_up_w))

    def gain_grad(gain, *pairs):
        total = sum(jnp.sum(w.astype(jnp.float32) * grad, axis=1) for w, grad in pairs)
        return total / gain.astype(jnp.float32)

    gain_one_g = gain_grad(
        attn_gain,
        (w_query, query_g),
        (w_key, key_g),
        (w_value, value_g),
        (w_outgate, outgate_g),
        (w_forget, forget_g),
    )
    gain_two_g = gain_grad(ffn_gain, (w_gate, gate_g), (w_up, up_g))
    return (
        layer_out,
        tokens_grad,
        gain_one_g,
        query_g,
        key_g,
        value_g,
        outgate_g,
        forget_g,
        grad_bias,
        output_g,
        gain_two_g,
        gate_g,
        up_g,
        down_own.astype(jnp.float32).reshape(shard_ff, model_width),
    )


def solution(mesh):
    in_specs = (
        P(("rep", "shard"), None),
        P(("rep", "shard"), None),
        P(("rep", "shard"), None),
        P("shard"),
        P("shard", None),
        P("shard", None),
        P("shard", None),
        P("shard", None),
        P("shard", None),
        P(),
        P("shard", None),
        P("shard"),
        P("shard", None),
        P("shard", None),
        P("shard", None),
        P(("rep", "shard"), None),
    )
    out_specs = (
        P(("rep", "shard"), None),
        P(("rep", "shard"), None),
        P("shard"),
        P("shard", None),
        P("shard", None),
        P("shard", None),
        P("shard", None),
        P("shard", None),
        P(),
        P("shard", None),
        P("shard"),
        P("shard", None),
        P("shard", None),
        P("shard", None),
    )

    def program(*arrays):
        return local(*arrays, reps=mesh.shape["rep"], count=mesh.shape["shard"])

    return jax.shard_map(program, mesh=mesh, in_specs=in_specs, out_specs=out_specs, check_vma=False)
```
